32 devices in a mesh: batch: 4 (over y, core), expert: 8 (over z, x).
Axes of the slice: x: 2, y: 2, z: 4, core: 2. Of those that a mesh axis runs over, the one named last changes fastest.
Arguments:
- tokens: bfloat16 [32768, 768], P(('batch', 'expert')), may hold values from -10 to 10
- cotangent: bfloat16 [32768, 768], P(('batch', 'expert')), may hold values from -6 to 6
- lengths: int32 [32, 6], P(('batch', 'expert')), may hold values from 1 to 512, 1024 in all within a row
- routes: int32 [32768, 1], P(('batch', 'expert')), may hold values from 0 to 7; in each aligned block of 1024 rows (0 to 1023, 1024 to 2047, ...) at most 192 rows name the same one
- mixer_weight: bfloat16 [768, 2304], P(('batch', 'expert')), may hold values from -0.21875 to 0.21875
- output_weight: bfloat16 [768, 768], P(('batch', 'expert')), may hold values from -1.75 to 1.75
- first_gain: bfloat16 [768], P(('batch', 'expert')), may hold values from 0.5 to 1.5
- first_shift: bfloat16 [768], P(('batch', 'expert')), may hold values from -1.25 to 1.25
- second_gain: bfloat16 [768], P(('batch', 'expert')), may hold values from 0.5 to 1.5
- second_shift: bfloat16 [768], P(('batch', 'expert')), may hold values from -1.25 to 1.25
- router_weight: bfloat16 [768, 8], P(('batch', 'expert')), may hold values from -0.15625 to 0.15625
- inner_weight: bfloat16 [8, 768, 3072], P('expert'), may hold values from -0.21875 to 0.21875
- inner_bias: bfloat16 [8, 3072], P('expert'), may hold values from -1.75 to 1.75
- outer_weight: bfloat16 [8, 3072, 768], P('expert'), may hold values from -0.3125 to 0.3125
- outer_bias: bfloat16 [8, 768], P('expert'), may hold values from -1.75 to 1.75
Outputs:
- block_output: bfloat16 [32768, 768], P(('batch', 'expert'))
- input_grad: float32 [32768, 768], P(('batch', 'expert'))
- mixer_grad: float32 [768, 2304], P(('batch', 'expert'))
- output_grad: float32 [768, 768], P(('batch', 'expert'))
- first_gain_grad: float32 [768], P(('batch', 'expert'))
- first_shift_grad: float32 [768], P(('batch', 'expert'))
- second_gain_grad: float32 [768], P(('batch', 'expert'))
- second_shift_grad: float32 [768], P(('batch', 'expert'))
- router_grad: float32 [768, 8], P(('batch', 'expert'))
- inner_weight_grad: float32 [8, 768, 3072], P('expert')
- inner_bias_grad: float32 [8, 3072], P('expert')
- outer_weight_grad: float32 [8, 3072, 768], P('expert')
- outer_bias_grad: float32 [8, 768], P('expert')
- balance_loss: float32 [], replicated
- stream_rms: float32 [3], replicated
The draws below stay inside these ranges and needn't reach their ends.
Inputs may be any that keep to these rules, and one draw needn't show every extreme that they name: Each row lists the lengths of the 6 sequences of one device's 1024 tokens, in order; they sum to 1024 and the largest is half of 1024. `routes`: among the 1024 rows of one device no expert is named more than 192 times, a bound that some block reaches.
All inputs are finite; a program needn't handle non-finite values.
Results may differ from the reference program's by a relative error of at most 0.013.
Values may be sent and summed in bfloat16 or wider, within the bound.
No kernel may reach another device: no remote copies, remote signals or barrier semaphores. Data moves between devices by JAX's collectives and lax.ppermute only.
A program may use at most 256 MiB of HBM per device.

```python
import math
import jax
import jax.numpy as jnp
import numpy as np
from jax import lax

D = 768
FF = 3072
HEADS = 12
HEAD_DIM = 64
TOK_DEV = 1024
SEQS_DEV = 6
EXPERTS = 8
CAP = 192
TOKENS = 32768
DEVICES = 32


def draw_tokens(key, part):
    device_count = TOKENS // TOK_DEV
    owner = (jnp.arange(TOKENS, dtype=jnp.int32) // TOK_DEV).astype(jnp.float32)
    place = owner / max(device_count - 1, 1)
    values = jnp.clip(jax.random.normal(key, (TOKENS, D), jnp.float32), -4.0, 4.0)
    row_scale = 0.6 + 1.2 * place
    return (values * row_scale[:, None]).astype(jnp.bfloat16)


def level_of(rng, shape, shards, smallest, top_value):
    level = 1.0
    for position, parts in shards:
        heights = jax.random.uniform(jax.random.fold_in(jax.random.fold_in(rng, 6), position), (parts,), jnp.float32, smallest / len(shards), top_value / len(shards))
        level = level * jnp.repeat(jnp.exp(heights), shape[position] // parts).reshape((-1,) + (1,) * (len(shape) - 1 - position))
    return level


def split_up(count, total, most, lean):
    weights = [(1 << 20) // math.isqrt(rank ** lean) + 1 for rank in range(2, count + 1)]
    rest, given = total - most - (count - 1), [1] * (count - 1)
    while rest > 0:
        candidates = [i for i in range(count - 1) if given[i] < most]
        pool, budget = sum([weights[i] for i in candidates]), rest
        for i in candidates:
            addition = min(most - given[i], max(1, budget * weights[i] // pool), rest)
            given[i] = given[i] + addition
            rest = rest - addition
    return np.array([most] + given)


def ragged_sizes(own_key, number_of, total, bound, skew):
    if number_of == 2:
        one = jax.random.randint(own_key, (), max(1, total - bound), min(bound, total - 1) + 1)
        return jnp.stack([one, total - one])
    sizes = jnp.asarray(split_up(number_of, total, bound, skew), jnp.int32)
    pairs = (number_of - 1) // 2
    giver, taker = sizes[1:1 + 2 * pairs:2], sizes[2:2 + 2 * pairs:2]
    slack = jnp.minimum(giver - 1, bound - taker)
    moved = jax.random.randint(jax.random.fold_in(own_key, 1), (pairs,), 0, 1 << 20) % (slack + 1)
    sizes = sizes.at[1:1 + 2 * pairs:2].set(giver - moved).at[2:2 + 2 * pairs:2].set(taker + moved)
    return sizes[jax.random.permutation(jax.random.fold_in(own_key, 2), number_of)]


def deal_out(stream_key, own, number, rows, number_of, top, most, lean):
    ranking = jax.random.permutation(stream_key, number_of)
    heavy_load, usual = portions_of(number_of, rows * top, most, lean, True), portions_of(number_of, rows * top, most, lean, False)
    places = jnp.arange(number_of)

    def named(tallies, rotation):
        used = int((tallies > 0).sum())
        fixed = max(1, used // 4)
        shifted = fixed + (places - fixed + rotation * (used - fixed)) % max(1, number_of - fixed)
        return jnp.zeros((number_of,), jnp.int32).at[ranking[jnp.where(places < fixed, places, shifted)]].set(jnp.asarray(tallies, jnp.int32))

    tallies = jnp.where(number % 4 == 0, named(heavy_load, number // 4), named(usual, number - number // 4 - 1))
    mixed = jax.random.permutation(jax.random.fold_in(own, 3), number_of)
    donor, sink = mixed[0:number_of // 2 * 2:2], mixed[1:number_of // 2 * 2:2]
    slack = jnp.minimum(tallies[donor] - 1, most - tallies[sink]) // 2
    slack = jnp.where((donor == ranking[0]) | (sink == ranking[0]) | (tallies[sink] == 0), 0, jnp.maximum(slack, 0))
    shifted = jax.random.randint(jax.random.fold_in(own, 4), (number_of // 2,), 0, 1 << 20) % (slack + 1)
    tallies = tallies.at[donor].add(-shifted).at[sink].add(shifted)
    members = jnp.searchsorted(jnp.cumsum(tallies), jnp.arange(rows * top), side="right").astype(jnp.int32)
    grid = members.reshape(top, rows).T
    grid = grid[jax.random.permutation(jax.random.fold_in(own, 1), rows)]
    rotation = jax.random.randint(jax.random.fold_in(own, 2), (rows, 1), 0, top)
    return jnp.take_along_axis(grid, (jnp.arange(top)[None, :] + rotation) % top, axis=1)


def portions_of(amount, total, reach, slope, full):
    loads = [(1 << 20) // math.isqrt(standing ** slope) + 1 for standing in range(1, amount + 1)]
    largest = reach if full else min(reach, max(-(-total // amount), total * loads[0] // sum(loads)))
    least = 1 if total - largest >= amount - 1 else 0
    given, spare = [largest] + [least] * (amount - 1), total - largest - least * (amount - 1)
    while spare > 0:
        movable = [i for i in range(1, amount) if given[i] < largest] or [i for i in range(1, amount) if given[i] < reach]
        pool, budget = sum([loads[i] for i in movable]), spare
        for i in movable:
            more = min(reach - given[i], max(1, budget * loads[i] // pool), spare)
            given[i] = given[i] + more
            spare = spare - more
    return np.array(given)


def scatter_about(rng, extent, scale, limit, split=(), kind=jnp.bfloat16):
    values = scale * jax.random.normal(rng, extent, jnp.float32)
    if split:
        values = values * level_of(rng, extent, split, -0.22, 0.18)
    return jnp.clip(values, -limit, limit).astype(kind)


def setup_inputs(seed: int = 0) -> dict:
    key_of = jax.random.split(jax.random.key(seed), 16)
    tokens = draw_tokens(jax.random.fold_in(key_of[15], 71), 0)
    cotangent = scatter_about(key_of[1], (TOKENS, D), 1.0, 6.0, ((0, 32),))
    lengths = jax.vmap(lambda own: ragged_sizes(own, SEQS_DEV, TOK_DEV, TOK_DEV // 2, 2))(jax.random.split(key_of[2], DEVICES)).reshape((DEVICES, SEQS_DEV)).astype(jnp.int32)
    routes_keys = jax.random.split(jax.random.fold_in(key_of[3], 1), TOKENS // TOK_DEV)
    routes_turns = jax.random.permutation(jax.random.fold_in(key_of[3], 3), TOKENS // TOK_DEV)
    routes = jax.vmap(lambda own, number: deal_out(jax.random.fold_in(key_of[3], 2), own, number, TOK_DEV, EXPERTS, 1, CAP, 2))(routes_keys, routes_turns).reshape((TOKENS, 1))
    mixer_weight = scatter_about(key_of[4], (D, 3 * D), D ** -0.5, 0.21875, ((0, 32),))
    output_weight = scatter_about(key_of[5], (D, D), (D // 64) ** -0.5, 1.75, ((0, 32),))
    first_gain = jnp.clip(1.0 + 0.1 * jax.random.normal(key_of[6], (D,), jnp.float32), 0.5, 1.5).astype(jnp.bfloat16)
    first_shift = scatter_about(key_of[7], (D,), 0.2, 1.25, ((0, 32),))
    second_gain = jnp.clip(1.0 + 0.1 * jax.random.normal(key_of[8], (D,), jnp.float32), 0.5, 1.5).astype(jnp.bfloat16)
    second_shift = scatter_about(key_of[9], (D,), 0.2, 1.25, ((0, 32),))
    router_weight = scatter_about(key_of[10], (D, EXPERTS), (2 * D) ** -0.5, 0.15625, ((0, 32),))
    inner_weight = scatter_about(key_of[11], (EXPERTS, D, FF), D ** -0.5, 0.21875, ((0, 8),))
    inner_bias = scatter_about(key_of[12], (EXPERTS, FF), 0.3, 1.75, ((0, 8),))
    outer_weight = scatter_about(key_of[13], (EXPERTS, FF, D), (FF // 8) ** -0.5, 0.3125, ((0, 8),))
    outer_bias = scatter_about(key_of[14], (EXPERTS, D), 0.3, 1.75, ((0, 8),))
    return {"tokens": tokens, "cotangent": cotangent, "lengths": lengths, "routes": routes, "mixer_weight": mixer_weight, "output_weight": output_weight, "first_gain": first_gain, "first_shift": first_shift, "second_gain": second_gain, "second_shift": second_shift, "router_weight": router_weight, "inner_weight": inner_weight, "inner_bias": inner_bias, "outer_weight": outer_weight, "outer_bias": outer_bias}


@jax.custom_vjp
def low(v):
    return lax.optimization_barrier(v.astype(jnp.bfloat16)).astype(jnp.float32)

@jax.custom_vjp
def low_back(v):
    return v

def low_keep(v):
    return (low(v), None)

def low_pass(kept, grad):
    return (grad,)

def back_keep(v):
    return (v, None)

def back_low(kept, grad):
    return (low(grad),)
low.defvjp(low_keep, low_pass)
low_back.defvjp(back_keep, back_low)
EPSILON = 1e-05

def layer_norm(values, gain, shift):
    centre = values - lax.optimization_barrier(jnp.mean(values, axis=-1, keepdims=True))
    spread = lax.optimization_barrier(jnp.mean(centre * centre, axis=-1, keepdims=True))
    return centre * lax.rsqrt(spread + EPSILON) * gain + shift

def visible_mask(lengths_row, rows_here):
    ends = jnp.cumsum(lengths_row)
    places = jnp.arange(rows_here, dtype=jnp.int32)
    segment = lax.optimization_barrier(jnp.sum((places[:, None] >= ends[None, :]).astype(jnp.int32), axis=1))
    return (segment[:, None] == segment[None, :]) & (places[None, :] <= places[:, None])

def attend(operands):
    mixed, lengths_row = operands
    rows_here = mixed.shape[0]
    queries = mixed[:, :D].reshape(rows_here, HEADS, HEAD_DIM)
    keys_all = mixed[:, D:2 * D].reshape(rows_here, HEADS, HEAD_DIM)
    values_all = mixed[:, 2 * D:].reshape(rows_here, HEADS, HEAD_DIM)
    scores = jnp.einsum('qhd,khd->hqk', queries, keys_all, precision=lax.Precision.HIGHEST) * HEAD_DIM ** (-0.5)
    scores = low_back(scores)
    scores = jnp.where(visible_mask(lengths_row, rows_here)[None], scores, -1e+30)
    attn_probs = jax.nn.softmax(scores, axis=-1)
    attended = jnp.einsum('hqk,khd->qhd', low(attn_probs), values_all, precision=lax.Precision.HIGHEST)
    return attended.reshape(rows_here, D)

def expert_apply(operands):
    rows_in, inner_w, inner_b, outer_w, outer_b = operands
    hidden_pre = low_back(jnp.dot(rows_in, inner_w, precision=lax.Precision.HIGHEST) + inner_b)
    hidden_act = low(jax.nn.gelu(hidden_pre, approximate=False))
    return low(low_back(jnp.dot(hidden_act, outer_w, precision=lax.Precision.HIGHEST) + outer_b))

def block_forward(tokens_f, mixer_w, output_w, gain_one, shift_one, gain_two, shift_two, router_w, inner_w, inner_b, outer_w, outer_b, lengths, routes):
    normed_one = layer_norm(tokens_f, gain_one, shift_one)
    mixed = low(low_back(jnp.dot(low(normed_one), mixer_w, precision=lax.Precision.HIGHEST)))
    attended = lax.map(jax.checkpoint(attend), (mixed.reshape(DEVICES, TOK_DEV, 3 * D), lengths))
    attended = low(low_back(attended.reshape(TOKENS, D)))
    attn_out = low_back(jnp.dot(attended, output_w, precision=lax.Precision.HIGHEST))
    stream = tokens_f + attn_out
    normed_two = low(layer_norm(stream, gain_two, shift_two))
    chosen = routes[:, 0]
    hits = chosen[:, None] == jnp.arange(EXPERTS, dtype=jnp.int32)[None, :]
    onehot = hits.astype(jnp.float32)
    onehot_int = hits.astype(jnp.int32).reshape(DEVICES, TOK_DEV, EXPERTS)
    logits = lax.optimization_barrier(jnp.sum(jnp.dot(normed_two, router_w, precision=lax.Precision.HIGHEST) * onehot, axis=1))
    gates = jax.nn.sigmoid(logits)
    ranks = lax.optimization_barrier(jnp.sum((jnp.cumsum(onehot_int, axis=1) - onehot_int) * onehot_int, axis=2)).reshape(TOKENS).astype(jnp.int32)
    sources = (jnp.arange(TOKENS, dtype=jnp.int32) // TOK_DEV).astype(jnp.int32)
    targets = ((sources * EXPERTS + chosen) * CAP + ranks).astype(jnp.int32)
    buffer = jnp.zeros((DEVICES * EXPERTS * CAP, D), jnp.float32).at[targets].set(low_back(normed_two))
    buffer = buffer.reshape(DEVICES, EXPERTS, CAP, D).transpose(1, 0, 2, 3).reshape(EXPERTS, DEVICES * CAP, D)
    expert_rows = lax.map(jax.checkpoint(expert_apply), (buffer, inner_w, inner_b, outer_w, outer_b))
    expert_rows = expert_rows.reshape(EXPERTS, DEVICES, CAP, D).transpose(1, 0, 2, 3).reshape(DEVICES * EXPERTS * CAP, D)
    picked = expert_rows[targets]
    moe_out = gates[:, None] * picked
    result = stream + moe_out
    counts = lax.optimization_barrier(jnp.sum(onehot, axis=0))
    gate_sums = lax.optimization_barrier(jnp.sum(onehot * gates[:, None], axis=0))
    average = TOKENS / EXPERTS
    balance = jnp.sum((counts - average) / average * gate_sums) / TOKENS
    squares = jnp.stack([jnp.mean(result * result), jnp.mean(attn_out * attn_out), jnp.mean(moe_out * moe_out)])
    root_means = jnp.sqrt(squares + 1e-06)
    return ((result, balance), root_means)

def reference(tokens, cotangent, lengths, routes, mixer_weight, output_weight, first_gain, first_shift, second_gain, second_shift, router_weight, inner_weight, inner_bias, outer_weight, outer_bias):

    def forward(tokens_f, mixer_w, output_w, gain_one, shift_one, gain_two, shift_two, router_w, inner_w, inner_b, outer_w, outer_b):
        return block_forward(tokens_f, mixer_w, output_w, gain_one, shift_one, gain_two, shift_two, router_w, inner_w, inner_b, outer_w, outer_b, lengths, routes)
    floats = tuple((array_in.astype(jnp.float32) for array_in in (tokens, mixer_weight, output_weight, first_gain, first_shift, second_gain, second_shift, router_weight, inner_weight, inner_bias, outer_weight, outer_bias)))
    outputs, pullback, root_means = jax.vjp(forward, *floats, has_aux=True)
    result, balance = outputs
    grads = pullback((cotangent.astype(jnp.float32), jnp.ones((), jnp.float32)))
    return (result.astype(jnp.bfloat16), grads[0], grads[1], grads[2], grads[3], grads[4], grads[5], grads[6], grads[7], grads[8], grads[9], grads[10], grads[11], balance, root_means)
```

```python
import functools

import jax
import jax.numpy as jnp
import numpy as np
from jax import lax
from jax.experimental import pallas as pl
from jax.experimental.pallas import tpu as pltpu
from jax.sharding import PartitionSpec as P

HEADS = 12
HEAD_DIM = 64
PAIRS = HEADS // 2
WINDOW = 512
BLOCK = 256
EPSILON = 1e-05
LANES = 128
BF = jnp.bfloat16
F32 = jnp.float32
ANYWHERE = ("batch", "expert")

NT = (((1,), (1,)), ((), ()))
NN = (((1,), (0,)), ((), ()))


def mm(a, b, dims=NN):
    return lax.dot_general(a, b, dims, preferred_element_type=F32)


def call(body, name, grid, in_specs, out_specs, out_shape, scratch=(), flops=0, bytes_=0, prefetch=0, aliases=None):
    return pl.pallas_call(
        body,
        name=name,
        grid_spec=pltpu.PrefetchScalarGridSpec(
            num_scalar_prefetch=prefetch,
            grid=grid,
            in_specs=in_specs,
            out_specs=out_specs,
            scratch_shapes=list(scratch),
        ),
        out_shape=out_shape,
        input_output_aliases=aliases or {},
        cost_estimate=pl.CostEstimate(flops=int(flops), bytes_accessed=int(bytes_), transcendentals=0),
    )


def sds(shape, dtype):
    return jax.ShapeDtypeStruct(shape, dtype)


def full(shape):
    return pl.BlockSpec(shape, lambda *_: (0,) * len(shape))


def bits_of(size):
    return size.bit_length() - 1


def swap(value, axis, bit):
    size = lax.axis_size(axis)
    return lax.ppermute(value, axis, [(i, i ^ (1 << bit)) for i in range(size)])


def my_bit(axis, bit):
    return (lax.axis_index(axis) >> bit) & 1


def gather_rows(shard):
    nb, ne = lax.axis_size("batch"), lax.axis_size("expert")
    value = shard
    placed = []
    order = [("expert", b) for b in reversed(range(bits_of(ne)))] + [("batch", b) for b in reversed(range(bits_of(nb)))]
    for axis, bit in order:
        weight = bit + (bits_of(ne) if axis == "batch" else 0)
        spot = sum(1 for w in placed if w > weight)
        placed.append(weight)
        other = swap(value, axis, bit)
        mine_high = my_bit(axis, bit) == 1
        low = jnp.where(mine_high, other, value)
        high = jnp.where(mine_high, value, other)
        value = jnp.stack([low, high], axis=spot)
    return value.reshape(nb * ne * shard.shape[0], shard.shape[1])


def scatter_rows(parts, rows_each):
    nb, ne = lax.axis_size("batch"), lax.axis_size("expert")
    ny = nb // 2
    core = my_bit("batch", 0)

    def half(which):
        return jnp.concatenate(
            [
                lax.dynamic_index_in_dim(p.reshape(ny, 2, ne, rows_each, p.shape[1]), which, 1, keepdims=False).astype(BF)
                for p in parts
            ],
            axis=-1,
        )

    got = swap(half(1 - core), "batch", 0)
    total = (half(core).astype(F32) + got.astype(F32)).astype(BF)
    total = jnp.swapaxes(total, 0, 1)
    pieces = lax.all_to_all(total, "expert", split_axis=0, concat_axis=0, tiled=True)
    value = jnp.sum(pieces.astype(F32), axis=0)
    for bit in reversed(range(1, bits_of(nb))):
        here = my_bit("batch", bit)
        value = value.reshape((2, value.shape[0] // 2) + value.shape[1:])
        out = lax.dynamic_index_in_dim(value, 1 - here, 0, keepdims=False)
        value = lax.dynamic_index_in_dim(value, here, 0, keepdims=False) + swap(out, "batch", bit)
    return value[0]


def sum_all(value):
    for axis in ("expert", "batch"):
        for bit in range(bits_of(lax.axis_size(axis))):
            value = value + swap(value, axis, bit)
    return value


def prep_body(lengths_ref, routes_col, routes_row, tgt_row, start_row, counts, *, capacity):
    rows = routes_row.shape[1]
    at = lax.broadcasted_iota(jnp.int32, (1, rows), 1)
    start = jnp.zeros((1, rows), jnp.int32)
    off = jnp.int32(0)
    for s in range(lengths_ref.shape[1]):
        start = jnp.where(at >= off, off, start)
        off = off + lengths_ref[0, s]
    start_row[...] = start
    hot = routes_row[...] == lax.broadcasted_iota(jnp.int32, (LANES, rows), 0)
    hot_low = jnp.where(hot, 1.0, 0.0).astype(BF)
    before = lax.broadcasted_iota(jnp.int32, (rows, rows), 0) < lax.broadcasted_iota(jnp.int32, (rows, rows), 1)
    ranks = mm(hot_low, jnp.where(before, 1.0, 0.0).astype(BF))
    rank = jnp.sum(jnp.where(hot, ranks, 0.0), axis=0, keepdims=True)
    tgt_row[...] = routes_row[...] * capacity + rank.astype(jnp.int32)
    hot_col = routes_col[...] == lax.broadcasted_iota(jnp.int32, (rows, LANES), 1)
    counts[...] = jnp.sum(jnp.where(hot_col, 1.0, 0.0), axis=0, keepdims=True)


def prepare(lengths, routes, capacity):
    rows = routes.shape[0]
    return call(
        functools.partial(prep_body, capacity=capacity),
        "prep",
        (1,),
        [pl.BlockSpec(memory_space=pltpu.SMEM), full((rows, 1)), full((1, rows))],
        [full((1, rows)), full((1, rows)), full((1, LANES))],
        [sds((1, rows), jnp.int32), sds((1, rows), jnp.int32), sds((1, LANES), F32)],
        flops=2 * rows * rows * LANES,
        bytes_=rows * 1024,
    )(lengths, routes, routes.reshape(1, rows))


def dispatch_body(slots, tgt, x, out):
    hot = jnp.where(slots[...] == tgt[...], 1.0, 0.0).astype(BF)
    out[0] = mm(hot, x[...]).astype(BF)


def dispatch(slots_col, tgt_row, x):
    rows, width = x.shape
    half = slots_col.shape[0] // 2
    tile = BLOCK
    per = half // tile
    return call(
        dispatch_body,
        "dispatch",
        (2, per),
        [
            pl.BlockSpec((tile, 1), lambda c, t: (c * per + t, 0)),
            full((1, rows)),
            full((rows, width)),
        ],
        pl.BlockSpec((1, tile, width), lambda c, t: (c, t, 0)),
        sds((2, half, width), BF),
        flops=4 * half * rows * width,
        bytes_=rows * width * 5,
    )(slots_col, tgt_row, x)


def normalise(v):
    centre = v - jnp.mean(v, axis=-1, keepdims=True)
    spread = jnp.mean(centre * centre, axis=-1, keepdims=True)
    scale = lax.rsqrt(spread + EPSILON)
    return centre * scale, scale


def first_body(tokens, gains, mixer, mixed, normed_t, *, gain_at):
    hat, _ = normalise(tokens[...].astype(F32))
    normed = hat * gains[gain_at : gain_at + 1, :] + gains[gain_at + 1 : gain_at + 2, :]
    low = normed.astype(BF)
    normed_t[...] = low.T
    mixed[...] = mm(low, mixer[...]).astype(BF)


def first_stage(tokens, gains, gathered, gain_at):
    rows, width = tokens.shape
    wide = 3 * width
    return call(
        functools.partial(first_body, gain_at=gain_at),
        "first",
        (rows // BLOCK,),
        [
            pl.BlockSpec((BLOCK, width), lambda i: (i, 0)),
            full((LANES, width)),
            pl.BlockSpec((width, wide), lambda i: (0, 0)),
        ],
        [pl.BlockSpec((BLOCK, wide), lambda i: (i, 0)), pl.BlockSpec((width, BLOCK), lambda i: (0, i))],
        [sds((rows, wide), BF), sds((width, rows), BF)],
        flops=2 * rows * width * wide,
        bytes_=2 * (rows * (2 * width + wide) + width * wide),
    )(tokens, gains, gathered)


def fill_bias(bias, start):
    rows = bias.shape[0]
    for q in range(rows // BLOCK):
        k0 = max(0, (q + 1) * BLOCK - WINDOW - BLOCK)
        n = (q + 1) * BLOCK - k0
        key = k0 + lax.broadcasted_iota(jnp.int32, (n, BLOCK), 0)
        query = q * BLOCK + lax.broadcasted_iota(jnp.int32, (n, BLOCK), 1)
        seen = (key <= query) & (key >= start[:, q * BLOCK : (q + 1) * BLOCK])
        bias[k0 : k0 + n, q * BLOCK : (q + 1) * BLOCK] = jnp.where(seen, 0.0, -1e30)


def head_of(value, h):
    lane = lax.broadcasted_iota(jnp.int32, value.shape, 1)
    return jnp.where((lane >= HEAD_DIM * h) & (lane < HEAD_DIM * (h + 1)), value, jnp.zeros_like(value))


def attend_body(start, q, k, v, att, att_t, lse, bias, v_t):
    rows = q.shape[0]

    @pl.when(pl.program_id(0) == 0)
    def _():
        fill_bias(bias, start[...])

    v_t[...] = v[...].T
    for i in range(rows // BLOCK):
        k0 = max(0, (i + 1) * BLOCK - WINDOW - BLOCK)
        k1 = (i + 1) * BLOCK
        here = slice(i * BLOCK, k1)
        scaled = q[here, :] * jnp.asarray(HEAD_DIM**-0.5, BF)
        for h in range(2):
            s = mm(k[k0:k1, :], head_of(scaled, h), NT) + bias[k0:k1, here]
            top = jnp.max(s, axis=0, keepdims=True)
            e = jnp.exp(s - top)
            total = jnp.sum(e, axis=0, keepdims=True)
            o = mm(v_t[HEAD_DIM * h : HEAD_DIM * (h + 1), k0:k1], e.astype(BF)) / total
            att_t[HEAD_DIM * h : HEAD_DIM * (h + 1), here] = o.astype(BF)
            lse[0, h : h + 1, here] = top + jnp.log(total)
    att[...] = att_t[...].T


def attend(mixed, start_row):
    rows = mixed.shape[0]
    width = mixed.shape[1] // 3
    return call(
        attend_body,
        "attend",
        (PAIRS,),
        [
            full((1, rows)),
            pl.BlockSpec((rows, LANES), lambda p: (0, p)),
            pl.BlockSpec((rows, LANES), lambda p: (0, PAIRS + p)),
            pl.BlockSpec((rows, LANES), lambda p: (0, 2 * PAIRS + p)),
        ],
        [
            pl.BlockSpec((rows, LANES), lambda p: (0, p)),
            pl.BlockSpec((LANES, rows), lambda p: (p, 0)),
            pl.BlockSpec((1, 8, rows), lambda p: (p, 0, 0)),
        ],
        [sds((rows, width), BF), sds((width, rows), BF), sds((PAIRS, 8, rows), F32)],
        [pltpu.VMEM((rows, rows), F32), pltpu.VMEM((LANES, rows), BF)],
        flops=8 * HEADS * rows * rows * HEAD_DIM,
        bytes_=2 * rows * width * 5,
    )(start_row, mixed, mixed, mixed)


def attend_back_body(start, q, k, v, g, lse, normed_t, dq, dk, dv, wq, wk, wv, bias, k_t, dq_t, dk_acc, dv_acc):
    rows = q.shape[0]

    @pl.when(pl.program_id(0) == 0)
    def _():
        fill_bias(bias, start[...])

    k_t[...] = k[...].T
    dk_acc[...] = jnp.zeros_like(dk_acc)
    dv_acc[...] = jnp.zeros_like(dv_acc)
    for i in range(rows // BLOCK):
        k0 = max(0, (i + 1) * BLOCK - WINDOW - BLOCK)
        k1 = (i + 1) * BLOCK
        here = slice(i * BLOCK, k1)
        scaled = q[here, :] * jnp.asarray(HEAD_DIM**-0.5, BF)
        g_here = g[here, :]
        for h in range(2):
            q_h = head_of(scaled, h)
            g_h = head_of(g_here, h)
            s = mm(k[k0:k1, :], q_h, NT) + bias[k0:k1, here]
            p = jnp.exp(s - lse[0, h : h + 1, here])
            dp = mm(v[k0:k1, :], g_h, NT)
            inner = jnp.sum(p * dp, axis=0, keepdims=True)
            ds = (p * (dp - inner)).astype(BF)
            dv_acc[k0:k1, :] += mm(p.astype(BF), g_h)
            dk_acc[k0:k1, :] += mm(ds, q_h)
            dq_t[HEAD_DIM * h : HEAD_DIM * (h + 1), here] = mm(k_t[HEAD_DIM * h : HEAD_DIM * (h + 1), k0:k1], ds)
    dq[...] = (dq_t[...].T * HEAD_DIM**-0.5).astype(BF)
    dk[...] = dk_acc[...].astype(BF)
    dv[...] = dv_acc[...].astype(BF)
    wq[...] = mm(normed_t[...], dq[...]).astype(BF)
    wk[...] = mm(normed_t[...], dk[...]).astype(BF)
    wv[...] = mm(normed_t[...], dv[...]).astype(BF)


def attend_back(mixed, attended_grad, lse, start_row, normed_t):
    rows, width = attended_grad.shape
    column = pl.BlockSpec((rows, LANES), lambda p: (0, p))
    return call(
        attend_back_body,
        "attend_back",
        (PAIRS,),
        [
            full((1, rows)),
            column,
            pl.BlockSpec((rows, LANES), lambda p: (0, PAIRS + p)),
            pl.BlockSpec((rows, LANES), lambda p: (0, 2 * PAIRS + p)),
            column,
            pl.BlockSpec((1, 8, rows), lambda p: (p, 0, 0)),
            full((width, rows)),
        ],
        [column] * 3 + [pl.BlockSpec((width, LANES), lambda p: (0, p))] * 3,
        [sds((rows, width), BF)] * 3 + [sds((width, width), BF)] * 3,
        [
            pltpu.VMEM((rows, rows), F32),
            pltpu.VMEM((LANES, rows), BF),
            pltpu.VMEM((LANES, rows), F32),
            pltpu.VMEM((rows, LANES), F32),
            pltpu.VMEM((rows, LANES), F32),
        ],
        flops=20 * HEADS * rows * rows * HEAD_DIM,
        bytes_=2 * rows * width * 10,
    )(start_row, mixed, mixed, mixed, attended_grad, lse, normed_t)


def second_body(att, w, tokens, gains, router, routes, stream, low, gates, sums, *, gain_at):
    attn = mm(att[...], w[...])
    total = tokens[...].astype(F32) + attn
    stream[...] = total
    hat, _ = normalise(total)
    normed = (hat * gains[gain_at : gain_at + 1, :] + gains[gain_at + 1 : gain_at + 2, :]).astype(BF)
    low[...] = normed
    logits = mm(normed, router[...])
    hot = routes[...] == lax.broadcasted_iota(jnp.int32, logits.shape, 1)
    gate = jax.nn.sigmoid(jnp.sum(jnp.where(hot, logits, 0.0), axis=1, keepdims=True))
    gates[...] = gate

    @pl.when(pl.program_id(0) == 0)
    def _():
        sums[...] = jnp.zeros_like(sums)

    row = lax.broadcasted_iota(jnp.int32, sums.shape, 0)
    by_expert = jnp.sum(jnp.where(hot, gate, 0.0), axis=0, keepdims=True)
    squares = jnp.sum(attn * attn)
    sums[...] += jnp.where(row == 0, by_expert, jnp.where(row == 1, squares, 0.0))


def second_stage(att, gathered, tokens, gains, routes, gain_at):
    rows, width = tokens.shape
    block = pl.BlockSpec((BLOCK, width), lambda i: (i, 0))
    thin = pl.BlockSpec((BLOCK, 1), lambda i: (i, 0))
    return call(
        functools.partial(second_body, gain_at=gain_at),
        "second",
        (rows // BLOCK,),
        [
            block,
            pl.BlockSpec((width, width), lambda i: (0, 3)),
            block,
            full((LANES, width)),
            pl.BlockSpec((width, LANES), lambda i: (0, 4 * width // LANES)),
            thin,
        ],
        [block, block, thin, full((8, LANES))],
        [sds((rows, width), F32), sds((rows, width), BF), sds((rows, 1), F32), sds((8, LANES), F32)],
        flops=2 * rows * width * width,
        bytes_=rows * width * 10 + width * width * 2,
    )(att, gathered, tokens, gains, gathered, routes)


def expert_body(
    bal, x, c, w1t, w2, w2t, w1, b1, b2, rw, act_t, pre_t, g_out, x_t, out, in_grad, b1_grad, rows_out,
    g, gate, out_acc, in_acc,
):
    step = pl.program_id(0)

    @pl.when(step == 0)
    def _():
        logits = jnp.sum(x[...].astype(F32) * rw[...], axis=1, keepdims=True)
        gate[...] = jax.nn.sigmoid(logits)
        g[...] = (gate[...] * c[...].astype(F32)).astype(BF)
        out_acc[...] = jnp.zeros_like(out_acc)
        in_acc[...] = jnp.zeros_like(in_acc)

    pre = mm(w1t[...], x[...], NT) + b1[...]
    cdf = 0.5 * (1.0 + lax.erf(pre * (0.5**0.5)))
    act = (pre * cdf).astype(BF)
    slope = cdf + pre * jnp.exp(-0.5 * pre * pre) * ((2.0 * np.pi) ** -0.5)
    act_t[...] = act
    out_acc[...] += mm(w2t[...], act)
    back = (mm(w2[...], g[...], NT) * slope).astype(BF)
    pre_t[...] = back
    in_acc[...] += mm(w1[...], back)
    b1_grad[...] = jnp.sum(back.astype(F32), axis=1, keepdims=True)

    @pl.when(step == pl.num_programs(0) - 1)
    def _():
        result = (out_acc[...].T + b2[...]).astype(BF)
        out[...] = result
        gate_grad = jnp.sum(c[...].astype(F32) * result.astype(F32), axis=1, keepdims=True) + bal[0, 0]
        logit_grad = gate_grad * gate[...] * (1.0 - gate[...])
        in_grad[...] = (in_acc[...].T + logit_grad * rw[...]).astype(BF)
        g_out[...] = g[...]
        x_t[...] = x[...].T
        row = lax.broadcasted_iota(jnp.int32, rows_out.shape, 0)
        router_part = jnp.sum(x[...].astype(F32) * logit_grad, axis=0, keepdims=True)
        bias_part = jnp.sum(g[...].astype(F32), axis=0, keepdims=True)
        rows_out[...] = jnp.where(row == 0, router_part, jnp.where(row == 1, bias_part, 0.0))


def expert_stage(bal, x, c, w1t, w2, w2t, w1, b1, b2, rw):
    rows, width = x.shape
    wide = w1.shape[1]
    tile = BLOCK
    across = pl.BlockSpec((tile, width), lambda f: (f, 0))
    down = pl.BlockSpec((width, tile), lambda f: (0, f))
    whole = full((rows, width))
    return call(
        expert_body,
        "expert",
        (wide // tile,),
        [
            pl.BlockSpec(memory_space=pltpu.SMEM),
            whole,
            whole,
            across,
            across,
            down,
            down,
            pl.BlockSpec((tile, 1), lambda f: (f, 0)),
            full((1, width)),
            full((1, width)),
        ],
        [
            pl.BlockSpec((tile, rows), lambda f: (f, 0)),
            pl.BlockSpec((tile, rows), lambda f: (f, 0)),
            whole,
            full((width, rows)),
            whole,
            whole,
            pl.BlockSpec((tile, 1), lambda f: (f, 0)),
            full((8, width)),
        ],
        [
            sds((wide, rows), BF),
            sds((wide, rows), BF),
            sds((rows, width), BF),
            sds((width, rows), BF),
            sds((rows, width), BF),
            sds((rows, width), BF),
            sds((wide, 1), F32),
            sds((8, width), F32),
        ],
        [
            pltpu.VMEM((rows, width), BF),
            pltpu.VMEM((rows, 1), F32),
            pltpu.VMEM((width, rows), F32),
            pltpu.VMEM((width, rows), F32),
        ],
        flops=8 * rows * width * wide,
        bytes_=2 * (4 * width * wide + 2 * wide * rows + 6 * rows * width),
    )(bal, x, c, w1t, w2, w2t, w1, b1, b2, rw)


def outer_grad_body(core, a0, a1, g0, g1, *rest):
    total = mm(a0[...], g0[...]) + mm(a1[...], g1[...])
    if len(rest) == 2:
        total = total + rest[0][...].astype(F32)
    rest[-1][...] = total.astype(BF)


def inner_grad_body(core, a0, a1, x0, x1, *rest):
    total = mm(x0[...], a0[...], NT) + mm(x1[...], a1[...], NT)
    if len(rest) == 2:
        total = total + rest[0][...].astype(F32)
    rest[-1][...] = total.astype(BF)


def weight_grad(which, outer, acts, others, width, wide, add=None):
    tile = 512
    steps = wide // 2 // tile
    rows = acts[0].shape[1]
    a_spec = pl.BlockSpec((tile, rows), lambda f, s: (s[0] * steps + f, 0))
    if outer:
        o_spec = pl.BlockSpec((tile, width), lambda f, s: (f, 0))
        shape = (wide // 2, width)
    else:
        o_spec = pl.BlockSpec((width, tile), lambda f, s: (0, f))
        shape = (width, wide // 2)
    specs = [a_spec, a_spec, full(others[0].shape), full(others[1].shape)]
    operands = [which, acts[0], acts[1], others[0], others[1]]
    if add is not None:
        specs.append(o_spec)
        operands.append(add)
    return call(
        outer_grad_body if outer else inner_grad_body,
        "weight_grad",
        (steps,),
        specs,
        o_spec,
        sds(shape, BF),
        flops=2 * rows * width * wide,
        bytes_=2 * (wide * rows + 2 * rows * width + width * wide),
        prefetch=1,
    )(*operands)


def own_half_body(which, a, b, out, low):
    total = a[...].astype(F32) + b[...].astype(F32)
    low[...] = total.astype(BF)
    out[0] = total.astype(BF).astype(F32)


def other_half_body(which, held, a, out):
    out[0] = a[...].astype(F32)


def half_specs(outer, shape):
    steps = 3
    if outer:
        block = (shape[0] // steps, shape[1])
        small = pl.BlockSpec(block, lambda i, s: (i, 0))
        large = pl.BlockSpec((1,) + block, lambda i, s: (0, s[0] * steps + i, 0))
        whole = (1, 2 * shape[0], shape[1])
    else:
        block = (shape[0], shape[1] // steps)
        small = pl.BlockSpec(block, lambda i, s: (0, i))
        large = pl.BlockSpec((1,) + block, lambda i, s: (0, 0, s[0] * steps + i))
        whole = (1, shape[0], 2 * shape[1])
    return steps, small, large, whole


def own_half(which, outer, a, b):
    steps, small, large, whole = half_specs(outer, a.shape)
    return call(
        own_half_body, "own_half", (steps,), [small, small], [large, small],
        [sds(whole, F32), sds(a.shape, BF)], bytes_=a.size * 10, flops=a.size, prefetch=1,
    )(which, a, b)


def other_half(which, outer, held, a):
    steps, small, large, whole = half_specs(outer, a.shape)
    return call(
        other_half_body, "other_half", (steps,), [pl.BlockSpec(memory_space=pl.ANY), small], large,
        sds(whole, F32), bytes_=a.size * 6, flops=a.size, prefetch=1, aliases={1: 0},
    )(which, held, a)


def layer_back(hat, scale, gain, grad):
    scaled = grad * gain
    return scale * (
        scaled - jnp.mean(scaled, axis=-1, keepdims=True) - hat * jnp.mean(scaled * hat, axis=-1, keepdims=True)
    )


def return_body(slots, tgt, r0, r1, stream, cot, gains, att_t, w, stream_grad, back, sums, w_grad, w_acc, *, gain_at):
    step = pl.program_id(0)

    @pl.when(step == 0)
    def _():
        sums[...] = jnp.zeros_like(sums)
        w_acc[...] = jnp.zeros_like(w_acc)

    grad = mm(jnp.where(tgt[...] == slots[0:1, :], 1.0, 0.0).astype(BF), r0[...])
    grad += mm(jnp.where(tgt[...] == slots[1:2, :], 1.0, 0.0).astype(BF), r1[...])
    hat, scale = normalise(stream[...])
    total = cot[...].astype(F32) + layer_back(hat, scale, gains[gain_at : gain_at + 1, :], grad)
    stream_grad[...] = total
    low = total.astype(BF)
    back[...] = mm(low, w[...], NT).astype(BF)
    w_acc[...] += mm(att_t[...], low)
    row = lax.broadcasted_iota(jnp.int32, sums.shape, 0)
    sums[...] += jnp.where(
        row == 0,
        jnp.sum(grad * hat, axis=0, keepdims=True),
        jnp.where(row == 1, jnp.sum(grad, axis=0, keepdims=True), 0.0),
    )

    @pl.when(step == pl.num_programs(0) - 1)
    def _():
        w_grad[...] = w_acc[...].astype(BF)


def return_stage(slots_row, tgt_col, r0, r1, stream, cot, gains, att_t, gathered, gain_at):
    rows, width = stream.shape
    block = pl.BlockSpec((BLOCK, width), lambda i: (i, 0))
    return call(
        functools.partial(return_body, gain_at=gain_at),
        "return",
        (rows // BLOCK,),
        [
            full(slots_row.shape),
            pl.BlockSpec((BLOCK, 1), lambda i: (i, 0)),
            full(r0.shape),
            full(r1.shape),
            block,
            block,
            full((LANES, width)),
            pl.BlockSpec((width, BLOCK), lambda i: (0, i)),
            pl.BlockSpec((width, width), lambda i: (0, 3)),
        ],
        [block, block, full((8, width)), full((width, width))],
        [sds((rows, width), F32), sds((rows, width), BF), sds((8, width), F32), sds((width, width), BF)],
        [pltpu.VMEM((width, width), F32)],
        flops=2 * rows * width * (2 * r0.shape[0] + 2 * width),
        bytes_=rows * width * 16 + 4 * width * width,
    )(slots_row, tgt_col, r0, r1, stream, cot, gains, att_t, gathered)


def last_body(dq, dk, dv, wq, wk, wv, tokens, stream_grad, gains, out, sums, *, gain_at):
    @pl.when(pl.program_id(0) == 0)
    def _():
        sums[...] = jnp.zeros_like(sums)

    grad = mm(dq[...], wq[...], NT) + mm(dk[...], wk[...], NT) + mm(dv[...], wv[...], NT)
    hat, scale = normalise(tokens[...].astype(F32))
    out[...] = stream_grad[...] + layer_back(hat, scale, gains[gain_at : gain_at + 1, :], grad)
    row = lax.broadcasted_iota(jnp.int32, sums.shape, 0)
    sums[...] += jnp.where(
        row == 0,
        jnp.sum(grad * hat, axis=0, keepdims=True),
        jnp.where(row == 1, jnp.sum(grad, axis=0, keepdims=True), 0.0),
    )


def last_stage(dq, dk, dv, gathered, tokens, stream_grad, gains, gain_at):
    rows, width = tokens.shape
    block = pl.BlockSpec((BLOCK, width), lambda i: (i, 0))
    weights = [pl.BlockSpec((width, width), functools.partial(lambda j, i: (0, j), j)) for j in range(3)]
    return call(
        functools.partial(last_body, gain_at=gain_at),
        "last",
        (rows // BLOCK,),
        [block] * 3 + weights + [block, block, full((LANES, width))],
        [block, full((8, width))],
        [sds((rows, width), F32), sds((8, width), F32)],
        flops=6 * rows * width * width,
        bytes_=rows * width * 16 + 6 * width * width,
    )(dq, dk, dv, gathered, gathered, gathered, tokens, stream_grad, gains)


def result_body(slots, tgt, r0, r1, stream, gates, out, sums):
    @pl.when(pl.program_id(0) == 0)
    def _():
        sums[...] = jnp.zeros_like(sums)

    picked = mm(jnp.where(tgt[...] == slots[0:1, :], 1.0, 0.0).astype(BF), r0[...])
    picked += mm(jnp.where(tgt[...] == slots[1:2, :], 1.0, 0.0).astype(BF), r1[...])
    moe = gates[...] * picked
    total = stream[...] + moe
    out[...] = total.astype(BF)
    row = lax.broadcasted_iota(jnp.int32, sums.shape, 0)
    sums[...] += jnp.where(row == 0, jnp.sum(total * total), jnp.where(row == 1, jnp.sum(moe * moe), 0.0))


def result_stage(slots_row, tgt_col, r0, r1, stream, gates):
    rows, width = stream.shape
    block = pl.BlockSpec((BLOCK, width), lambda i: (i, 0))
    thin = pl.BlockSpec((BLOCK, 1), lambda i: (i, 0))
    return call(
        result_body,
        "result",
        (rows // BLOCK,),
        [full(slots_row.shape), thin, full(r0.shape), full(r1.shape), block, thin],
        [block, full((8, LANES))],
        [sds((rows, width), BF), sds((8, LANES), F32)],
        flops=4 * rows * width * r0.shape[0],
        bytes_=rows * width * 10,
    )(slots_row, tgt_col, r0, r1, stream, gates)


def shards(
    tokens, cotangent, lengths, routes, mixer_weight, output_weight, first_gain, first_shift, second_gain,
    second_shift, router_weight, inner_weight, inner_bias, outer_weight, outer_bias,
):
    rows, width = tokens.shape
    shard_rows = mixer_weight.shape[0]
    experts = router_weight.shape[1]
    wide = inner_weight.shape[2]
    devices = lax.axis_size(ANYWHERE)
    capacity = 3 * rows // (2 * experts)
    half_cap = capacity // 2
    half = experts * half_cap
    total_tokens = rows * devices
    average = total_tokens / experts
    gain_one_at, gain_two_at, counts_at = experts, experts + 2, experts + 4

    slot_ids = np.arange(experts * capacity, dtype=np.int32).reshape(experts, 2, half_cap).swapaxes(0, 1).reshape(2, half)
    slots_row = jnp.asarray(slot_ids)
    slots_col = jnp.asarray(slot_ids.reshape(2 * half, 1))

    tgt_row, start_row, counts_here = prepare(lengths, routes, capacity)
    tgt_col = tgt_row.reshape(rows, 1)

    first_row = (lax.broadcasted_iota(jnp.int32, (shard_rows, 1), 0) == 0).astype(F32)
    small = jnp.concatenate(
        [
            router_weight,
            first_gain[:, None],
            first_shift[:, None],
            second_gain[:, None],
            second_shift[:, None],
            (first_row * counts_here[:, :experts]).astype(BF),
            jnp.zeros((shard_rows, LANES - 2 * experts - 4), BF),
        ],
        axis=1,
    )
    gathered = gather_rows(jnp.concatenate([mixer_weight, output_weight, small], axis=1))
    small_t = gathered[:, 4 * width :].T.astype(F32)
    counts = jnp.sum(small_t[counts_at : counts_at + experts], axis=1)
    expert_here = lax.axis_index("expert")
    balance_terms = (counts - average) / (average * total_tokens)
    bal = lax.dynamic_slice_in_dim(balance_terms, expert_here, 1).reshape(1, 1)
    rw = lax.dynamic_slice_in_dim(small_t, expert_here, 1, axis=0)

    def exchange(value):
        shaped = value.reshape(experts, half_cap, width)
        return lax.all_to_all(shaped, "expert", split_axis=0, concat_axis=0, tiled=True).reshape(half, width)

    mixed, normed_t = first_stage(tokens, small_t, gathered, gain_one_at)
    cot_placed = dispatch(slots_col, tgt_row, cotangent)
    cot_in, mixed = lax.optimization_barrier((cot_placed, mixed))
    cots = [exchange(cot_in[0]), exchange(cot_in[1])]
    att, att_t, lse = attend(mixed, start_row)
    stream, second_low, gates, second_sums = second_stage(att, gathered, tokens, small_t, routes, gain_two_at)
    placed = dispatch(slots_col, tgt_row, second_low)

    w1, w2 = inner_weight[0], outer_weight[0]
    w1t, w2t = w1.T, w2.T
    b1 = inner_bias.reshape(wide, 1).astype(F32)
    b2 = outer_bias.astype(F32)
    x0 = exchange(placed[0])
    second_half, x0 = lax.optimization_barrier((placed[1], x0))
    x1 = exchange(second_half)
    e0 = expert_stage(bal, x0, cots[0], w1t, w2, w2t, w1, b1, b2, rw)
    in0 = exchange(e0[5])
    e1 = expert_stage(bal, x1, cots[1], w1t, w2, w2t, w1, b1, b2, rw)
    in1 = exchange(e1[5])

    core = my_bit("batch", 0).reshape(1).astype(jnp.int32)
    nb_bits = bits_of(lax.axis_size("batch"))

    def over_batch(outer, acts, others):
        sent = swap(weight_grad(1 - core, outer, acts, others, width, wide), "batch", 0)
        mine = weight_grad(core, outer, acts, others, width, wide, add=sent)
        for bit in range(2, nb_bits):
            mine = (mine.astype(F32) + swap(mine, "batch", bit).astype(F32)).astype(BF)
        held, low = own_half(core, outer, mine, swap(mine, "batch", 1))
        return other_half(1 - core, outer, held, swap(low, "batch", 0))

    outer_w_sum = over_batch(True, (e0[0], e1[0]), (e0[2], e1[2]))
    inner_w_sum = over_batch(False, (e0[1], e1[1]), (e0[3], e1[3]))
    expert_rows = e0[7] + e1[7]
    biases = jnp.concatenate([expert_rows[1:2], (e0[6] + e1[6]).reshape(wide // width, width)], axis=0)
    for bit in range(nb_bits):
        biases = biases + swap(biases, "batch", bit)
    outer_b_sum = biases[:1]
    inner_b_sum = biases[1:].reshape(1, wide)

    stream_grad, attended_grad, second_grads, output_grad = return_stage(
        slots_row, tgt_col, in0, in1, stream, cotangent, small_t, att_t, gathered, gain_two_at
    )
    out0, out1, attended_grad = lax.optimization_barrier((e0[4], e1[4], attended_grad))
    outs = [exchange(out0), exchange(out1)]
    dq, dk, dv, wq, wk, wv = attend_back(mixed, attended_grad, lse, start_row, normed_t)
    input_grad, first_grads = last_stage(dq, dk, dv, gathered, tokens, stream_grad, small_t, gain_one_at)

    lane = lax.broadcasted_iota(jnp.int32, (width, LANES), 1)
    second_t = jnp.swapaxes(second_grads, 0, 1)
    router_col = jnp.swapaxes(expert_rows, 0, 1)[:, 0:1]
    small_two = jnp.where(
        lane == expert_here,
        router_col,
        jnp.where(lane == experts, second_t[:, 0:1], jnp.where(lane == experts + 1, second_t[:, 1:2], 0.0)),
    ).astype(BF)
    first_t = jnp.swapaxes(first_grads, 0, 1)
    small_one = jnp.where(lane == 0, first_t[:, 0:1], jnp.where(lane == 1, first_t[:, 1:2], 0.0)).astype(BF)
    summed_two = scatter_rows([output_grad, small_two], shard_rows)
    summed_one = scatter_rows([wq, wk, wv, small_one], shard_rows)

    block_output, result_sums = result_stage(slots_row, tgt_col, outs[0], outs[1], stream, gates)
    sums = sum_all(jnp.concatenate([second_sums[:2], result_sums[:2]], axis=0))
    gate_sums = sums[0, :experts]
    balance = jnp.sum((counts - average) / average * gate_sums) / total_tokens
    squares = jnp.stack([sums[2, 0], sums[1, 0], sums[3, 0]])
    root_means = jnp.sqrt(squares / (total_tokens * width) + 1e-06)

    return (
        block_output,
        input_grad,
        summed_one[:, : 3 * width],
        summed_two[:, :width],
        summed_one[:, 3 * width],
        summed_one[:, 3 * width + 1],
        summed_two[:, width + experts],
        summed_two[:, width + experts + 1],
        summed_two[:, width : width + experts],
        inner_w_sum,
        inner_b_sum,
        outer_w_sum,
        outer_b_sum,
        balance,
        root_means,
    )


def solution(mesh):
    everywhere = P(ANYWHERE, None)
    line = P(ANYWHERE)
    in_specs = (
        everywhere, everywhere, everywhere, everywhere, everywhere, everywhere, line, line, line, line, everywhere,
        P("expert", None, None), P("expert", None), P("expert", None, None), P("expert", None),
    )
    out_specs = (
        everywhere, everywhere, everywhere, everywhere, line, line, line, line, everywhere,
        P("expert", None, None), P("expert", None), P("expert", None, None), P("expert", None), P(), P(),
    )
    return jax.shard_map(shards, mesh=mesh, in_specs=in_specs, out_specs=out_specs, check_vma=False)
```

```python
import functools

import jax
import jax.numpy as jnp
import numpy as np
from jax import lax
from jax.experimental import pallas as pl
from jax.experimental.pallas import tpu as pltpu
from jax.sharding import PartitionSpec as P

HEADS = 12
HEAD_DIM = 64
PAIRS = HEADS // 2
WINDOW = 512
BLOCK = 256
EPSILON = 1e-05
LANES = 128
BF = jnp.bfloat16
F32 = jnp.float32
ANYWHERE = ("batch", "expert")

NT = (((1,), (1,)), ((), ()))
NN = (((1,), (0,)), ((), ()))


def mm(a, b, dims=NN):
    return lax.dot_general(a, b, dims, preferred_element_type=F32)


def call(body, name, grid, in_specs, out_specs, out_shape, scratch=(), flops=0, bytes_=0, prefetch=0, aliases=None):
    return pl.pallas_call(
        body,
        name=name,
        grid_spec=pltpu.PrefetchScalarGridSpec(
            num_scalar_prefetch=prefetch,
            grid=grid,
            in_specs=in_specs,
            out_specs=out_specs,
            scratch_shapes=list(scratch),
        ),
        out_shape=out_shape,
        input_output_aliases=aliases or {},
        cost_estimate=pl.CostEstimate(flops=int(flops), bytes_accessed=int(bytes_), transcendentals=0),
    )


def sds(shape, dtype):
    return jax.ShapeDtypeStruct(shape, dtype)


def full(shape):
    return pl.BlockSpec(shape, lambda *_: (0,) * len(shape))


def bits_of(size):
    return size.bit_length() - 1


def swap(value, axis, bit):
    size = lax.axis_size(axis)
    return lax.ppermute(value, axis, [(i, i ^ (1 << bit)) for i in range(size)])


def my_bit(axis, bit):
    return (lax.axis_index(axis) >> bit) & 1


def gather_rows(shard, beside):
    nb, ne = lax.axis_size("batch"), lax.axis_size("expert")
    value = shard
    placed = []
    order = [("expert", b) for b in reversed(range(bits_of(ne)))] + [("batch", b) for b in reversed(range(1, bits_of(nb)))]
    for step, (axis, bit) in enumerate(order):
        weight = bit + (bits_of(ne) if axis == "batch" else 0)
        spot = sum(1 for w in placed if w > weight)
        placed.append(weight)
        other = swap(value, axis, bit)
        late = step + len(beside) - len(order)
        if late >= 0:
            other = beside[late](other)
        value, other = jnp.expand_dims(value, spot), jnp.expand_dims(other, spot)
        place = lax.broadcasted_iota(jnp.int32, value.shape[:spot] + (2,) + value.shape[spot + 1 :], spot)
        value = jnp.where(place == my_bit(axis, bit), value, other)
    value = value.reshape(nb // 2, ne * shard.shape[0], shard.shape[1])
    return value, swap(value, "batch", 0)


def merge_rows(out, own, other, core, first, last):
    ny, rows = own.shape[:2]
    for y in range(ny):
        for part, which in ((own, core), (other, 1 - core)):
            out[pl.ds(pl.multiple_of((2 * y + which) * rows, 16), rows), :] = part[y, :, first:last]


def scatter_rows(keep, send, rows_each):
    nb, ne = lax.axis_size("batch"), lax.axis_size("expert")
    ny, width = keep.shape[0], keep.shape[2]
    got = swap(send, "batch", 0)
    total = (keep.astype(F32) + got.astype(F32)).astype(BF)
    total = total.reshape(ny, ne // 2, 2, rows_each, width).transpose(2, 1, 0, 3, 4)
    low = my_bit("expert", 0)
    got = swap(lax.dynamic_index_in_dim(total, 1 - low, 0, keepdims=False), "expert", 0)
    total = (lax.dynamic_index_in_dim(total, low, 0, keepdims=False).astype(F32) + got.astype(F32)).astype(BF)
    groups = [list(range(b, ne, 2)) for b in range(2)]
    pieces = lax.all_to_all(total, "expert", split_axis=0, concat_axis=0, axis_index_groups=groups, tiled=True)
    value = jnp.sum(pieces.astype(F32), axis=0)
    for bit in reversed(range(1, bits_of(nb))):
        here = my_bit("batch", bit)
        value = value.reshape((2, value.shape[0] // 2) + value.shape[1:])
        out = lax.dynamic_index_in_dim(value, 1 - here, 0, keepdims=False)
        value = lax.dynamic_index_in_dim(value, here, 0, keepdims=False) + swap(out, "batch", bit)
    return value[0]


def sum_over(value, axis):
    for bit in range(bits_of(lax.axis_size(axis))):
        value = value + swap(value, axis, bit)
    return value


def prep_body(lengths_ref, routes_row, mixer, output, router, *rest, capacity, experts):
    vectors, (tgt_row, start_row, packed) = rest[:4], rest[4:]
    rows = routes_row.shape[1]
    at = lax.broadcasted_iota(jnp.int32, (1, rows), 1)
    start = jnp.zeros((1, rows), jnp.int32)
    off = jnp.int32(0)
    for s in range(lengths_ref.shape[1]):
        start = jnp.where(at >= off, off, start)
        off = off + lengths_ref[0, s]
    start_row[...] = start
    hot = routes_row[...] == lax.broadcasted_iota(jnp.int32, (LANES, rows), 0)
    hot_low = jnp.where(hot, 1.0, 0.0).astype(BF)
    before = lax.broadcasted_iota(jnp.int32, (rows, rows), 0) < lax.broadcasted_iota(jnp.int32, (rows, rows), 1)
    ranks = mm(hot_low, jnp.where(before, 1.0, 0.0).astype(BF))
    rank = jnp.sum(jnp.where(hot, ranks, 0.0), axis=0, keepdims=True)
    tgt_row[...] = routes_row[...] * capacity + rank.astype(jnp.int32)

    own, first = mixer.shape
    wide = first + output.shape[1]
    packed[:, :first] = mixer[...]
    packed[:, first:wide] = output[...]
    row = lax.broadcasted_iota(jnp.int32, (own, LANES), 0)
    lane = lax.broadcasted_iota(jnp.int32, (own, LANES), 1)
    lane_of = lax.broadcasted_iota(jnp.int32, (LANES, LANES), 1)
    row_of = lax.broadcasted_iota(jnp.int32, (LANES, LANES), 0)
    counts = jnp.sum(jnp.where(hot, 1.0, 0.0), axis=1, keepdims=True)
    counts = jnp.sum(jnp.where(lane_of == row_of + experts + 4, counts, 0.0), axis=0, keepdims=True)
    small = jnp.where((row == 0) & (lane < 2 * experts + 4), counts, 0.0)
    for k, vector in enumerate(vectors):
        across = lax.broadcasted_iota(jnp.int32, (own, own), 0) == lax.broadcasted_iota(jnp.int32, (own, own), 1)
        column = jnp.sum(jnp.where(across, vector[...].astype(F32), 0.0), axis=1, keepdims=True)
        small = jnp.where(lane == experts + k, column, small)
    packed[:, wide:] = small.astype(BF)
    packed[:, wide : wide + experts] = router[...]


def prepare(lengths, routes, mixer, output, router, vectors, capacity):
    rows = routes.shape[0]
    own, experts = router.shape
    wide = mixer.shape[1] + output.shape[1] + LANES
    return call(
        functools.partial(prep_body, capacity=capacity, experts=experts),
        "prep",
        (1,),
        [pl.BlockSpec(memory_space=pltpu.SMEM), full((1, rows)), full(mixer.shape), full(output.shape), full(router.shape)]
        + [full((1, own))] * 4,
        [full((1, rows)), full((1, rows)), full((own, wide))],
        [sds((1, rows), jnp.int32), sds((1, rows), jnp.int32), sds((own, wide), BF)],
        flops=2 * rows * rows * LANES,
        bytes_=rows * 1024,
    )(lengths, routes.reshape(1, rows), mixer, output, router, *[v.reshape(1, own) for v in vectors])


def dispatch_body(slots, tgt, x, out):
    hot = jnp.where(slots[...] == tgt[...], 1.0, 0.0).astype(BF)
    out[...] = mm(hot, x[...]).astype(BF)


def dispatch(slots_col, tgt_row, x):
    rows, width = x.shape
    half = slots_col.shape[0]
    tile = BLOCK
    return call(
        dispatch_body,
        "dispatch",
        (half // tile,),
        [pl.BlockSpec((tile, 1), lambda t: (t, 0)), full((1, rows)), full((rows, width))],
        pl.BlockSpec((tile, width), lambda t: (t, 0)),
        sds((half, width), BF),
        flops=2 * half * rows * width,
        bytes_=rows * width * 4,
    )(slots_col, tgt_row, x)


def normalise(v):
    centre = v - jnp.mean(v, axis=-1, keepdims=True)
    spread = jnp.mean(centre * centre, axis=-1, keepdims=True)
    scale = lax.rsqrt(spread + EPSILON)
    return centre * scale, scale


def first_body(core, tokens, own, other, mixed, normed_t, output, small, gains, mixer, *, gain_at):
    @pl.when(pl.program_id(0) == 0)
    def _():
        wide, width = mixer.shape[1], output.shape[1]
        merge_rows(mixer, own, other, core[0], 0, wide)
        merge_rows(output, own, other, core[0], wide, wide + width)
        merge_rows(small, own, other, core[0], wide + width, wide + width + LANES)
        gains[...] = small[...].astype(F32).T

    hat, _ = normalise(tokens[...].astype(F32))
    normed = hat * gains[gain_at : gain_at + 1, :] + gains[gain_at + 1 : gain_at + 2, :]
    low = normed.astype(BF)
    normed_t[...] = low.T
    mixed[...] = mm(low, mixer[...]).astype(BF)


def first_stage(core, tokens, own, other, gain_at):
    rows, width = tokens.shape
    wide = 3 * width
    return call(
        functools.partial(first_body, gain_at=gain_at),
        "first",
        (rows // BLOCK,),
        [pl.BlockSpec((BLOCK, width), lambda i, s: (i, 0)), full(own.shape), full(own.shape)],
        [
            pl.BlockSpec((BLOCK, wide), lambda i, s: (i, 0)),
            pl.BlockSpec((width, BLOCK), lambda i, s: (0, i)),
            full((width, width)),
            full((width, LANES)),
            full((LANES, width)),
        ],
        [
            sds((rows, wide), BF),
            sds((width, rows), BF),
            sds((width, width), BF),
            sds((width, LANES), BF),
            sds((LANES, width), F32),
        ],
        [pltpu.VMEM((width, wide), BF)],
        flops=2 * rows * width * wide,
        bytes_=2 * (rows * (2 * width + wide) + width * wide),
        prefetch=1,
    )(core, tokens, own, other)


def fill_bias(bias, start):
    rows = bias.shape[0]
    for q in range(rows // BLOCK):
        k0 = max(0, (q + 1) * BLOCK - WINDOW - BLOCK)
        n = (q + 1) * BLOCK - k0
        key = k0 + lax.broadcasted_iota(jnp.int32, (n, BLOCK), 0)
        query = q * BLOCK + lax.broadcasted_iota(jnp.int32, (n, BLOCK), 1)
        seen = (key <= query) & (key >= start[:, q * BLOCK : (q + 1) * BLOCK])
        bias[k0 : k0 + n, q * BLOCK : (q + 1) * BLOCK] = jnp.where(seen, 0.0, -1e30)


def head_of(value, h):
    lane = lax.broadcasted_iota(jnp.int32, value.shape, 1)
    return jnp.where((lane >= HEAD_DIM * h) & (lane < HEAD_DIM * (h + 1)), value, jnp.zeros_like(value))


def attend_body(start, q, k, v, att, att_t, lse, bias, v_t):
    rows = q.shape[0]

    @pl.when(pl.program_id(0) == 0)
    def _():
        fill_bias(bias, start[...])

    v_t[...] = v[...].T
    for i in range(rows // BLOCK):
        k0 = max(0, (i + 1) * BLOCK - WINDOW - BLOCK)
        k1 = (i + 1) * BLOCK
        here = slice(i * BLOCK, k1)
        scaled = q[here, :] * jnp.asarray(HEAD_DIM**-0.5, BF)
        for h in range(2):
            s = mm(k[k0:k1, :], head_of(scaled, h), NT) + bias[k0:k1, here]
            top = jnp.max(s, axis=0, keepdims=True)
            e = jnp.exp(s - top)
            total = jnp.sum(e, axis=0, keepdims=True)
            o = mm(v_t[HEAD_DIM * h : HEAD_DIM * (h + 1), k0:k1], e.astype(BF)) / total
            att_t[HEAD_DIM * h : HEAD_DIM * (h + 1), here] = o.astype(BF)
            lse[0, h : h + 1, here] = top + jnp.log(total)
    att[...] = att_t[...].T


def attend(mixed, start_row):
    rows = mixed.shape[0]
    width = mixed.shape[1] // 3
    return call(
        attend_body,
        "attend",
        (PAIRS,),
        [
            full((1, rows)),
            pl.BlockSpec((rows, LANES), lambda p: (0, p)),
            pl.BlockSpec((rows, LANES), lambda p: (0, PAIRS + p)),
            pl.BlockSpec((rows, LANES), lambda p: (0, 2 * PAIRS + p)),
        ],
        [
            pl.BlockSpec((rows, LANES), lambda p: (0, p)),
            pl.BlockSpec((LANES, rows), lambda p: (p, 0)),
            pl.BlockSpec((1, 8, rows), lambda p: (p, 0, 0)),
        ],
        [sds((rows, width), BF), sds((width, rows), BF), sds((PAIRS, 8, rows), F32)],
        [pltpu.VMEM((rows, rows), F32), pltpu.VMEM((LANES, rows), BF)],
        flops=8 * HEADS * rows * rows * HEAD_DIM,
        bytes_=2 * rows * width * 5,
    )(start_row, mixed, mixed, mixed)


def attend_back_body(
    core, start, q, k, v, g, lse, normed_t, dq, dk, dv, keep, send, bias, k_t, dq_t, dk_acc, dv_acc, wide
):
    rows = q.shape[0]

    @pl.when(pl.program_id(0) == 0)
    def _():
        fill_bias(bias, start[...])

    k_t[...] = k[...].T
    dk_acc[...] = jnp.zeros_like(dk_acc)
    dv_acc[...] = jnp.zeros_like(dv_acc)
    for i in range(rows // BLOCK):
        k0 = max(0, (i + 1) * BLOCK - WINDOW - BLOCK)
        k1 = (i + 1) * BLOCK
        here = slice(i * BLOCK, k1)
        scaled = q[here, :] * jnp.asarray(HEAD_DIM**-0.5, BF)
        g_here = g[here, :]
        for h in range(2):
            q_h = head_of(scaled, h)
            g_h = head_of(g_here, h)
            s = mm(k[k0:k1, :], q_h, NT) + bias[k0:k1, here]
            p = jnp.exp(s - lse[0, h : h + 1, here])
            dp = mm(v[k0:k1, :], g_h, NT)
            inner = jnp.sum(p * dp, axis=0, keepdims=True)
            ds = (p * (dp - inner)).astype(BF)
            dv_acc[k0:k1, :] += mm(p.astype(BF), g_h)
            dk_acc[k0:k1, :] += mm(ds, q_h)
            dq_t[HEAD_DIM * h : HEAD_DIM * (h + 1), here] = mm(k_t[HEAD_DIM * h : HEAD_DIM * (h + 1), k0:k1], ds)
    wide[:, :LANES] = (dq_t[...].T * HEAD_DIM**-0.5).astype(BF)
    wide[:, LANES : 2 * LANES] = dk_acc[...].astype(BF)
    wide[:, 2 * LANES :] = dv_acc[...].astype(BF)
    dq[...] = wide[:, :LANES]
    dk[...] = wide[:, LANES : 2 * LANES]
    dv[...] = wide[:, 2 * LANES :]
    ny, block = keep.shape[:2]
    for y in range(ny):
        for out, which in ((keep, core[0]), (send, 1 - core[0])):
            at = pl.multiple_of((2 * y + which) * block, 16)
            out[y] = mm(normed_t[pl.ds(at, block), :], wide[...]).astype(BF)


def attend_back(core, mixed, attended_grad, lse, start_row, normed_t, first, count, ny):
    rows, width = attended_grad.shape
    block = width // (2 * ny)

    def column(offset):
        return pl.BlockSpec((rows, LANES), lambda p, s: (0, offset + first + p))

    out_column = pl.BlockSpec((rows, LANES), lambda p, s: (0, p))
    grads = pl.BlockSpec((ny, block, 3 * LANES), lambda p, s: (0, 0, p))
    return call(
        attend_back_body,
        "attend_back",
        (count,),
        [
            full((1, rows)),
            column(0),
            column(PAIRS),
            column(2 * PAIRS),
            column(0),
            pl.BlockSpec((1, 8, rows), lambda p, s: (first + p, 0, 0)),
            full((width, rows)),
        ],
        [out_column] * 3 + [grads] * 2,
        [sds((rows, LANES * count), BF)] * 3 + [sds((ny, block, 3 * LANES * count), BF)] * 2,
        [
            pltpu.VMEM((rows, rows), F32),
            pltpu.VMEM((LANES, rows), BF),
            pltpu.VMEM((LANES, rows), F32),
            pltpu.VMEM((rows, LANES), F32),
            pltpu.VMEM((rows, LANES), F32),
            pltpu.VMEM((rows, 3 * LANES), BF),
        ],
        flops=40 * count * rows * rows * HEAD_DIM,
        bytes_=2 * rows * LANES * count * 10,
        prefetch=1,
    )(core, start_row, mixed, mixed, mixed, attended_grad, lse, normed_t)


def second_body(att, w, tokens, gains, router, routes, stream, low, gates, sums, *, gain_at):
    attn = mm(att[...], w[...])
    total = tokens[...].astype(F32) + attn
    stream[...] = total
    hat, _ = normalise(total)
    normed = (hat * gains[gain_at : gain_at + 1, :] + gains[gain_at + 1 : gain_at + 2, :]).astype(BF)
    low[...] = normed
    logits = mm(normed, router[...])
    hot = routes[...] == lax.broadcasted_iota(jnp.int32, logits.shape, 1)
    gate = jax.nn.sigmoid(jnp.sum(jnp.where(hot, logits, 0.0), axis=1, keepdims=True))
    gates[...] = gate

    @pl.when(pl.program_id(0) == 0)
    def _():
        sums[...] = jnp.zeros_like(sums)

    row = lax.broadcasted_iota(jnp.int32, sums.shape, 0)
    by_expert = jnp.sum(jnp.where(hot, gate, 0.0), axis=0, keepdims=True)
    squares = jnp.sum(attn * attn)
    sums[...] += jnp.where(row == 0, by_expert, jnp.where(row == 1, squares, 0.0))


def second_stage(att, output, small, tokens, gains, routes, gain_at):
    rows, width = tokens.shape
    block = pl.BlockSpec((BLOCK, width), lambda i: (i, 0))
    thin = pl.BlockSpec((BLOCK, 1), lambda i: (i, 0))
    return call(
        functools.partial(second_body, gain_at=gain_at),
        "second",
        (rows // BLOCK,),
        [
            block,
            full((width, width)),
            block,
            full((LANES, width)),
            full((width, LANES)),
            thin,
        ],
        [block, block, thin, full((8, LANES))],
        [sds((rows, width), F32), sds((rows, width), BF), sds((rows, 1), F32), sds((8, LANES), F32)],
        flops=2 * rows * width * width,
        bytes_=rows * width * 10 + width * width * 2,
    )(att, output, tokens, gains, small, routes)


def flip_body(a, b, a_t, b_t):
    a_t[...] = a[...].T
    b_t[...] = b[...].T


def flip(inner, outer):
    width, wide = inner.shape
    tile = 512
    across = pl.BlockSpec((tile, width), lambda f: (f, 0))
    down = pl.BlockSpec((width, tile), lambda f: (0, f))
    return call(
        flip_body, "flip", (wide // tile,), [down, across], [across, down],
        [sds((wide, width), BF), sds((width, wide), BF)], bytes_=8 * width * wide,
    )(inner, outer)


def expert_body(
    bal, x, c, w1t, w2, w2t, w1, b1, b2, rw, act_t, pre_t, g_out, x_t, out, in_grad, b1_grad, rows_out,
    g, gate, out_acc, in_acc,
):
    step = pl.program_id(0)

    @pl.when(step == 0)
    def _():
        logits = jnp.sum(x[...].astype(F32) * rw[...], axis=1, keepdims=True)
        gate[...] = jax.nn.sigmoid(logits)
        g[...] = (gate[...] * c[...].astype(F32)).astype(BF)
        out_acc[...] = jnp.zeros_like(out_acc)
        in_acc[...] = jnp.zeros_like(in_acc)

    bias = jnp.broadcast_to(b1[...].astype(F32), (LANES, b1.shape[1])).T[:, :1]
    pre = mm(w1t[...], x[...], NT) + bias
    cdf = 0.5 * (1.0 + lax.erf(pre * (0.5**0.5)))
    act = (pre * cdf).astype(BF)
    slope = cdf + pre * jnp.exp(-0.5 * pre * pre) * ((2.0 * np.pi) ** -0.5)
    act_t[...] = act
    out_acc[...] += mm(w2t[...], act)
    back = (mm(w2[...], g[...], NT) * slope).astype(BF)
    pre_t[...] = back
    in_acc[...] += mm(w1[...], back)
    b1_grad[...] = mm(jnp.ones((8, back.shape[1]), BF), back, NT)

    @pl.when(step == pl.num_programs(0) - 1)
    def _():
        result = (out_acc[...].T + b2[...].astype(F32)).astype(BF)
        out[...] = result
        gate_grad = jnp.sum(c[...].astype(F32) * result.astype(F32), axis=1, keepdims=True) + bal[0, 0]
        logit_grad = gate_grad * gate[...] * (1.0 - gate[...])
        in_grad[...] = (in_acc[...].T + logit_grad * rw[...]).astype(BF)
        g_out[...] = g[...]
        x_t[...] = x[...].T
        row = lax.broadcasted_iota(jnp.int32, rows_out.shape, 0)
        router_part = jnp.sum(x[...].astype(F32) * logit_grad, axis=0, keepdims=True)
        bias_part = jnp.sum(g[...].astype(F32), axis=0, keepdims=True)
        rows_out[...] = jnp.where(row == 0, router_part, jnp.where(row == 1, bias_part, 0.0))


def expert_stage(bal, x, c, w1t, w2, w2t, w1, b1, b2, rw):
    rows, width = x.shape
    wide = w1.shape[1]
    tile = BLOCK
    across = pl.BlockSpec((tile, width), lambda f: (f, 0))
    down = pl.BlockSpec((width, tile), lambda f: (0, f))
    whole = full((rows, width))
    return call(
        expert_body,
        "expert",
        (wide // tile,),
        [
            pl.BlockSpec(memory_space=pltpu.SMEM),
            whole,
            whole,
            across,
            across,
            down,
            down,
            pl.BlockSpec((1, tile), lambda f: (0, f)),
            full((1, width)),
            full((1, width)),
        ],
        [
            pl.BlockSpec((tile, rows), lambda f: (f, 0)),
            pl.BlockSpec((tile, rows), lambda f: (f, 0)),
            whole,
            full((width, rows)),
            whole,
            whole,
            pl.BlockSpec((8, tile), lambda f: (0, f)),
            full((8, width)),
        ],
        [
            sds((wide, rows), BF),
            sds((wide, rows), BF),
            sds((rows, width), BF),
            sds((width, rows), BF),
            sds((rows, width), BF),
            sds((rows, width), BF),
            sds((8, wide), F32),
            sds((8, width), F32),
        ],
        [
            pltpu.VMEM((rows, width), BF),
            pltpu.VMEM((rows, 1), F32),
            pltpu.VMEM((width, rows), F32),
            pltpu.VMEM((width, rows), F32),
        ],
        flops=8 * rows * width * wide,
        bytes_=2 * (4 * width * wide + 2 * wide * rows + 6 * rows * width),
    )(bal, x, c, w1t, w2, w2t, w1, b1, b2, rw)


def outer_grad_body(core, a0, a1, g0, g1, *rest):
    total = mm(a0[...], g0[...]) + mm(a1[...], g1[...])
    if len(rest) == 2:
        total = total + rest[0][...].astype(F32)
    rest[-1][...] = total.astype(BF)


def inner_grad_body(core, a0, a1, x0, x1, *rest):
    total = mm(x0[...], a0[...], NT) + mm(x1[...], a1[...], NT)
    if len(rest) == 2:
        total = total + rest[0][...].astype(F32)
    rest[-1][...] = total.astype(BF)


def weight_grad(which, outer, acts, others, width, wide, add=None):
    tile = 512
    steps = wide // 2 // tile
    rows = acts[0].shape[1]
    a_spec = pl.BlockSpec((tile, rows), lambda f, s: (s[0] * steps + f, 0))
    if outer:
        o_spec = pl.BlockSpec((tile, width), lambda f, s: (f, 0))
        shape = (wide // 2, width)
    else:
        o_spec = pl.BlockSpec((width, tile), lambda f, s: (0, f))
        shape = (width, wide // 2)
    specs = [a_spec, a_spec, full(others[0].shape), full(others[1].shape)]
    operands = [which, acts[0], acts[1], others[0], others[1]]
    if add is not None:
        specs.append(o_spec)
        operands.append(add)
    return call(
        outer_grad_body if outer else inner_grad_body,
        "weight_grad",
        (steps,),
        specs,
        o_spec,
        sds(shape, BF),
        flops=2 * rows * width * wide,
        bytes_=2 * (wide * rows + 2 * rows * width + width * wide),
        prefetch=1,
    )(*operands)


def own_half_body(which, a, b, out, low):
    total = a[...].astype(F32) + b[...].astype(F32)
    low[...] = total.astype(BF)
    out[0] = total.astype(BF).astype(F32)


def other_half_body(which, held, a, out):
    out[0] = a[...].astype(F32)


def half_specs(outer, shape):
    steps = 3
    if outer:
        block = (shape[0] // steps, shape[1])
        small = pl.BlockSpec(block, lambda i, s: (i, 0))
        large = pl.BlockSpec((1,) + block, lambda i, s: (0, s[0] * steps + i, 0))
        whole = (1, 2 * shape[0], shape[1])
    else:
        block = (shape[0], shape[1] // steps)
        small = pl.BlockSpec(block, lambda i, s: (0, i))
        large = pl.BlockSpec((1,) + block, lambda i, s: (0, 0, s[0] * steps + i))
        whole = (1, shape[0], 2 * shape[1])
    return steps, small, large, whole


def own_half(which, outer, a, b):
    steps, small, large, whole = half_specs(outer, a.shape)
    return call(
        own_half_body, "own_half", (steps,), [small, small], [large, small],
        [sds(whole, F32), sds(a.shape, BF)], bytes_=a.size * 10, flops=a.size, prefetch=1,
    )(which, a, b)


def other_half(which, outer, held, a):
    steps, small, large, whole = half_specs(outer, a.shape)
    return call(
        other_half_body, "other_half", (steps,), [pl.BlockSpec(memory_space=pl.ANY), small], large,
        sds(whole, F32), bytes_=a.size * 6, flops=a.size, prefetch=1, aliases={1: 0},
    )(which, held, a)


def layer_back(hat, scale, gain, grad):
    scaled = grad * gain
    return scale * (
        scaled - jnp.mean(scaled, axis=-1, keepdims=True) - hat * jnp.mean(scaled * hat, axis=-1, keepdims=True)
    )


def return_body(
    core, slots, tgt, r0, r1, stream, cot, gains, att_t, w, stream_grad, back, sums, keep, send, w_acc, *, gain_at
):
    step = pl.program_id(0)

    @pl.when(step == 0)
    def _():
        sums[...] = jnp.zeros_like(sums)
        w_acc[...] = jnp.zeros_like(w_acc)

    grad = mm(jnp.where(tgt[...] == slots[0:1, :], 1.0, 0.0).astype(BF), r0[...])
    grad += mm(jnp.where(tgt[...] == slots[1:2, :], 1.0, 0.0).astype(BF), r1[...])
    hat, scale = normalise(stream[...])
    total = cot[...].astype(F32) + layer_back(hat, scale, gains[gain_at : gain_at + 1, :], grad)
    stream_grad[...] = total
    low = total.astype(BF)
    back[...] = mm(low, w[...], NT).astype(BF)
    w_acc[...] += mm(att_t[...], low)
    row = lax.broadcasted_iota(jnp.int32, sums.shape, 0)
    sums[...] += jnp.where(
        row == 0,
        jnp.sum(grad * hat, axis=0, keepdims=True),
        jnp.where(row == 1, jnp.sum(grad, axis=0, keepdims=True), 0.0),
    )

    @pl.when(step == pl.num_programs(0) - 1)
    def _():
        ny, block = keep.shape[:2]
        for y in range(ny):
            for out, which in ((keep, core[0]), (send, 1 - core[0])):
                at = pl.multiple_of((2 * y + which) * block, 16)
                out[y] = w_acc[pl.ds(at, block), :].astype(BF)


def return_stage(core, slots_row, tgt_col, r0, r1, stream, cot, gains, att_t, output, gain_at, ny):
    rows, width = stream.shape
    block = pl.BlockSpec((BLOCK, width), lambda i, s: (i, 0))
    grads = (ny, width // (2 * ny), width)
    return call(
        functools.partial(return_body, gain_at=gain_at),
        "return",
        (rows // BLOCK,),
        [
            full(slots_row.shape),
            pl.BlockSpec((BLOCK, 1), lambda i, s: (i, 0)),
            full(r0.shape),
            full(r1.shape),
            block,
            block,
            full((LANES, width)),
            pl.BlockSpec((width, BLOCK), lambda i, s: (0, i)),
            full((width, width)),
        ],
        [block, block, full((8, width)), full(grads), full(grads)],
        [sds((rows, width), F32), sds((rows, width), BF), sds((8, width), F32), sds(grads, BF), sds(grads, BF)],
        [pltpu.VMEM((width, width), F32)],
        flops=2 * rows * width * (2 * r0.shape[0] + 2 * width),
        bytes_=rows * width * 16 + 4 * width * width,
        prefetch=1,
    )(core, slots_row, tgt_col, r0, r1, stream, cot, gains, att_t, output)


def last_body(*refs, gain_at, splits):
    core, parts, (own, other, tokens, stream_grad, gains, out, sums, mixer) = refs[0], refs[1:-8], refs[-8:]

    @pl.when(pl.program_id(0) == 0)
    def _():
        merge_rows(mixer, own, other, core[0], 0, mixer.shape[1])
        sums[...] = jnp.zeros_like(sums)

    width = tokens.shape[1]
    grad = jnp.zeros(tokens.shape, F32)
    for n, (first, count) in enumerate(splits):
        for j in range(3):
            at = j * width + first * LANES
            grad += mm(parts[3 * n + j][...], mixer[:, at : at + count * LANES], NT)
    hat, scale = normalise(tokens[...].astype(F32))
    out[...] = stream_grad[...] + layer_back(hat, scale, gains[gain_at : gain_at + 1, :], grad)
    row = lax.broadcasted_iota(jnp.int32, sums.shape, 0)
    sums[...] += jnp.where(
        row == 0,
        jnp.sum(grad * hat, axis=0, keepdims=True),
        jnp.where(row == 1, jnp.sum(grad, axis=0, keepdims=True), 0.0),
    )


def last_stage(core, parts, splits, own, other, tokens, stream_grad, gains, gain_at):
    rows, width = tokens.shape
    block = pl.BlockSpec((BLOCK, width), lambda i, s: (i, 0))
    weight = pl.BlockSpec(own.shape[:2] + (3 * width,), lambda i, s: (0, 0, 0))
    return call(
        functools.partial(last_body, gain_at=gain_at, splits=splits),
        "last",
        (rows // BLOCK,),
        [pl.BlockSpec((BLOCK, p.shape[1]), lambda i, s: (i, 0)) for p in parts]
        + [weight, weight, block, block, full((LANES, width))],
        [block, full((8, width))],
        [sds((rows, width), F32), sds((8, width), F32)],
        [pltpu.VMEM((width, 3 * width), BF)],
        flops=6 * rows * width * width,
        bytes_=rows * width * 16 + 6 * width * width,
        prefetch=1,
    )(core, *parts, own, other, tokens, stream_grad, gains)


def result_body(slots, tgt, r0, r1, stream, gates, out, sums):
    @pl.when(pl.program_id(0) == 0)
    def _():
        sums[...] = jnp.zeros_like(sums)

    picked = mm(jnp.where(tgt[...] == slots[0:1, :], 1.0, 0.0).astype(BF), r0[...])
    picked += mm(jnp.where(tgt[...] == slots[1:2, :], 1.0, 0.0).astype(BF), r1[...])
    moe = gates[...] * picked
    total = stream[...] + moe
    out[...] = total.astype(BF)
    row = lax.broadcasted_iota(jnp.int32, sums.shape, 0)
    sums[...] += jnp.where(row == 0, jnp.sum(total * total), jnp.where(row == 1, jnp.sum(moe * moe), 0.0))


def result_stage(slots_row, tgt_col, r0, r1, stream, gates):
    rows, width = stream.shape
    block = pl.BlockSpec((BLOCK, width), lambda i: (i, 0))
    thin = pl.BlockSpec((BLOCK, 1), lambda i: (i, 0))
    return call(
        result_body,
        "result",
        (rows // BLOCK,),
        [full(slots_row.shape), thin, full(r0.shape), full(r1.shape), block, thin],
        [block, full((8, LANES))],
        [sds((rows, width), BF), sds((8, LANES), F32)],
        flops=4 * rows * width * r0.shape[0],
        bytes_=rows * width * 10,
    )(slots_row, tgt_col, r0, r1, stream, gates)


def collect_body(expert_here, r0, r1, b0, b1, second, first, forward, result, out, *, experts):
    row = lax.broadcasted_iota(jnp.int32, (experts, out.shape[1]), 0)
    router = r0[0:1, :] + r1[0:1, :]
    width = out.shape[1]
    out[...] = jnp.zeros_like(out)
    out[:experts, :] = jnp.where(row == expert_here[0], router, 0.0)
    out[experts : experts + 2, :] = second[0:2, :]
    out[experts + 2 : experts + 4, :] = first[0:2, :]
    at = experts + 4
    for k, (ref, line) in enumerate(((forward, 0), (forward, 1), (result, 0), (result, 1))):
        out[at : at + 1, k * LANES : (k + 1) * LANES] = ref[line : line + 1, :]
    out[at + 1 : at + 2, :] = r0[1:2, :] + r1[1:2, :]
    for k in range(b0.shape[1] // width):
        cut = slice(k * width, (k + 1) * width)
        out[at + 2 + k : at + 3 + k, :] = b0[0:1, cut] + b1[0:1, cut]


def collect(expert_here, experts, arrays):
    width = arrays[0].shape[1]
    shape = (experts + 6 + arrays[2].shape[1] // width, width)
    return call(
        functools.partial(collect_body, experts=experts),
        "collect",
        (1,),
        [pl.BlockSpec(memory_space=pltpu.SMEM)] + [full(a.shape) for a in arrays],
        full(shape),
        sds(shape, F32),
        bytes_=4 * shape[0] * width,
    )(expert_here, *arrays)


def shards(
    tokens, cotangent, lengths, routes, mixer_weight, output_weight, first_gain, first_shift, second_gain,
    second_shift, router_weight, inner_weight, inner_bias, outer_weight, outer_bias,
):
    rows, width = tokens.shape
    shard_rows = mixer_weight.shape[0]
    experts = router_weight.shape[1]
    wide = inner_weight.shape[2]
    devices = lax.axis_size(ANYWHERE)
    capacity = 3 * rows // (2 * experts)
    half_cap = capacity // 2
    half = experts * half_cap
    total_tokens = rows * devices
    average = total_tokens / experts
    gain_one_at, gain_two_at, counts_at = experts, experts + 2, experts + 4

    slot_ids = np.arange(experts * capacity, dtype=np.int32).reshape(experts, 2, half_cap).swapaxes(0, 1).reshape(2, half)
    slots_row = jnp.asarray(slot_ids)
    slots_col = [jnp.asarray(slot_ids[c].reshape(half, 1)) for c in range(2)]

    tgt_row, start_row, packed = prepare(
        lengths, routes, mixer_weight, output_weight, router_weight,
        (first_gain, first_shift, second_gain, second_shift), capacity,
    )
    tgt_col = tgt_row.reshape(rows, 1)
    expert_here = lax.axis_index("expert")
    core = my_bit("batch", 0).reshape(1).astype(jnp.int32)
    nb_bits = bits_of(lax.axis_size("batch"))
    ny = lax.axis_size("batch") // 2

    def exchange(value):
        shaped = value.reshape(experts, half_cap, width)
        return lax.all_to_all(shaped, "expert", split_axis=0, concat_axis=0, tiled=True).reshape(half, width)

    w1, w2 = inner_weight[0], outer_weight[0]
    ready = {}

    def beside(name, make):
        def run(other):
            other, *ready[name] = lax.optimization_barrier((other, *make()))
            return other

        return run

    own_rows, other_rows = gather_rows(
        packed,
        [
            beside("cot0", lambda: [dispatch(slots_col[0], tgt_row, cotangent)]),
            beside("cot1", lambda: [dispatch(slots_col[1], tgt_row, cotangent)]),
            beside("weights", lambda: flip(w1, w2)),
            beside("sent0", lambda: [exchange(ready["cot0"][0])]),
        ],
    )
    w1t, w2t = ready["weights"]
    (cot0,) = ready["sent0"]
    cot1 = exchange(ready["cot1"][0])

    mixed, normed_t, output_full, small, small_t = first_stage(core, tokens, own_rows, other_rows, gain_one_at)
    counts = jnp.sum(small_t[counts_at : counts_at + experts], axis=1)
    balance_terms = (counts - average) / (average * total_tokens)
    bal = lax.dynamic_slice_in_dim(balance_terms, expert_here, 1).reshape(1, 1)
    rw = lax.dynamic_slice_in_dim(small_t, expert_here, 1, axis=0)
    att, att_t, lse = attend(mixed, start_row)
    att, bal, rw, tgt_col = lax.optimization_barrier((att, bal, rw, tgt_col))
    stream, second_low, gates, second_sums = second_stage(att, output_full, small, tokens, small_t, routes, gain_two_at)
    placed = [dispatch(slots_col[c], tgt_row, second_low) for c in range(2)]

    placed0, cot1 = lax.optimization_barrier((placed[0], cot1))
    x0 = exchange(placed0)
    second_half, x0 = lax.optimization_barrier((placed[1], x0))
    x1 = exchange(second_half)
    e0 = expert_stage(bal, x0, cot0, w1t, w2, w2t, w1, inner_bias, outer_bias, rw)
    in0 = exchange(e0[5])
    e1 = expert_stage(bal, x1, cot1, w1t, w2, w2t, w1, inner_bias, outer_bias, rw)
    in1 = exchange(e1[5])

    def halves(outer, acts, others):
        sent = swap(weight_grad(1 - core, outer, acts, others, width, wide), "batch", 0)
        return sent, weight_grad(core, outer, acts, others, width, wide)

    def together(parts):
        mine = (parts[0].astype(F32) + parts[1].astype(F32)).astype(BF)
        for bit in range(2, nb_bits):
            mine = (mine.astype(F32) + swap(mine, "batch", bit).astype(F32)).astype(BF)
        return mine

    outer_parts = halves(True, (e0[0], e1[0]), (e0[2], e1[2]))
    inner_parts = halves(False, (e0[1], e1[1]), (e0[3], e1[3]))
    in0, in1, outer_parts, inner_parts, out0_in = lax.optimization_barrier((in0, in1, outer_parts, inner_parts, e0[4]))
    outer_mine, inner_mine = together(outer_parts), together(inner_parts)
    outer_far = swap(outer_mine, "batch", 1)
    out0 = exchange(out0_in)

    in1, inner_mine = lax.optimization_barrier((in1, inner_mine))
    stream_grad, attended_grad, second_grads, out_keep, out_send = return_stage(
        core, slots_row, tgt_col, in0, in1, stream, cotangent, small_t, att_t, output_full, gain_two_at, ny
    )
    splits = ((0, PAIRS - 2), (PAIRS - 2, 2))
    *parts_a, keep_a, send_a = attend_back(core, mixed, attended_grad, lse, start_row, normed_t, *splits[0], ny)
    attended_grad, send_a, out0, out1_in, outer_far, inner_mine = lax.optimization_barrier(
        (attended_grad, send_a, out0, e1[4], outer_far, inner_mine)
    )
    inner_far = swap(inner_mine, "batch", 1)
    out1 = exchange(out1_in)
    *parts_b, keep_b, send_b = attend_back(core, mixed, attended_grad, lse, start_row, normed_t, *splits[1], ny)
    output_grad = scatter_rows(out_keep, out_send, shard_rows)
    mixer_a = scatter_rows(keep_a, send_a, shard_rows)
    mixer_b = scatter_rows(keep_b, send_b, shard_rows)
    input_grad, first_grads = last_stage(
        core, parts_a + parts_b, splits, own_rows, other_rows, tokens, stream_grad, small_t, gain_one_at
    )
    mixer_grad = jnp.concatenate([mixer_a, mixer_b], axis=1).reshape(shard_rows, PAIRS, 3, LANES)
    mixer_grad = jnp.swapaxes(mixer_grad, 1, 2).reshape(shard_rows, 3 * width)

    def give_back(outer, mine, far):
        held, low = own_half(core, outer, mine, far)
        return other_half(1 - core, outer, held, swap(low, "batch", 0))

    outer_w_sum = give_back(True, outer_mine, outer_far)
    inner_w_sum = give_back(False, inner_mine, inner_far)

    block_output, result_sums = result_stage(slots_row, tgt_col, out0, out1, stream, gates)
    sums = collect(
        expert_here.reshape(1).astype(jnp.int32), experts,
        (e0[7], e1[7], e0[6], e1[6], second_grads, first_grads, second_sums, result_sums),
    )
    sums = sum_over(sums, "batch")
    outer_b_sum = sums[experts + 5 : experts + 6]
    inner_b_sum = sums[experts + 6 :].reshape(1, wide)
    sums = sum_over(sums[: experts + 5], "expert")
    device = lax.axis_index("batch") * experts + expert_here
    mine = lax.dynamic_slice_in_dim(sums[: experts + 4], device * shard_rows, shard_rows, axis=1)
    numbers = sums[experts + 4]
    balance = jnp.sum((counts - average) / average * numbers[:experts]) / total_tokens
    squares = jnp.stack([numbers[2 * LANES], numbers[LANES], numbers[3 * LANES]])
    root_means = jnp.sqrt(squares / (total_tokens * width) + 1e-06)

    return (
        block_output,
        input_grad,
        mixer_grad,
        output_grad,
        mine[experts + 2],
        mine[experts + 3],
        mine[experts],
        mine[experts + 1],
        mine[:experts].T,
        inner_w_sum,
        inner_b_sum,
        outer_w_sum,
        outer_b_sum,
        balance,
        root_means,
    )


def solution(mesh):
    everywhere = P(ANYWHERE, None)
    line = P(ANYWHERE)
    in_specs = (
        everywhere, everywhere, everywhere, everywhere, everywhere, everywhere, line, line, line, line, everywhere,
        P("expert", None, None), P("expert", None), P("expert", None, None), P("expert", None),
    )
    out_specs = (
        everywhere, everywhere, everywhere, everywhere, line, line, line, line, everywhere,
        P("expert", None, None), P("expert", None), P("expert", None, None), P("expert", None), P(), P(),
    )
    return jax.shard_map(shards, mesh=mesh, in_specs=in_specs, out_specs=out_specs, check_vma=False)
```

```python
import functools

import jax
import jax.numpy as jnp
import numpy as np
from jax import lax
from jax.experimental import pallas as pl
from jax.experimental.pallas import tpu as pltpu
from jax.sharding import PartitionSpec as P

HEADS = 12
HEAD_DIM = 64
PAIRS = HEADS // 2
WINDOW = 512
BLOCK = 256
EPSILON = 1e-05
LANES = 128
BF = jnp.bfloat16
F32 = jnp.float32
ANYWHERE = ("batch", "expert")

NT = (((1,), (1,)), ((), ()))
NN = (((1,), (0,)), ((), ()))


def mm(a, b, dims=NN):
    return lax.dot_general(a, b, dims, preferred_element_type=F32)


def call(body, name, grid, in_specs, out_specs, out_shape, scratch=(), flops=0, bytes_=0, prefetch=0, aliases=None):
    return pl.pallas_call(
        body,
        name=name,
        grid_spec=pltpu.PrefetchScalarGridSpec(
            num_scalar_prefetch=prefetch,
            grid=grid,
            in_specs=in_specs,
            out_specs=out_specs,
            scratch_shapes=list(scratch),
        ),
        out_shape=out_shape,
        input_output_aliases=aliases or {},
        cost_estimate=pl.CostEstimate(flops=int(flops), bytes_accessed=int(bytes_), transcendentals=0),
    )


def sds(shape, dtype):
    return jax.ShapeDtypeStruct(shape, dtype)


def full(shape):
    return pl.BlockSpec(shape, lambda *_: (0,) * len(shape))


def bits_of(size):
    return size.bit_length() - 1


def swap(value, axis, bit):
    size = lax.axis_size(axis)
    return lax.ppermute(value, axis, [(i, i ^ (1 << bit)) for i in range(size)])


def my_bit(axis, bit):
    return (lax.axis_index(axis) >> bit) & 1


def gather_rows(shard, beside):
    nb, ne = lax.axis_size("batch"), lax.axis_size("expert")
    value = shard
    placed = []
    order = [("expert", b) for b in reversed(range(bits_of(ne)))] + [("batch", b) for b in reversed(range(1, bits_of(nb)))]
    for step, (axis, bit) in enumerate(order):
        weight = bit + (bits_of(ne) if axis == "batch" else 0)
        spot = sum(1 for w in placed if w > weight)
        placed.append(weight)
        other = swap(value, axis, bit)
        late = step + len(beside) - len(order)
        if late >= 0:
            other = beside[late](other)
        value, other = jnp.expand_dims(value, spot), jnp.expand_dims(other, spot)
        place = lax.broadcasted_iota(jnp.int32, value.shape[:spot] + (2,) + value.shape[spot + 1 :], spot)
        value = jnp.where(place == my_bit(axis, bit), value, other)
    value = value.reshape(nb // 2, ne * shard.shape[0], shard.shape[1])
    return value, swap(value, "batch", 0)


def merge_rows(out, own, other, core, first, last):
    ny, rows = own.shape[:2]
    for y in range(ny):
        for part, which in ((own, core), (other, 1 - core)):
            out[pl.ds(pl.multiple_of((2 * y + which) * rows, 16), rows), :] = part[y, :, first:last]


def add_low(a, b):
    return (a.astype(F32) + b.astype(F32)).astype(BF)


def over_cores(keep, send):
    return add_low(keep, swap(send, "batch", 0))


def over_x(total):
    ny, rows, width = total.shape
    ne = lax.axis_size("expert")
    total = total.reshape(ny, ne // 2, 2, rows // ne, width).transpose(2, 1, 0, 3, 4)
    low = my_bit("expert", 0)
    got = swap(lax.dynamic_index_in_dim(total, 1 - low, 0, keepdims=False), "expert", 0)
    return add_low(lax.dynamic_index_in_dim(total, low, 0, keepdims=False), got)


def over_rest(total):
    ne = lax.axis_size("expert")
    groups = [list(range(b, ne, 2)) for b in range(2)]
    pieces = lax.all_to_all(total, "expert", split_axis=0, concat_axis=0, axis_index_groups=groups, tiled=True)
    value = jnp.sum(pieces.astype(F32), axis=0)
    for bit in reversed(range(1, bits_of(lax.axis_size("batch")))):
        here = my_bit("batch", bit)
        value = value.reshape((2, value.shape[0] // 2) + value.shape[1:])
        out = lax.dynamic_index_in_dim(value, 1 - here, 0, keepdims=False)
        value = lax.dynamic_index_in_dim(value, here, 0, keepdims=False) + swap(out, "batch", bit)
    return value[0]


def prep_body(lengths_ref, routes_row, mixer, output, router, *rest, capacity, experts):
    vectors, (tgt_row, start_row, packed) = rest[:4], rest[4:]
    rows = routes_row.shape[1]
    at = lax.broadcasted_iota(jnp.int32, (1, rows), 1)
    start = jnp.zeros((1, rows), jnp.int32)
    off = jnp.int32(0)
    for s in range(lengths_ref.shape[1]):
        start = jnp.where(at >= off, off, start)
        off = off + lengths_ref[0, s]
    start_row[...] = start
    hot = routes_row[...] == lax.broadcasted_iota(jnp.int32, (LANES, rows), 0)
    hot_low = jnp.where(hot, 1.0, 0.0).astype(BF)
    before = lax.broadcasted_iota(jnp.int32, (rows, rows), 0) < lax.broadcasted_iota(jnp.int32, (rows, rows), 1)
    ranks = mm(hot_low, jnp.where(before, 1.0, 0.0).astype(BF))
    rank = jnp.sum(jnp.where(hot, ranks, 0.0), axis=0, keepdims=True)
    tgt_row[...] = routes_row[...] * capacity + rank.astype(jnp.int32)

    own, first = mixer.shape
    wide = first + output.shape[1]
    packed[:, :first] = mixer[...]
    packed[:, first:wide] = output[...]
    row = lax.broadcasted_iota(jnp.int32, (own, LANES), 0)
    lane = lax.broadcasted_iota(jnp.int32, (own, LANES), 1)
    lane_of = lax.broadcasted_iota(jnp.int32, (LANES, LANES), 1)
    row_of = lax.broadcasted_iota(jnp.int32, (LANES, LANES), 0)
    counts = jnp.sum(jnp.where(hot, 1.0, 0.0), axis=1, keepdims=True)
    counts = jnp.sum(jnp.where(lane_of == row_of + experts + 4, counts, 0.0), axis=0, keepdims=True)
    small = jnp.where((row == 0) & (lane < 2 * experts + 4), counts, 0.0)
    for k, vector in enumerate(vectors):
        across = lax.broadcasted_iota(jnp.int32, (own, own), 0) == lax.broadcasted_iota(jnp.int32, (own, own), 1)
        column = jnp.sum(jnp.where(across, vector[...].astype(F32), 0.0), axis=1, keepdims=True)
        small = jnp.where(lane == experts + k, column, small)
    packed[:, wide:] = small.astype(BF)
    packed[:, wide : wide + experts] = router[...]


def prepare(lengths, routes, mixer, output, router, vectors, capacity):
    rows = routes.shape[0]
    own, experts = router.shape
    wide = mixer.shape[1] + output.shape[1] + LANES
    return call(
        functools.partial(prep_body, capacity=capacity, experts=experts),
        "prep",
        (1,),
        [pl.BlockSpec(memory_space=pltpu.SMEM), full((1, rows)), full(mixer.shape), full(output.shape), full(router.shape)]
        + [full((1, own))] * 4,
        [full((1, rows)), full((1, rows)), full((own, wide))],
        [sds((1, rows), jnp.int32), sds((1, rows), jnp.int32), sds((own, wide), BF)],
        flops=2 * rows * rows * LANES,
        bytes_=rows * 1024,
    )(lengths, routes.reshape(1, rows), mixer, output, router, *[v.reshape(1, own) for v in vectors])


def dispatch_body(slots, tgt, x, out):
    hot = jnp.where(slots[...] == tgt[...], 1.0, 0.0).astype(BF)
    out[...] = mm(hot, x[...]).astype(BF)


def dispatch(slots_col, tgt_row, x):
    rows, width = x.shape
    half = slots_col.shape[0]
    tile = BLOCK
    return call(
        dispatch_body,
        "dispatch",
        (half // tile,),
        [pl.BlockSpec((tile, 1), lambda t: (t, 0)), full((1, rows)), full((rows, width))],
        pl.BlockSpec((tile, width), lambda t: (t, 0)),
        sds((half, width), BF),
        flops=2 * half * rows * width,
        bytes_=rows * width * 4,
    )(slots_col, tgt_row, x)


def normalise(v):
    centre = v - jnp.mean(v, axis=-1, keepdims=True)
    spread = jnp.mean(centre * centre, axis=-1, keepdims=True)
    scale = lax.rsqrt(spread + EPSILON)
    return centre * scale, scale


def first_body(core, tokens, own, other, mixed, normed_t, output, small, gains, mixer, *, gain_at):
    @pl.when(pl.program_id(0) == 0)
    def _():
        wide, width = mixer.shape[1], output.shape[1]
        merge_rows(mixer, own, other, core[0], 0, wide)
        merge_rows(output, own, other, core[0], wide, wide + width)
        merge_rows(small, own, other, core[0], wide + width, wide + width + LANES)
        gains[...] = small[...].astype(F32).T

    hat, _ = normalise(tokens[...].astype(F32))
    normed = hat * gains[gain_at : gain_at + 1, :] + gains[gain_at + 1 : gain_at + 2, :]
    low = normed.astype(BF)
    normed_t[...] = low.T
    mixed[...] = mm(low, mixer[...]).astype(BF)


def first_stage(core, tokens, own, other, gain_at):
    rows, width = tokens.shape
    wide = 3 * width
    return call(
        functools.partial(first_body, gain_at=gain_at),
        "first",
        (rows // BLOCK,),
        [pl.BlockSpec((BLOCK, width), lambda i, s: (i, 0)), full(own.shape), full(own.shape)],
        [
            pl.BlockSpec((BLOCK, wide), lambda i, s: (i, 0)),
            pl.BlockSpec((width, BLOCK), lambda i, s: (0, i)),
            full((width, width)),
            full((width, LANES)),
            full((LANES, width)),
        ],
        [
            sds((rows, wide), BF),
            sds((width, rows), BF),
            sds((width, width), BF),
            sds((width, LANES), BF),
            sds((LANES, width), F32),
        ],
        [pltpu.VMEM((width, wide), BF)],
        flops=2 * rows * width * wide,
        bytes_=2 * (rows * (2 * width + wide) + width * wide),
        prefetch=1,
    )(core, tokens, own, other)


def fill_bias(bias, start):
    rows = bias.shape[0]
    for q in range(rows // BLOCK):
        k0 = max(0, (q + 1) * BLOCK - WINDOW - BLOCK)
        n = (q + 1) * BLOCK - k0
        key = k0 + lax.broadcasted_iota(jnp.int32, (n, BLOCK), 0)
        query = q * BLOCK + lax.broadcasted_iota(jnp.int32, (n, BLOCK), 1)
        seen = (key <= query) & (key >= start[:, q * BLOCK : (q + 1) * BLOCK])
        bias[k0 : k0 + n, q * BLOCK : (q + 1) * BLOCK] = jnp.where(seen, 0.0, -1e30)


def head_of(value, h):
    lane = lax.broadcasted_iota(jnp.int32, value.shape, 1)
    return jnp.where((lane >= HEAD_DIM * h) & (lane < HEAD_DIM * (h + 1)), value, jnp.zeros_like(value))


def attend_body(start, q, k, v, att, att_t, lse, bias, v_t):
    rows = q.shape[0]

    @pl.when(pl.program_id(0) == 0)
    def _():
        fill_bias(bias, start[...])

    v_t[...] = v[...].T
    for i in range(rows // BLOCK):
        k0 = max(0, (i + 1) * BLOCK - WINDOW - BLOCK)
        k1 = (i + 1) * BLOCK
        here = slice(i * BLOCK, k1)
        scaled = q[here, :] * jnp.asarray(HEAD_DIM**-0.5, BF)
        for h in range(2):
            s = mm(k[k0:k1, :], head_of(scaled, h), NT) + bias[k0:k1, here]
            top = jnp.max(s, axis=0, keepdims=True)
            e = jnp.exp(s - top)
            total = jnp.sum(e, axis=0, keepdims=True)
            o = mm(v_t[HEAD_DIM * h : HEAD_DIM * (h + 1), k0:k1], e.astype(BF)) / total
            att_t[HEAD_DIM * h : HEAD_DIM * (h + 1), here] = o.astype(BF)
            lse[0, h : h + 1, here] = top + jnp.log(total)
    att[...] = att_t[...].T


def attend(mixed, start_row):
    rows = mixed.shape[0]
    width = mixed.shape[1] // 3
    return call(
        attend_body,
        "attend",
        (PAIRS,),
        [
            full((1, rows)),
            pl.BlockSpec((rows, LANES), lambda p: (0, p)),
            pl.BlockSpec((rows, LANES), lambda p: (0, PAIRS + p)),
            pl.BlockSpec((rows, LANES), lambda p: (0, 2 * PAIRS + p)),
        ],
        [
            pl.BlockSpec((rows, LANES), lambda p: (0, p)),
            pl.BlockSpec((LANES, rows), lambda p: (p, 0)),
            pl.BlockSpec((1, 8, rows), lambda p: (p, 0, 0)),
        ],
        [sds((rows, width), BF), sds((width, rows), BF), sds((PAIRS, 8, rows), F32)],
        [pltpu.VMEM((rows, rows), F32), pltpu.VMEM((LANES, rows), BF)],
        flops=8 * HEADS * rows * rows * HEAD_DIM,
        bytes_=2 * rows * width * 5,
    )(start_row, mixed, mixed, mixed)


def attend_back_body(
    core, start, q, k, v, g, lse, normed_t, dq, dk, dv, keep, send, bias, k_t, dq_t, dk_acc, dv_acc, wide
):
    rows = q.shape[0]

    @pl.when(pl.program_id(0) == 0)
    def _():
        fill_bias(bias, start[...])

    k_t[...] = k[...].T
    dk_acc[...] = jnp.zeros_like(dk_acc)
    dv_acc[...] = jnp.zeros_like(dv_acc)
    for i in range(rows // BLOCK):
        k0 = max(0, (i + 1) * BLOCK - WINDOW - BLOCK)
        k1 = (i + 1) * BLOCK
        here = slice(i * BLOCK, k1)
        scaled = q[here, :] * jnp.asarray(HEAD_DIM**-0.5, BF)
        g_here = g[here, :]
        for h in range(2):
            q_h = head_of(scaled, h)
            g_h = head_of(g_here, h)
            s = mm(k[k0:k1, :], q_h, NT) + bias[k0:k1, here]
            p = jnp.exp(s - lse[0, h : h + 1, here])
            dp = mm(v[k0:k1, :], g_h, NT)
            inner = jnp.sum(p * dp, axis=0, keepdims=True)
            ds = (p * (dp - inner)).astype(BF)
            dv_acc[k0:k1, :] += mm(p.astype(BF), g_h)
            dk_acc[k0:k1, :] += mm(ds, q_h)
            dq_t[HEAD_DIM * h : HEAD_DIM * (h + 1), here] = mm(k_t[HEAD_DIM * h : HEAD_DIM * (h + 1), k0:k1], ds)
    wide[:, :LANES] = (dq_t[...].T * HEAD_DIM**-0.5).astype(BF)
    wide[:, LANES : 2 * LANES] = dk_acc[...].astype(BF)
    wide[:, 2 * LANES :] = dv_acc[...].astype(BF)
    dq[...] = wide[:, :LANES]
    dk[...] = wide[:, LANES : 2 * LANES]
    dv[...] = wide[:, 2 * LANES :]
    ny, block = keep.shape[:2]
    for y in range(ny):
        for out, which in ((keep, core[0]), (send, 1 - core[0])):
            at = pl.multiple_of((2 * y + which) * block, 16)
            out[y] = mm(normed_t[pl.ds(at, block), :], wide[...]).astype(BF)


def attend_back(core, mixed, attended_grad, lse, start_row, normed_t, first, count, ny):
    rows, width = attended_grad.shape
    block = width // (2 * ny)

    def column(offset):
        return pl.BlockSpec((rows, LANES), lambda p, s: (0, offset + first + p))

    out_column = pl.BlockSpec((rows, LANES), lambda p, s: (0, p))
    grads = pl.BlockSpec((ny, block, 3 * LANES), lambda p, s: (0, 0, p))
    return call(
        attend_back_body,
        "attend_back",
        (count,),
        [
            full((1, rows)),
            column(0),
            column(PAIRS),
            column(2 * PAIRS),
            column(0),
            pl.BlockSpec((1, 8, rows), lambda p, s: (first + p, 0, 0)),
            full((width, rows)),
        ],
        [out_column] * 3 + [grads] * 2,
        [sds((rows, LANES * count), BF)] * 3 + [sds((ny, block, 3 * LANES * count), BF)] * 2,
        [
            pltpu.VMEM((rows, rows), F32),
            pltpu.VMEM((LANES, rows), BF),
            pltpu.VMEM((LANES, rows), F32),
            pltpu.VMEM((rows, LANES), F32),
            pltpu.VMEM((rows, LANES), F32),
            pltpu.VMEM((rows, 3 * LANES), BF),
        ],
        flops=40 * count * rows * rows * HEAD_DIM,
        bytes_=2 * rows * LANES * count * 10,
        prefetch=1,
    )(core, start_row, mixed, mixed, mixed, attended_grad, lse, normed_t)


def second_body(att, w, tokens, gains, router, routes, stream, low, gates, sums, *, gain_at):
    attn = mm(att[...], w[...])
    total = tokens[...].astype(F32) + attn
    stream[...] = total
    hat, _ = normalise(total)
    normed = (hat * gains[gain_at : gain_at + 1, :] + gains[gain_at + 1 : gain_at + 2, :]).astype(BF)
    low[...] = normed
    logits = mm(normed, router[...])
    hot = routes[...] == lax.broadcasted_iota(jnp.int32, logits.shape, 1)
    gate = jax.nn.sigmoid(jnp.sum(jnp.where(hot, logits, 0.0), axis=1, keepdims=True))
    gates[...] = gate

    @pl.when(pl.program_id(0) == 0)
    def _():
        sums[...] = jnp.zeros_like(sums)

    row = lax.broadcasted_iota(jnp.int32, sums.shape, 0)
    by_expert = jnp.sum(jnp.where(hot, gate, 0.0), axis=0, keepdims=True)
    squares = jnp.sum(attn * attn)
    sums[...] += jnp.where(row == 0, by_expert, jnp.where(row == 1, squares, 0.0))


def second_stage(att, output, small, tokens, gains, routes, gain_at):
    rows, width = tokens.shape
    block = pl.BlockSpec((BLOCK, width), lambda i: (i, 0))
    thin = pl.BlockSpec((BLOCK, 1), lambda i: (i, 0))
    return call(
        functools.partial(second_body, gain_at=gain_at),
        "second",
        (rows // BLOCK,),
        [
            block,
            full((width, width)),
            block,
            full((LANES, width)),
            full((width, LANES)),
            thin,
        ],
        [block, block, thin, full((8, LANES))],
        [sds((rows, width), F32), sds((rows, width), BF), sds((rows, 1), F32), sds((8, LANES), F32)],
        flops=2 * rows * width * width,
        bytes_=rows * width * 10 + width * width * 2,
    )(att, output, tokens, gains, small, routes)


def flip_body(a, b, a_t, b_t):
    a_t[...] = a[...].T
    b_t[...] = b[...].T


def flip(inner, outer):
    width, wide = inner.shape
    tile = 512
    across = pl.BlockSpec((tile, width), lambda f: (f, 0))
    down = pl.BlockSpec((width, tile), lambda f: (0, f))
    return call(
        flip_body, "flip", (wide // tile,), [down, across], [across, down],
        [sds((wide, width), BF), sds((width, wide), BF)], bytes_=8 * width * wide,
    )(inner, outer)


def expert_body(
    bal, x, c, w1t, w2, w2t, w1, b1, b2, rw, act_t, pre_t, g_out, x_t, out, in_grad, b1_grad, rows_out,
    g, gate, out_acc, in_acc,
):
    step = pl.program_id(0)

    @pl.when(step == 0)
    def _():
        logits = jnp.sum(x[...].astype(F32) * rw[...], axis=1, keepdims=True)
        gate[...] = jax.nn.sigmoid(logits)
        g[...] = (gate[...] * c[...].astype(F32)).astype(BF)
        out_acc[...] = jnp.zeros_like(out_acc)
        in_acc[...] = jnp.zeros_like(in_acc)

    bias = jnp.broadcast_to(b1[...].astype(F32), (LANES, b1.shape[1])).T[:, :1]
    pre = mm(w1t[...], x[...], NT) + bias
    cdf = 0.5 * (1.0 + lax.erf(pre * (0.5**0.5)))
    act = (pre * cdf).astype(BF)
    slope = cdf + pre * jnp.exp(-0.5 * pre * pre) * ((2.0 * np.pi) ** -0.5)
    act_t[...] = act
    out_acc[...] += mm(w2t[...], act)
    back = (mm(w2[...], g[...], NT) * slope).astype(BF)
    pre_t[...] = back
    in_acc[...] += mm(w1[...], back)
    b1_grad[...] = mm(jnp.ones((8, back.shape[1]), BF), back, NT)

    @pl.when(step == pl.num_programs(0) - 1)
    def _():
        result = (out_acc[...].T + b2[...].astype(F32)).astype(BF)
        out[...] = result
        gate_grad = jnp.sum(c[...].astype(F32) * result.astype(F32), axis=1, keepdims=True) + bal[0, 0]
        logit_grad = gate_grad * gate[...] * (1.0 - gate[...])
        in_grad[...] = (in_acc[...].T + logit_grad * rw[...]).astype(BF)
        g_out[...] = g[...]
        x_t[...] = x[...].T
        row = lax.broadcasted_iota(jnp.int32, rows_out.shape, 0)
        router_part = jnp.sum(x[...].astype(F32) * logit_grad, axis=0, keepdims=True)
        bias_part = jnp.sum(g[...].astype(F32), axis=0, keepdims=True)
        rows_out[...] = jnp.where(row == 0, router_part, jnp.where(row == 1, bias_part, 0.0))


def expert_stage(bal, x, c, w1t, w2, w2t, w1, b1, b2, rw):
    rows, width = x.shape
    wide = w1.shape[1]
    tile = BLOCK
    across = pl.BlockSpec((tile, width), lambda f: (f, 0))
    down = pl.BlockSpec((width, tile), lambda f: (0, f))
    whole = full((rows, width))
    return call(
        expert_body,
        "expert",
        (wide // tile,),
        [
            pl.BlockSpec(memory_space=pltpu.SMEM),
            whole,
            whole,
            across,
            across,
            down,
            down,
            pl.BlockSpec((1, tile), lambda f: (0, f)),
            full((1, width)),
            full((1, width)),
        ],
        [
            pl.BlockSpec((tile, rows), lambda f: (f, 0)),
            pl.BlockSpec((tile, rows), lambda f: (f, 0)),
            whole,
            full((width, rows)),
            whole,
            whole,
            pl.BlockSpec((8, tile), lambda f: (0, f)),
            full((8, width)),
        ],
        [
            sds((wide, rows), BF),
            sds((wide, rows), BF),
            sds((rows, width), BF),
            sds((width, rows), BF),
            sds((rows, width), BF),
            sds((rows, width), BF),
            sds((8, wide), F32),
            sds((8, width), F32),
        ],
        [
            pltpu.VMEM((rows, width), BF),
            pltpu.VMEM((rows, 1), F32),
            pltpu.VMEM((width, rows), F32),
            pltpu.VMEM((width, rows), F32),
        ],
        flops=8 * rows * width * wide,
        bytes_=2 * (4 * width * wide + 2 * wide * rows + 6 * rows * width),
    )(bal, x, c, w1t, w2, w2t, w1, b1, b2, rw)


def weight_grad_body(
    core, a0, a1, g0, g1, p0, p1, x0, x1, outer_send, inner_send, outer_keep, inner_keep
):
    outer = (mm(a0[...], g0[...]) + mm(a1[...], g1[...])).astype(BF)
    inner = (mm(x0[...], p0[...], NT) + mm(x1[...], p1[...], NT)).astype(BF)

    @pl.when(pl.program_id(0) == 0)
    def _():
        outer_send[...] = outer
        inner_send[...] = inner

    @pl.when(pl.program_id(0) == 1)
    def _():
        outer_keep[...] = outer
        inner_keep[...] = inner


def weight_grads(core, acts, outs, pres, ins):
    tile = 512
    wide, rows = acts[0].shape
    width = outs[0].shape[1]
    steps = wide // 2 // tile

    def half(w, s):
        return jnp.where(w == 0, 1 - s[0], s[0])

    hidden = pl.BlockSpec((tile, rows), lambda w, f, s: (half(w, s) * steps + f, 0))

    def sent(w, f):
        return jnp.where(w == 0, f, steps - 1)

    def kept(w, f):
        return jnp.where(w == 0, 0, f)

    return call(
        weight_grad_body,
        "weight_grads",
        (2, steps),
        [hidden, hidden, full(outs[0].shape), full(outs[0].shape), hidden, hidden, full(ins[0].shape), full(ins[0].shape)],
        [
            pl.BlockSpec((tile, width), lambda w, f, s: (sent(w, f), 0)),
            pl.BlockSpec((width, tile), lambda w, f, s: (0, sent(w, f))),
            pl.BlockSpec((tile, width), lambda w, f, s: (kept(w, f), 0)),
            pl.BlockSpec((width, tile), lambda w, f, s: (0, kept(w, f))),
        ],
        [sds((wide // 2, width), BF), sds((width, wide // 2), BF)] * 2,
        flops=8 * rows * width * wide,
        bytes_=8 * (wide * rows + rows * width + width * wide),
        prefetch=1,
    )(core, *acts, *outs, *pres, *ins)


def place_body(which, a, b, *rest):
    rest[-1][0] = a[...].astype(F32) + b[...].astype(F32)


def place(which, outer, a, b, held=None, piece=0, pieces=1):
    steps = 4 // pieces
    offset = piece * steps
    if outer:
        block = (a.shape[0] // (steps * pieces), a.shape[1])
        whole = (1, 2 * a.shape[0], a.shape[1])
        a_spec = pl.BlockSpec(block, lambda i, s: (offset + i, 0))
        b_spec = pl.BlockSpec(block, lambda i, s: (i, 0))
        large = pl.BlockSpec((1,) + block, lambda i, s: (0, s[0] * steps * pieces + offset + i, 0))
    else:
        block = (a.shape[0], a.shape[1] // (steps * pieces))
        whole = (1, a.shape[0], 2 * a.shape[1])
        a_spec = pl.BlockSpec(block, lambda i, s: (0, offset + i))
        b_spec = pl.BlockSpec(block, lambda i, s: (0, i))
        large = pl.BlockSpec((1,) + block, lambda i, s: (0, 0, s[0] * steps * pieces + offset + i))
    extra = [] if held is None else [held]
    return call(
        place_body, "place", (steps,), [a_spec, b_spec] + [pl.BlockSpec(memory_space=pl.ANY)] * len(extra), large,
        sds(whole, F32), bytes_=b.size * 8, flops=b.size, prefetch=1, aliases={3: 0} if extra else None,
    )(which, a, b, *extra)


def layer_back(hat, scale, gain, grad):
    scaled = grad * gain
    return scale * (
        scaled - jnp.mean(scaled, axis=-1, keepdims=True) - hat * jnp.mean(scaled * hat, axis=-1, keepdims=True)
    )


def return_body(
    core, slots, tgt, r0, r1, stream, cot, gains, att_t, w, stream_grad, back, sums, keep, send, w_acc, *, gain_at
):
    step = pl.program_id(0)

    @pl.when(step == 0)
    def _():
        sums[...] = jnp.zeros_like(sums)
        w_acc[...] = jnp.zeros_like(w_acc)

    grad = mm(jnp.where(tgt[...] == slots[0:1, :], 1.0, 0.0).astype(BF), r0[...])
    grad += mm(jnp.where(tgt[...] == slots[1:2, :], 1.0, 0.0).astype(BF), r1[...])
    hat, scale = normalise(stream[...])
    total = cot[...].astype(F32) + layer_back(hat, scale, gains[gain_at : gain_at + 1, :], grad)
    stream_grad[...] = total
    low = total.astype(BF)
    back[...] = mm(low, w[...], NT).astype(BF)
    w_acc[...] += mm(att_t[...], low)
    row = lax.broadcasted_iota(jnp.int32, sums.shape, 0)
    sums[...] += jnp.where(
        row == 0,
        jnp.sum(grad * hat, axis=0, keepdims=True),
        jnp.where(row == 1, jnp.sum(grad, axis=0, keepdims=True), 0.0),
    )

    @pl.when(step == pl.num_programs(0) - 1)
    def _():
        ny, block = keep.shape[:2]
        for y in range(ny):
            for out, which in ((keep, core[0]), (send, 1 - core[0])):
                at = pl.multiple_of((2 * y + which) * block, 16)
                out[y] = w_acc[pl.ds(at, block), :].astype(BF)


def return_stage(core, slots_row, tgt_col, r0, r1, stream, cot, gains, att_t, output, gain_at, ny):
    rows, width = stream.shape
    block = pl.BlockSpec((BLOCK, width), lambda i, s: (i, 0))
    grads = (ny, width // (2 * ny), width)
    return call(
        functools.partial(return_body, gain_at=gain_at),
        "return",
        (rows // BLOCK,),
        [
            full(slots_row.shape),
            pl.BlockSpec((BLOCK, 1), lambda i, s: (i, 0)),
            full(r0.shape),
            full(r1.shape),
            block,
            block,
            full((LANES, width)),
            pl.BlockSpec((width, BLOCK), lambda i, s: (0, i)),
            full((width, width)),
        ],
        [block, block, full((8, width)), full(grads), full(grads)],
        [sds((rows, width), F32), sds((rows, width), BF), sds((8, width), F32), sds(grads, BF), sds(grads, BF)],
        [pltpu.VMEM((width, width), F32)],
        flops=2 * rows * width * (2 * r0.shape[0] + 2 * width),
        bytes_=rows * width * 16 + 4 * width * width,
        prefetch=1,
    )(core, slots_row, tgt_col, r0, r1, stream, cot, gains, att_t, output)


def last_body(*refs, gain_at, splits):
    core, parts, (own, other, tokens, stream_grad, gains, out, sums, mixer) = refs[0], refs[1:-8], refs[-8:]

    @pl.when(pl.program_id(0) == 0)
    def _():
        merge_rows(mixer, own, other, core[0], 0, mixer.shape[1])
        sums[...] = jnp.zeros_like(sums)

    width = tokens.shape[1]
    grad = jnp.zeros(tokens.shape, F32)
    for n, (first, count) in enumerate(splits):
        for j in range(3):
            at = j * width + first * LANES
            grad += mm(parts[3 * n + j][...], mixer[:, at : at + count * LANES], NT)
    hat, scale = normalise(tokens[...].astype(F32))
    out[...] = stream_grad[...] + layer_back(hat, scale, gains[gain_at : gain_at + 1, :], grad)
    row = lax.broadcasted_iota(jnp.int32, sums.shape, 0)
    sums[...] += jnp.where(
        row == 0,
        jnp.sum(grad * hat, axis=0, keepdims=True),
        jnp.where(row == 1, jnp.sum(grad, axis=0, keepdims=True), 0.0),
    )


def last_stage(core, parts, splits, own, other, tokens, stream_grad, gains, gain_at):
    rows, width = tokens.shape
    block = pl.BlockSpec((BLOCK, width), lambda i, s: (i, 0))
    weight = pl.BlockSpec(own.shape[:2] + (3 * width,), lambda i, s: (0, 0, 0))
    return call(
        functools.partial(last_body, gain_at=gain_at, splits=splits),
        "last",
        (rows // BLOCK,),
        [pl.BlockSpec((BLOCK, p.shape[1]), lambda i, s: (i, 0)) for p in parts]
        + [weight, weight, block, block, full((LANES, width))],
        [block, full((8, width))],
        [sds((rows, width), F32), sds((8, width), F32)],
        [pltpu.VMEM((width, 3 * width), BF)],
        flops=6 * rows * width * width,
        bytes_=rows * width * 16 + 6 * width * width,
        prefetch=1,
    )(core, *parts, own, other, tokens, stream_grad, gains)


def result_body(slots, tgt, r0, r1, stream, gates, out, sums):
    @pl.when(pl.program_id(0) == 0)
    def _():
        sums[...] = jnp.zeros_like(sums)

    picked = mm(jnp.where(tgt[...] == slots[0:1, :], 1.0, 0.0).astype(BF), r0[...])
    picked += mm(jnp.where(tgt[...] == slots[1:2, :], 1.0, 0.0).astype(BF), r1[...])
    moe = gates[...] * picked
    total = stream[...] + moe
    out[...] = total.astype(BF)
    row = lax.broadcasted_iota(jnp.int32, sums.shape, 0)
    sums[...] += jnp.where(row == 0, jnp.sum(total * total), jnp.where(row == 1, jnp.sum(moe * moe), 0.0))


def result_stage(slots_row, tgt_col, r0, r1, stream, gates):
    rows, width = stream.shape
    block = pl.BlockSpec((BLOCK, width), lambda i: (i, 0))
    thin = pl.BlockSpec((BLOCK, 1), lambda i: (i, 0))
    return call(
        result_body,
        "result",
        (rows // BLOCK,),
        [full(slots_row.shape), thin, full(r0.shape), full(r1.shape), block, thin],
        [block, full((8, LANES))],
        [sds((rows, width), BF), sds((8, LANES), F32)],
        flops=4 * rows * width * r0.shape[0],
        bytes_=rows * width * 10,
    )(slots_row, tgt_col, r0, r1, stream, gates)


def collect_body(expert_here, r0, r1, b0, b1, second, first, forward, result, out, *, experts):
    row = lax.broadcasted_iota(jnp.int32, (experts, out.shape[1]), 0)
    router = r0[0:1, :] + r1[0:1, :]
    width = out.shape[1]
    out[...] = jnp.zeros_like(out)
    out[:experts, :] = jnp.where(row == expert_here[0], router, 0.0)
    out[experts : experts + 2, :] = second[0:2, :]
    out[experts + 2 : experts + 4, :] = first[0:2, :]
    at = experts + 4
    for k, (ref, line) in enumerate(((forward, 0), (forward, 1), (result, 0), (result, 1))):
        out[at : at + 1, k * LANES : (k + 1) * LANES] = ref[line : line + 1, :]
    out[at + 1 : at + 2, :] = r0[1:2, :] + r1[1:2, :]
    for k in range(b0.shape[1] // width):
        cut = slice(k * width, (k + 1) * width)
        out[at + 2 + k : at + 3 + k, :] = b0[0:1, cut] + b1[0:1, cut]


def collect(expert_here, experts, arrays):
    width = arrays[0].shape[1]
    shape = (experts + 6 + arrays[2].shape[1] // width, width)
    return call(
        functools.partial(collect_body, experts=experts),
        "collect",
        (1,),
        [pl.BlockSpec(memory_space=pltpu.SMEM)] + [full(a.shape) for a in arrays],
        full(shape),
        sds(shape, F32),
        bytes_=4 * shape[0] * width,
    )(expert_here, *arrays)


def shards(
    tokens, cotangent, lengths, routes, mixer_weight, output_weight, first_gain, first_shift, second_gain,
    second_shift, router_weight, inner_weight, inner_bias, outer_weight, outer_bias,
):
    rows, width = tokens.shape
    shard_rows = mixer_weight.shape[0]
    experts = router_weight.shape[1]
    wide = inner_weight.shape[2]
    devices = lax.axis_size(ANYWHERE)
    capacity = 3 * rows // (2 * experts)
    half_cap = capacity // 2
    half = experts * half_cap
    total_tokens = rows * devices
    average = total_tokens / experts
    gain_one_at, gain_two_at, counts_at = experts, experts + 2, experts + 4

    slot_ids = np.arange(experts * capacity, dtype=np.int32).reshape(experts, 2, half_cap).swapaxes(0, 1).reshape(2, half)
    slots_row = jnp.asarray(slot_ids)
    slots_col = [jnp.asarray(slot_ids[c].reshape(half, 1)) for c in range(2)]

    tgt_row, start_row, packed = prepare(
        lengths, routes, mixer_weight, output_weight, router_weight,
        (first_gain, first_shift, second_gain, second_shift), capacity,
    )
    tgt_col = tgt_row.reshape(rows, 1)
    expert_here = lax.axis_index("expert")
    core = my_bit("batch", 0).reshape(1).astype(jnp.int32)
    nb_bits = bits_of(lax.axis_size("batch"))
    ny = lax.axis_size("batch") // 2

    def exchange(value):
        shaped = value.reshape(experts, half_cap, width)
        return lax.all_to_all(shaped, "expert", split_axis=0, concat_axis=0, tiled=True).reshape(half, width)

    w1, w2 = inner_weight[0], outer_weight[0]
    ready = {}

    def beside(name, make):
        def run(other):
            other, *ready[name] = lax.optimization_barrier((other, *make()))
            return other

        return run

    own_rows, other_rows = gather_rows(
        packed,
        [
            beside("cot0", lambda: [dispatch(slots_col[0], tgt_row, cotangent)]),
            beside("cot1", lambda: [dispatch(slots_col[1], tgt_row, cotangent)]),
            beside("weights", lambda: flip(w1, w2)),
            beside("sent0", lambda: [exchange(ready["cot0"][0])]),
        ],
    )
    w1t, w2t = ready["weights"]
    (cot0,) = ready["sent0"]
    cot1 = exchange(ready["cot1"][0])

    mixed, normed_t, output_full, small, small_t = first_stage(core, tokens, own_rows, other_rows, gain_one_at)
    counts = jnp.sum(small_t[counts_at : counts_at + experts], axis=1)
    balance_terms = (counts - average) / (average * total_tokens)
    bal = lax.dynamic_slice_in_dim(balance_terms, expert_here, 1).reshape(1, 1)
    rw = lax.dynamic_slice_in_dim(small_t, expert_here, 1, axis=0)
    att, att_t, lse = attend(mixed, start_row)
    att, bal, rw, tgt_col = lax.optimization_barrier((att, bal, rw, tgt_col))
    stream, second_low, gates, second_sums = second_stage(att, output_full, small, tokens, small_t, routes, gain_two_at)
    placed = [dispatch(slots_col[c], tgt_row, second_low) for c in range(2)]

    placed0, cot1 = lax.optimization_barrier((placed[0], cot1))
    x0 = exchange(placed0)
    second_half, x0 = lax.optimization_barrier((placed[1], x0))
    x1 = exchange(second_half)
    e0 = expert_stage(bal, x0, cot0, w1t, w2, w2t, w1, inner_bias, outer_bias, rw)
    in0 = exchange(e0[5])
    e1 = expert_stage(bal, x1, cot1, w1t, w2, w2t, w1, inner_bias, outer_bias, rw)
    in1 = exchange(e1[5])

    wgrads = weight_grads(core, (e0[0], e1[0]), (e0[2], e1[2]), (e0[1], e1[1]), (e0[3], e1[3]))
    in0, in1, wgrads, out0_in = lax.optimization_barrier((in0, in1, tuple(wgrads), e0[4]))
    outer_away, inner_away, outer_kept, inner_kept = wgrads

    def together(kept, away):
        mine = over_cores(kept, away)
        for bit in range(2, nb_bits):
            mine = add_low(mine, swap(mine, "batch", bit))
        return mine

    out0 = exchange(out0_in)

    stream_grad, attended_grad, second_grads, out_keep, out_send = return_stage(
        core, slots_row, tgt_col, in0, in1, stream, cotangent, small_t, att_t, output_full, gain_two_at, ny
    )

    outer_mine, inner_mine = together(outer_kept, outer_away), together(inner_kept, inner_away)
    attended_grad, outer_mine, inner_mine = lax.optimization_barrier((attended_grad, outer_mine, inner_mine))
    inner_far = swap(inner_mine, "batch", 1)

    def backward(first, grad):
        *parts, keep, send = attend_back(core, mixed, grad, lse, start_row, normed_t, first, 2, ny)
        return parts, keep, send

    parts_a, *sums_a = backward(0, attended_grad)
    sum_o = over_cores(out_keep, out_send)
    outer_beside, inner_beside = swap(outer_mine, "batch", 0), swap(inner_mine, "batch", 0)
    attended_grad, sum_o, out0, out1_in, *sums_a = lax.optimization_barrier(
        (attended_grad, sum_o, out0, e1[4], *sums_a)
    )
    out1 = exchange(out1_in)
    parts_b, *sums_b = backward(2, attended_grad)
    sum_o, sum_a = over_x(sum_o), over_cores(*sums_a)
    attended_grad, sum_o, sum_a, outer_beside, inner_beside, *sums_b = lax.optimization_barrier(
        (attended_grad, sum_o, sum_a, outer_beside, inner_beside, *sums_b)
    )
    parts_c, *sums_c = backward(4, attended_grad)
    sum_a, sum_b = over_x(sum_a), over_cores(*sums_b)
    stream_grad, gates, sum_a, sum_b, inner_far, outer_mine, *sums_c = lax.optimization_barrier(
        (stream_grad, gates, sum_a, sum_b, inner_far, outer_mine, *sums_c)
    )
    outer_far = swap(outer_mine[: wide // 4], "batch", 1)
    block_output, result_sums = result_stage(slots_row, tgt_col, out0, out1, stream, gates)
    splits = ((0, 2), (2, 2), (4, 2))
    input_grad, first_grads = last_stage(
        core, parts_a + parts_b + parts_c, splits, own_rows, other_rows, tokens, stream_grad, small_t, gain_one_at
    )
    sum_b, sum_c = over_x(sum_b), over_x(over_cores(*sums_c))
    total = jnp.concatenate([sum_o, sum_a, sum_b, sum_c], axis=-1)
    first_grads, result_sums, outer_far, outer_mine = lax.optimization_barrier(
        (first_grads, result_sums, outer_far, outer_mine)
    )
    outer_last = swap(outer_mine[wide // 4 :], "batch", 1)
    other = 1 - core
    inner_held = place(core, False, inner_mine, inner_far)

    sums = collect(
        expert_here.reshape(1).astype(jnp.int32), experts,
        (e0[7], e1[7], e0[6], e1[6], second_grads, first_grads, second_sums, result_sums),
    )
    common = sums[: experts + 5]
    for bit in reversed(range(bits_of(experts))):
        common = common + swap(common, "expert", bit)
        if bit == bits_of(experts) - 2:
            common, total = lax.optimization_barrier((common, total))
    inner_w_sum = place(other, False, inner_beside, swap(inner_far, "batch", 0), inner_held)
    total = over_rest(total)
    sums = jnp.concatenate([common, sums[experts + 5 :]], axis=0)
    sums = sums + swap(sums, "batch", 0)
    outer_w_sum = place(core, True, outer_mine, outer_far, None, 0, 2)
    outer_w_sum = place(other, True, outer_beside, swap(outer_far, "batch", 0), outer_w_sum, 0, 2)
    sums, outer_last, inner_w_sum, outer_w_sum = lax.optimization_barrier((sums, outer_last, inner_w_sum, outer_w_sum))
    for bit in range(1, nb_bits):
        sums = sums + swap(sums, "batch", bit)
    outer_w_sum = place(core, True, outer_mine, outer_last, outer_w_sum, 1, 2)
    outer_w_sum = place(other, True, outer_beside, swap(outer_last, "batch", 0), outer_w_sum, 1, 2)
    outer_b_sum = sums[experts + 5 : experts + 6]
    inner_b_sum = sums[experts + 6 :].reshape(1, wide)
    output_grad = total[:, :width]
    mixer_grad = jnp.swapaxes(total[:, width:].reshape(shard_rows, PAIRS, 3, LANES), 1, 2)
    mixer_grad = mixer_grad.reshape(shard_rows, 3 * width)

    device = lax.axis_index("batch") * experts + expert_here
    mine = lax.dynamic_slice_in_dim(sums[: experts + 4], device * shard_rows, shard_rows, axis=1)
    numbers = sums[experts + 4]
    balance = jnp.sum((counts - average) / average * numbers[:experts]) / total_tokens
    squares = jnp.stack([numbers[2 * LANES], numbers[LANES], numbers[3 * LANES]])
    root_means = jnp.sqrt(squares / (total_tokens * width) + 1e-06)

    return (
        block_output,
        input_grad,
        mixer_grad,
        output_grad,
        mine[experts + 2],
        mine[experts + 3],
        mine[experts],
        mine[experts + 1],
        mine[:experts].T,
        inner_w_sum,
        inner_b_sum,
        outer_w_sum,
        outer_b_sum,
        balance,
        root_means,
    )


def solution(mesh):
    everywhere = P(ANYWHERE, None)
    line = P(ANYWHERE)
    in_specs = (
        everywhere, everywhere, everywhere, everywhere, everywhere, everywhere, line, line, line, line, everywhere,
        P("expert", None, None), P("expert", None), P("expert", None, None), P("expert", None),
    )
    out_specs = (
        everywhere, everywhere, everywhere, everywhere, line, line, line, line, everywhere,
        P("expert", None, None), P("expert", None), P("expert", None, None), P("expert", None), P(), P(),
    )
    return jax.shard_map(shards, mesh=mesh, in_specs=in_specs, out_specs=out_specs, check_vma=False)
```

```python
import functools

import jax
import jax.numpy as jnp
import numpy as np
from jax import lax
from jax.experimental import pallas as pl
from jax.experimental.pallas import tpu as pltpu
from jax.sharding import PartitionSpec as P

HEADS = 12
HEAD_DIM = 64
PAIRS = HEADS // 2
WINDOW = 512
BLOCK = 256
EPSILON = 1e-05
LANES = 128
BF = jnp.bfloat16
F32 = jnp.float32
ANYWHERE = ("batch", "expert")

NT = (((1,), (1,)), ((), ()))
NN = (((1,), (0,)), ((), ()))


def mm(a, b, dims=NN):
    return lax.dot_general(a, b, dims, preferred_element_type=F32)


def call(body, name, grid, in_specs, out_specs, out_shape, scratch=(), flops=0, bytes_=0, prefetch=0, aliases=None):
    return pl.pallas_call(
        body,
        name=name,
        grid_spec=pltpu.PrefetchScalarGridSpec(
            num_scalar_prefetch=prefetch,
            grid=grid,
            in_specs=in_specs,
            out_specs=out_specs,
            scratch_shapes=list(scratch),
        ),
        out_shape=out_shape,
        input_output_aliases=aliases or {},
        cost_estimate=pl.CostEstimate(flops=int(flops), bytes_accessed=int(bytes_), transcendentals=0),
    )


def sds(shape, dtype):
    return jax.ShapeDtypeStruct(shape, dtype)


def full(shape):
    return pl.BlockSpec(shape, lambda *_: (0,) * len(shape))


def bits_of(size):
    return size.bit_length() - 1


def swap(value, axis, bit):
    size = lax.axis_size(axis)
    return lax.ppermute(value, axis, [(i, i ^ (1 << bit)) for i in range(size)])


def my_bit(axis, bit):
    return (lax.axis_index(axis) >> bit) & 1


def gather_rows(shard, beside):
    nb, ne = lax.axis_size("batch"), lax.axis_size("expert")
    value = shard
    placed = []
    order = [("expert", b) for b in reversed(range(bits_of(ne)))] + [("batch", b) for b in reversed(range(1, bits_of(nb)))]
    for step, (axis, bit) in enumerate(order):
        weight = bit + (bits_of(ne) if axis == "batch" else 0)
        spot = sum(1 for w in placed if w > weight)
        placed.append(weight)
        other = swap(value, axis, bit)
        late = step + len(beside) - len(order)
        if late >= 0:
            other = beside[late](other)
        value, other = jnp.expand_dims(value, spot), jnp.expand_dims(other, spot)
        place = lax.broadcasted_iota(jnp.int32, value.shape[:spot] + (2,) + value.shape[spot + 1 :], spot)
        value = jnp.where(place == my_bit(axis, bit), value, other)
    value = value.reshape(nb // 2, ne * shard.shape[0], shard.shape[1])
    return value, swap(value, "batch", 0)


def merge_rows(out, own, other, core, first, last):
    ny, rows = own.shape[:2]
    for y in range(ny):
        for part, which in ((own, core), (other, 1 - core)):
            out[pl.ds(pl.multiple_of((2 * y + which) * rows, 16), rows), :] = part[y, :, first:last]


def add_low(a, b):
    return (a.astype(F32) + b.astype(F32)).astype(BF)


def over_cores(keep, send):
    return add_low(keep, swap(send, "batch", 0))


def over_x(total):
    ny, rows, width = total.shape
    ne = lax.axis_size("expert")
    total = total.reshape(ny, ne // 2, 2, rows // ne, width).transpose(2, 1, 0, 3, 4)
    low = my_bit("expert", 0)
    got = swap(lax.dynamic_index_in_dim(total, 1 - low, 0, keepdims=False), "expert", 0)
    return add_low(lax.dynamic_index_in_dim(total, low, 0, keepdims=False), got)


def over_rest(total):
    ne = lax.axis_size("expert")
    groups = [list(range(b, ne, 2)) for b in range(2)]
    pieces = lax.all_to_all(total, "expert", split_axis=0, concat_axis=0, axis_index_groups=groups, tiled=True)
    value = jnp.sum(pieces.astype(F32), axis=0)
    for bit in reversed(range(1, bits_of(lax.axis_size("batch")))):
        here = my_bit("batch", bit)
        value = value.reshape((2, value.shape[0] // 2) + value.shape[1:])
        out = lax.dynamic_index_in_dim(value, 1 - here, 0, keepdims=False)
        value = lax.dynamic_index_in_dim(value, here, 0, keepdims=False) + swap(out, "batch", bit)
    return value[0]


def prep_body(lengths_ref, routes_row, mixer, output, router, *rest, capacity, experts):
    vectors, (tgt_row, start_row, packed) = rest[:4], rest[4:]
    rows = routes_row.shape[1]
    at = lax.broadcasted_iota(jnp.int32, (1, rows), 1)
    start = jnp.zeros((1, rows), jnp.int32)
    off = jnp.int32(0)
    for s in range(lengths_ref.shape[1]):
        start = jnp.where(at >= off, off, start)
        off = off + lengths_ref[0, s]
    start_row[...] = start
    hot = routes_row[...] == lax.broadcasted_iota(jnp.int32, (LANES, rows), 0)
    hot_low = jnp.where(hot, 1.0, 0.0).astype(BF)
    before = lax.broadcasted_iota(jnp.int32, (rows, rows), 0) < lax.broadcasted_iota(jnp.int32, (rows, rows), 1)
    ranks = mm(hot_low, jnp.where(before, 1.0, 0.0).astype(BF))
    rank = jnp.sum(jnp.where(hot, ranks, 0.0), axis=0, keepdims=True)
    tgt_row[...] = routes_row[...] * capacity + rank.astype(jnp.int32)

    own, first = mixer.shape
    wide = first + output.shape[1]
    packed[:, :first] = mixer[...]
    packed[:, first:wide] = output[...]
    row = lax.broadcasted_iota(jnp.int32, (own, LANES), 0)
    lane = lax.broadcasted_iota(jnp.int32, (own, LANES), 1)
    lane_of = lax.broadcasted_iota(jnp.int32, (LANES, LANES), 1)
    row_of = lax.broadcasted_iota(jnp.int32, (LANES, LANES), 0)
    counts = jnp.sum(jnp.where(hot, 1.0, 0.0), axis=1, keepdims=True)
    counts = jnp.sum(jnp.where(lane_of == row_of + experts + 4, counts, 0.0), axis=0, keepdims=True)
    small = jnp.where((row == 0) & (lane < 2 * experts + 4), counts, 0.0)
    across = lax.broadcasted_iota(jnp.int32, (own, own), 0) == lax.broadcasted_iota(jnp.int32, (own, own), 1)
    lines = router[...].astype(F32)
    lines = [lines[k : k + 1, :] for k in range(experts)] + [v[...].astype(F32) for v in vectors]
    for k, line in enumerate(lines):
        column = jnp.sum(jnp.where(across, line, 0.0), axis=1, keepdims=True)
        small = jnp.where(lane == k, column, small)
    packed[:, wide:] = small.astype(BF)


def prepare(lengths, routes, mixer, output, router, vectors, capacity):
    rows = routes.shape[0]
    experts, own = router.shape
    wide = mixer.shape[1] + output.shape[1] + LANES
    return call(
        functools.partial(prep_body, capacity=capacity, experts=experts),
        "prep",
        (1,),
        [pl.BlockSpec(memory_space=pltpu.SMEM), full((1, rows)), full(mixer.shape), full(output.shape), full(router.shape)]
        + [full((1, own))] * 4,
        [full((1, rows)), full((1, rows)), full((own, wide))],
        [sds((1, rows), jnp.int32), sds((1, rows), jnp.int32), sds((own, wide), BF)],
        flops=2 * rows * rows * LANES,
        bytes_=rows * 1024,
    )(lengths, routes.reshape(1, rows), mixer, output, router, *[v.reshape(1, own) for v in vectors])


def columns_body(a, b, a_col, b_col):
    for row, col in ((a, a_col), (b, b_col)):
        wide = jnp.broadcast_to(row[...].astype(F32), (LANES, row.shape[1]))
        col[...] = wide.T[:, :1].astype(jnp.int32)


def columns(a, b):
    rows = a.shape[1]
    return call(
        columns_body, "columns", (1,), [full(a.shape)] * 2, [full((rows, 1))] * 2, [sds((rows, 1), jnp.int32)] * 2, bytes_=rows * 1024
    )(a, b)


def dispatch_body(slots, tgt, x, out):
    hot = jnp.where(slots[...] == tgt[...], 1.0, 0.0).astype(BF)
    out[...] = mm(hot, x[...]).astype(BF)


def dispatch(slots_col, tgt_row, x):
    rows, width = x.shape
    half = slots_col.shape[0]
    tile = BLOCK
    return call(
        dispatch_body,
        "dispatch",
        (half // tile,),
        [pl.BlockSpec((tile, 1), lambda t: (t, 0)), full((1, rows)), full((rows, width))],
        pl.BlockSpec((tile, width), lambda t: (t, 0)),
        sds((half, width), BF),
        flops=2 * half * rows * width,
        bytes_=rows * width * 4,
    )(slots_col, tgt_row, x)


def normalise(v):
    centre = v - jnp.mean(v, axis=-1, keepdims=True)
    spread = jnp.mean(centre * centre, axis=-1, keepdims=True)
    scale = lax.rsqrt(spread + EPSILON)
    return centre * scale, scale


def first_body(core, tokens, own, other, mixed, normed_t, output, small, gains, mixer, *, gain_at):
    @pl.when(pl.program_id(0) == 0)
    def _():
        wide, width = mixer.shape[1], output.shape[1]
        merge_rows(mixer, own, other, core[0], 0, wide)
        merge_rows(output, own, other, core[0], wide, wide + width)
        merge_rows(small, own, other, core[0], wide + width, wide + width + LANES)
        gains[...] = small[...].astype(F32).T

    hat, _ = normalise(tokens[...].astype(F32))
    normed = hat * gains[gain_at : gain_at + 1, :] + gains[gain_at + 1 : gain_at + 2, :]
    low = normed.astype(BF)
    normed_t[...] = low.T
    mixed[...] = mm(low, mixer[...]).astype(BF)


def first_stage(core, tokens, own, other, gain_at):
    rows, width = tokens.shape
    wide = 3 * width
    return call(
        functools.partial(first_body, gain_at=gain_at),
        "first",
        (rows // BLOCK,),
        [pl.BlockSpec((BLOCK, width), lambda i, s: (i, 0)), full(own.shape), full(own.shape)],
        [
            pl.BlockSpec((BLOCK, wide), lambda i, s: (i, 0)),
            pl.BlockSpec((width, BLOCK), lambda i, s: (0, i)),
            full((width, width)),
            full((width, LANES)),
            full((LANES, width)),
        ],
        [
            sds((rows, wide), BF),
            sds((width, rows), BF),
            sds((width, width), BF),
            sds((width, LANES), BF),
            sds((LANES, width), F32),
        ],
        [pltpu.VMEM((width, wide), BF)],
        flops=2 * rows * width * wide,
        bytes_=2 * (rows * (2 * width + wide) + width * wide),
        prefetch=1,
    )(core, tokens, own, other)


def fill_bias(bias, start):
    rows = bias.shape[0]
    for q in range(rows // BLOCK):
        k0 = max(0, (q + 1) * BLOCK - WINDOW - BLOCK)
        n = (q + 1) * BLOCK - k0
        key = k0 + lax.broadcasted_iota(jnp.int32, (n, BLOCK), 0)
        query = q * BLOCK + lax.broadcasted_iota(jnp.int32, (n, BLOCK), 1)
        seen = (key <= query) & (key >= start[:, q * BLOCK : (q + 1) * BLOCK])
        bias[k0 : k0 + n, q * BLOCK : (q + 1) * BLOCK] = jnp.where(seen, 0.0, -1e30)


def head_of(value, h):
    lane = lax.broadcasted_iota(jnp.int32, value.shape, 1)
    return jnp.where((lane >= HEAD_DIM * h) & (lane < HEAD_DIM * (h + 1)), value, jnp.zeros_like(value))


def attend_body(start, q, k, v, att, att_t, lse, bias, v_t):
    rows = q.shape[0]

    @pl.when(pl.program_id(0) == 0)
    def _():
        fill_bias(bias, start[...])

    v_t[...] = v[...].T
    for i in range(rows // BLOCK):
        k0 = max(0, (i + 1) * BLOCK - WINDOW - BLOCK)
        k1 = (i + 1) * BLOCK
        here = slice(i * BLOCK, k1)
        scaled = q[here, :] * jnp.asarray(HEAD_DIM**-0.5, BF)
        for h in range(2):
            s = mm(k[k0:k1, :], head_of(scaled, h), NT) + bias[k0:k1, here]
            top = jnp.max(s, axis=0, keepdims=True)
            e = jnp.exp(s - top)
            total = jnp.sum(e, axis=0, keepdims=True)
            o = mm(v_t[HEAD_DIM * h : HEAD_DIM * (h + 1), k0:k1], e.astype(BF)) / total
            att_t[HEAD_DIM * h : HEAD_DIM * (h + 1), here] = o.astype(BF)
            lse[0, h : h + 1, here] = top + jnp.log(total)
    att[...] = att_t[...].T


def attend(mixed, start_row):
    rows = mixed.shape[0]
    width = mixed.shape[1] // 3
    return call(
        attend_body,
        "attend",
        (PAIRS,),
        [
            full((1, rows)),
            pl.BlockSpec((rows, LANES), lambda p: (0, p)),
            pl.BlockSpec((rows, LANES), lambda p: (0, PAIRS + p)),
            pl.BlockSpec((rows, LANES), lambda p: (0, 2 * PAIRS + p)),
        ],
        [
            pl.BlockSpec((rows, LANES), lambda p: (0, p)),
            pl.BlockSpec((LANES, rows), lambda p: (p, 0)),
            pl.BlockSpec((1, 8, rows), lambda p: (p, 0, 0)),
        ],
        [sds((rows, width), BF), sds((width, rows), BF), sds((PAIRS, 8, rows), F32)],
        [pltpu.VMEM((rows, rows), F32), pltpu.VMEM((LANES, rows), BF)],
        flops=8 * HEADS * rows * rows * HEAD_DIM,
        bytes_=2 * rows * width * 5,
    )(start_row, mixed, mixed, mixed)


def attend_back_body(
    core, start, q, k, v, g, lse, normed_t, dq, dk, dv, keep, send, bias, k_t, dq_t, dk_acc, dv_acc, wide
):
    rows = q.shape[0]

    @pl.when(pl.program_id(0) == 0)
    def _():
        fill_bias(bias, start[...])

    k_t[...] = k[...].T
    dk_acc[...] = jnp.zeros_like(dk_acc)
    dv_acc[...] = jnp.zeros_like(dv_acc)
    for i in range(rows // BLOCK):
        k0 = max(0, (i + 1) * BLOCK - WINDOW - BLOCK)
        k1 = (i + 1) * BLOCK
        here = slice(i * BLOCK, k1)
        scaled = q[here, :] * jnp.asarray(HEAD_DIM**-0.5, BF)
        g_here = g[here, :]
        for h in range(2):
            q_h = head_of(scaled, h)
            g_h = head_of(g_here, h)
            s = mm(k[k0:k1, :], q_h, NT) + bias[k0:k1, here]
            p = jnp.exp(s - lse[0, h : h + 1, here])
            dp = mm(v[k0:k1, :], g_h, NT)
            inner = jnp.sum(p * dp, axis=0, keepdims=True)
            ds = (p * (dp - inner)).astype(BF)
            dv_acc[k0:k1, :] += mm(p.astype(BF), g_h)
            dk_acc[k0:k1, :] += mm(ds, q_h)
            dq_t[HEAD_DIM * h : HEAD_DIM * (h + 1), here] = mm(k_t[HEAD_DIM * h : HEAD_DIM * (h + 1), k0:k1], ds)
    wide[:, :LANES] = (dq_t[...].T * HEAD_DIM**-0.5).astype(BF)
    wide[:, LANES : 2 * LANES] = dk_acc[...].astype(BF)
    wide[:, 2 * LANES :] = dv_acc[...].astype(BF)
    dq[...] = wide[:, :LANES]
    dk[...] = wide[:, LANES : 2 * LANES]
    dv[...] = wide[:, 2 * LANES :]
    ny, block = keep.shape[:2]
    for y in range(ny):
        for out, which in ((keep, core[0]), (send, 1 - core[0])):
            at = pl.multiple_of((2 * y + which) * block, 16)
            out[y] = mm(normed_t[pl.ds(at, block), :], wide[...]).astype(BF)


def attend_back(core, mixed, attended_grad, lse, start_row, normed_t, first, count, ny):
    rows, width = attended_grad.shape
    block = width // (2 * ny)

    def column(offset):
        return pl.BlockSpec((rows, LANES), lambda p, s: (0, offset + first + p))

    out_column = pl.BlockSpec((rows, LANES), lambda p, s: (0, p))
    grads = pl.BlockSpec((ny, block, 3 * LANES), lambda p, s: (0, 0, p))
    return call(
        attend_back_body,
        "attend_back",
        (count,),
        [
            full((1, rows)),
            column(0),
            column(PAIRS),
            column(2 * PAIRS),
            column(0),
            pl.BlockSpec((1, 8, rows), lambda p, s: (first + p, 0, 0)),
            full((width, rows)),
        ],
        [out_column] * 3 + [grads] * 2,
        [sds((rows, LANES * count), BF)] * 3 + [sds((ny, block, 3 * LANES * count), BF)] * 2,
        [
            pltpu.VMEM((rows, rows), F32),
            pltpu.VMEM((LANES, rows), BF),
            pltpu.VMEM((LANES, rows), F32),
            pltpu.VMEM((rows, LANES), F32),
            pltpu.VMEM((rows, LANES), F32),
            pltpu.VMEM((rows, 3 * LANES), BF),
        ],
        flops=40 * count * rows * rows * HEAD_DIM,
        bytes_=2 * rows * LANES * count * 10,
        prefetch=1,
    )(core, start_row, mixed, mixed, mixed, attended_grad, lse, normed_t)


def second_body(att, w, tokens, gains, router, routes, stream, low, gates, sums, *, gain_at):
    attn = mm(att[...], w[...])
    total = tokens[...].astype(F32) + attn
    stream[...] = total
    hat, _ = normalise(total)
    normed = (hat * gains[gain_at : gain_at + 1, :] + gains[gain_at + 1 : gain_at + 2, :]).astype(BF)
    low[...] = normed
    logits = mm(normed, router[...])
    hot = routes[...] == lax.broadcasted_iota(jnp.int32, logits.shape, 1)
    gate = jax.nn.sigmoid(jnp.sum(jnp.where(hot, logits, 0.0), axis=1, keepdims=True))
    gates[...] = gate

    @pl.when(pl.program_id(0) == 0)
    def _():
        sums[...] = jnp.zeros_like(sums)

    row = lax.broadcasted_iota(jnp.int32, sums.shape, 0)
    by_expert = jnp.sum(jnp.where(hot, gate, 0.0), axis=0, keepdims=True)
    squares = jnp.sum(attn * attn)
    sums[...] += jnp.where(row == 0, by_expert, jnp.where(row == 1, squares, 0.0))


def second_stage(att, output, small, tokens, gains, routes, gain_at):
    rows, width = tokens.shape
    block = pl.BlockSpec((BLOCK, width), lambda i: (i, 0))
    thin = pl.BlockSpec((BLOCK, 1), lambda i: (i, 0))
    return call(
        functools.partial(second_body, gain_at=gain_at),
        "second",
        (rows // BLOCK,),
        [
            block,
            full((width, width)),
            block,
            full((LANES, width)),
            full((width, LANES)),
            thin,
        ],
        [block, block, thin, full((8, LANES))],
        [sds((rows, width), F32), sds((rows, width), BF), sds((rows, 1), F32), sds((8, LANES), F32)],
        flops=2 * rows * width * width,
        bytes_=rows * width * 10 + width * width * 2,
    )(att, output, tokens, gains, small, routes)


def flip_body(a, b, a_t, b_t):
    a_t[...] = a[...].T
    b_t[...] = b[...].T


def flip(inner, outer):
    width, wide = inner.shape
    tile = 512
    across = pl.BlockSpec((tile, width), lambda f: (f, 0))
    down = pl.BlockSpec((width, tile), lambda f: (0, f))
    return call(
        flip_body, "flip", (wide // tile,), [down, across], [across, down],
        [sds((wide, width), BF), sds((width, wide), BF)], bytes_=8 * width * wide,
    )(inner, outer)


def expert_body(
    bal, x, c, w1t, w2, w2t, w1, b1, b2, rw, act_t, pre_t, g_out, x_t, out, in_grad, b1_grad, rows_out,
    g, gate, out_acc, in_acc,
):
    step = pl.program_id(0)

    @pl.when(step == 0)
    def _():
        logits = jnp.sum(x[...].astype(F32) * rw[...], axis=1, keepdims=True)
        gate[...] = jax.nn.sigmoid(logits)
        g[...] = (gate[...] * c[...].astype(F32)).astype(BF)
        out_acc[...] = jnp.zeros_like(out_acc)
        in_acc[...] = jnp.zeros_like(in_acc)

    bias = jnp.broadcast_to(b1[...].astype(F32), (LANES, b1.shape[1])).T[:, :1]
    pre = mm(w1t[...], x[...], NT) + bias
    cdf = 0.5 * (1.0 + lax.erf(pre * (0.5**0.5)))
    act = (pre * cdf).astype(BF)
    slope = cdf + pre * jnp.exp(-0.5 * pre * pre) * ((2.0 * np.pi) ** -0.5)
    act_t[...] = act
    out_acc[...] += mm(w2t[...], act)
    back = (mm(w2[...], g[...], NT) * slope).astype(BF)
    pre_t[...] = back
    in_acc[...] += mm(w1[...], back)
    b1_grad[...] = mm(jnp.ones((8, back.shape[1]), BF), back, NT)

    @pl.when(step == pl.num_programs(0) - 1)
    def _():
        result = (out_acc[...].T + b2[...].astype(F32)).astype(BF)
        out[...] = result
        gate_grad = jnp.sum(c[...].astype(F32) * result.astype(F32), axis=1, keepdims=True) + bal[0, 0]
        logit_grad = gate_grad * gate[...] * (1.0 - gate[...])
        in_grad[...] = (in_acc[...].T + logit_grad * rw[...]).astype(BF)
        g_out[...] = g[...]
        x_t[...] = x[...].T
        row = lax.broadcasted_iota(jnp.int32, rows_out.shape, 0)
        router_part = jnp.sum(x[...].astype(F32) * logit_grad, axis=0, keepdims=True)
        bias_part = jnp.sum(g[...].astype(F32), axis=0, keepdims=True)
        rows_out[...] = jnp.where(row == 0, router_part, jnp.where(row == 1, bias_part, 0.0))


def expert_stage(bal, x, c, w1t, w2, w2t, w1, b1, b2, rw):
    rows, width = x.shape
    wide = w1.shape[1]
    tile = BLOCK
    across = pl.BlockSpec((tile, width), lambda f: (f, 0))
    down = pl.BlockSpec((width, tile), lambda f: (0, f))
    whole = full((rows, width))
    return call(
        expert_body,
        "expert",
        (wide // tile,),
        [
            pl.BlockSpec(memory_space=pltpu.SMEM),
            whole,
            whole,
            across,
            across,
            down,
            down,
            pl.BlockSpec((1, tile), lambda f: (0, f)),
            full((1, width)),
            full((1, width)),
        ],
        [
            pl.BlockSpec((tile, rows), lambda f: (f, 0)),
            pl.BlockSpec((tile, rows), lambda f: (f, 0)),
            whole,
            full((width, rows)),
            whole,
            whole,
            pl.BlockSpec((8, tile), lambda f: (0, f)),
            full((8, width)),
        ],
        [
            sds((wide, rows), BF),
            sds((wide, rows), BF),
            sds((rows, width), BF),
            sds((width, rows), BF),
            sds((rows, width), BF),
            sds((rows, width), BF),
            sds((8, wide), F32),
            sds((8, width), F32),
        ],
        [
            pltpu.VMEM((rows, width), BF),
            pltpu.VMEM((rows, 1), F32),
            pltpu.VMEM((width, rows), F32),
            pltpu.VMEM((width, rows), F32),
        ],
        flops=8 * rows * width * wide,
        bytes_=2 * (4 * width * wide + 2 * wide * rows + 6 * rows * width),
    )(bal, x, c, w1t, w2, w2t, w1, b1, b2, rw)


def weight_grad_body(
    core, a0, a1, g0, g1, p0, p1, x0, x1, outer_send, inner_send, outer_keep, inner_keep
):
    outer = (mm(a0[...], g0[...]) + mm(a1[...], g1[...])).astype(BF)
    inner = (mm(x0[...], p0[...], NT) + mm(x1[...], p1[...], NT)).astype(BF)

    @pl.when(pl.program_id(0) == 0)
    def _():
        outer_send[...] = outer
        inner_send[...] = inner

    @pl.when(pl.program_id(0) == 1)
    def _():
        outer_keep[...] = outer
        inner_keep[...] = inner


def weight_grads(core, acts, outs, pres, ins):
    tile = 512
    wide, rows = acts[0].shape
    width = outs[0].shape[1]
    steps = wide // 2 // tile

    def half(w, s):
        return jnp.where(w == 0, 1 - s[0], s[0])

    hidden = pl.BlockSpec((tile, rows), lambda w, f, s: (half(w, s) * steps + f, 0))

    def sent(w, f):
        return jnp.where(w == 0, f, steps - 1)

    def kept(w, f):
        return jnp.where(w == 0, 0, f)

    return call(
        weight_grad_body,
        "weight_grads",
        (2, steps),
        [hidden, hidden, full(outs[0].shape), full(outs[0].shape), hidden, hidden, full(ins[0].shape), full(ins[0].shape)],
        [
            pl.BlockSpec((tile, width), lambda w, f, s: (sent(w, f), 0)),
            pl.BlockSpec((width, tile), lambda w, f, s: (0, sent(w, f))),
            pl.BlockSpec((tile, width), lambda w, f, s: (kept(w, f), 0)),
            pl.BlockSpec((width, tile), lambda w, f, s: (0, kept(w, f))),
        ],
        [sds((wide // 2, width), BF), sds((width, wide // 2), BF)] * 2,
        flops=8 * rows * width * wide,
        bytes_=8 * (wide * rows + rows * width + width * wide),
        prefetch=1,
    )(core, *acts, *outs, *pres, *ins)


def place_body(which, a, b, *rest):
    rest[-1][0] = a[...].astype(F32) + b[...].astype(F32)


def place(which, outer, a, b, held=None, piece=0, pieces=1):
    steps = 4 // pieces
    offset = piece * steps
    if outer:
        block = (a.shape[0] // (steps * pieces), a.shape[1])
        whole = (1, 2 * a.shape[0], a.shape[1])
        a_spec = pl.BlockSpec(block, lambda i, s: (offset + i, 0))
        b_spec = pl.BlockSpec(block, lambda i, s: (i, 0))
        large = pl.BlockSpec((1,) + block, lambda i, s: (0, s[0] * steps * pieces + offset + i, 0))
    else:
        block = (a.shape[0], a.shape[1] // (steps * pieces))
        whole = (1, a.shape[0], 2 * a.shape[1])
        a_spec = pl.BlockSpec(block, lambda i, s: (0, offset + i))
        b_spec = pl.BlockSpec(block, lambda i, s: (0, i))
        large = pl.BlockSpec((1,) + block, lambda i, s: (0, 0, s[0] * steps * pieces + offset + i))
    extra = [] if held is None else [held]
    return call(
        place_body, "place", (steps,), [a_spec, b_spec] + [pl.BlockSpec(memory_space=pl.ANY)] * len(extra), large,
        sds(whole, F32), bytes_=b.size * 8, flops=b.size, prefetch=1, aliases={3: 0} if extra else None,
    )(which, a, b, *extra)


def layer_back(hat, scale, gain, grad):
    scaled = grad * gain
    return scale * (
        scaled - jnp.mean(scaled, axis=-1, keepdims=True) - hat * jnp.mean(scaled * hat, axis=-1, keepdims=True)
    )


def return_body(
    core, slots, tgt, r0, r1, stream, cot, gains, att_t, w, stream_grad, back, sums, keep, send, w_acc, *, gain_at
):
    step = pl.program_id(0)

    @pl.when(step == 0)
    def _():
        sums[...] = jnp.zeros_like(sums)
        w_acc[...] = jnp.zeros_like(w_acc)

    grad = mm(jnp.where(tgt[...] == slots[0:1, :], 1.0, 0.0).astype(BF), r0[...])
    grad += mm(jnp.where(tgt[...] == slots[1:2, :], 1.0, 0.0).astype(BF), r1[...])
    hat, scale = normalise(stream[...])
    total = cot[...].astype(F32) + layer_back(hat, scale, gains[gain_at : gain_at + 1, :], grad)
    stream_grad[...] = total
    low = total.astype(BF)
    back[...] = mm(low, w[...], NT).astype(BF)
    w_acc[...] += mm(att_t[...], low)
    row = lax.broadcasted_iota(jnp.int32, sums.shape, 0)
    sums[...] += jnp.where(
        row == 0,
        jnp.sum(grad * hat, axis=0, keepdims=True),
        jnp.where(row == 1, jnp.sum(grad, axis=0, keepdims=True), 0.0),
    )

    @pl.when(step == pl.num_programs(0) - 1)
    def _():
        ny, block = keep.shape[:2]
        for y in range(ny):
            for out, which in ((keep, core[0]), (send, 1 - core[0])):
                at = pl.multiple_of((2 * y + which) * block, 16)
                out[y] = w_acc[pl.ds(at, block), :].astype(BF)


def return_stage(core, slots_row, tgt_col, r0, r1, stream, cot, gains, att_t, output, gain_at, ny):
    rows, width = stream.shape
    block = pl.BlockSpec((BLOCK, width), lambda i, s: (i, 0))
    grads = (ny, width // (2 * ny), width)
    return call(
        functools.partial(return_body, gain_at=gain_at),
        "return",
        (rows // BLOCK,),
        [
            full(slots_row.shape),
            pl.BlockSpec((BLOCK, 1), lambda i, s: (i, 0)),
            full(r0.shape),
            full(r1.shape),
            block,
            block,
            full((LANES, width)),
            pl.BlockSpec((width, BLOCK), lambda i, s: (0, i)),
            full((width, width)),
        ],
        [block, block, full((8, width)), full(grads), full(grads)],
        [sds((rows, width), F32), sds((rows, width), BF), sds((8, width), F32), sds(grads, BF), sds(grads, BF)],
        [pltpu.VMEM((width, width), F32)],
        flops=2 * rows * width * (2 * r0.shape[0] + 2 * width),
        bytes_=rows * width * 16 + 4 * width * width,
        prefetch=1,
    )(core, slots_row, tgt_col, r0, r1, stream, cot, gains, att_t, output)


def last_body(*refs, gain_at, splits):
    core, parts, (own, other, tokens, stream_grad, gains, out, sums, mixer) = refs[0], refs[1:-8], refs[-8:]

    @pl.when(pl.program_id(0) == 0)
    def _():
        merge_rows(mixer, own, other, core[0], 0, mixer.shape[1])
        sums[...] = jnp.zeros_like(sums)

    width = tokens.shape[1]
    grad = jnp.zeros(tokens.shape, F32)
    for n, (first, count) in enumerate(splits):
        for j in range(3):
            at = j * width + first * LANES
            grad += mm(parts[3 * n + j][...], mixer[:, at : at + count * LANES], NT)
    hat, scale = normalise(tokens[...].astype(F32))
    out[...] = stream_grad[...] + layer_back(hat, scale, gains[gain_at : gain_at + 1, :], grad)
    row = lax.broadcasted_iota(jnp.int32, sums.shape, 0)
    sums[...] += jnp.where(
        row == 0,
        jnp.sum(grad * hat, axis=0, keepdims=True),
        jnp.where(row == 1, jnp.sum(grad, axis=0, keepdims=True), 0.0),
    )


def last_stage(core, parts, splits, own, other, tokens, stream_grad, gains, gain_at):
    rows, width = tokens.shape
    block = pl.BlockSpec((BLOCK, width), lambda i, s: (i, 0))
    weight = pl.BlockSpec(own.shape[:2] + (3 * width,), lambda i, s: (0, 0, 0))
    return call(
        functools.partial(last_body, gain_at=gain_at, splits=splits),
        "last",
        (rows // BLOCK,),
        [pl.BlockSpec((BLOCK, p.shape[1]), lambda i, s: (i, 0)) for p in parts]
        + [weight, weight, block, block, full((LANES, width))],
        [block, full((8, width))],
        [sds((rows, width), F32), sds((8, width), F32)],
        [pltpu.VMEM((width, 3 * width), BF)],
        flops=6 * rows * width * width,
        bytes_=rows * width * 16 + 6 * width * width,
        prefetch=1,
    )(core, *parts, own, other, tokens, stream_grad, gains)


def result_body(slots, tgt, r0, r1, stream, gates, out, sums):
    @pl.when(pl.program_id(0) == 0)
    def _():
        sums[...] = jnp.zeros_like(sums)

    picked = mm(jnp.where(tgt[...] == slots[0:1, :], 1.0, 0.0).astype(BF), r0[...])
    picked += mm(jnp.where(tgt[...] == slots[1:2, :], 1.0, 0.0).astype(BF), r1[...])
    moe = gates[...] * picked
    total = stream[...] + moe
    out[...] = total.astype(BF)
    row = lax.broadcasted_iota(jnp.int32, sums.shape, 0)
    sums[...] += jnp.where(row == 0, jnp.sum(total * total), jnp.where(row == 1, jnp.sum(moe * moe), 0.0))


def result_stage(slots_row, tgt_col, r0, r1, stream, gates):
    rows, width = stream.shape
    block = pl.BlockSpec((BLOCK, width), lambda i: (i, 0))
    thin = pl.BlockSpec((BLOCK, 1), lambda i: (i, 0))
    return call(
        result_body,
        "result",
        (rows // BLOCK,),
        [full(slots_row.shape), thin, full(r0.shape), full(r1.shape), block, thin],
        [block, full((8, LANES))],
        [sds((rows, width), BF), sds((8, LANES), F32)],
        flops=4 * rows * width * r0.shape[0],
        bytes_=rows * width * 10,
    )(slots_row, tgt_col, r0, r1, stream, gates)


def collect_body(expert_here, r0, r1, b0, b1, second, first, forward, result, out, *, experts):
    row = lax.broadcasted_iota(jnp.int32, (experts, out.shape[1]), 0)
    router = r0[0:1, :] + r1[0:1, :]
    width = out.shape[1]
    out[...] = jnp.zeros_like(out)
    out[:experts, :] = jnp.where(row == expert_here[0], router, 0.0)
    out[experts : experts + 2, :] = second[0:2, :]
    out[experts + 2 : experts + 4, :] = first[0:2, :]
    at = experts + 4
    for k, (ref, line) in enumerate(((forward, 0), (forward, 1), (result, 0), (result, 1))):
        out[at : at + 1, k * LANES : (k + 1) * LANES] = ref[line : line + 1, :]
    out[at + 1 : at + 2, :] = r0[1:2, :] + r1[1:2, :]
    for k in range(b0.shape[1] // width):
        cut = slice(k * width, (k + 1) * width)
        out[at + 2 + k : at + 3 + k, :] = b0[0:1, cut] + b1[0:1, cut]


def collect(expert_here, experts, arrays):
    width = arrays[0].shape[1]
    shape = (experts + 6 + arrays[2].shape[1] // width, width)
    return call(
        functools.partial(collect_body, experts=experts),
        "collect",
        (1,),
        [pl.BlockSpec(memory_space=pltpu.SMEM)] + [full(a.shape) for a in arrays],
        full(shape),
        sds(shape, F32),
        bytes_=4 * shape[0] * width,
    )(expert_here, *arrays)


def shards(
    tokens, cotangent, lengths, routes, mixer_weight, output_weight, first_gain, first_shift, second_gain,
    second_shift, router_weight, inner_weight, inner_bias, outer_weight, outer_bias,
):
    rows, width = tokens.shape
    shard_rows = mixer_weight.shape[0]
    experts = router_weight.shape[1]
    wide = inner_weight.shape[2]
    devices = lax.axis_size(ANYWHERE)
    capacity = 3 * rows // (2 * experts)
    half_cap = capacity // 2
    half = experts * half_cap
    total_tokens = rows * devices
    average = total_tokens / experts
    gain_one_at, gain_two_at, counts_at = experts, experts + 2, experts + 4

    slot_ids = np.arange(experts * capacity, dtype=np.int32).reshape(experts, 2, half_cap).swapaxes(0, 1).reshape(2, half)
    slots_row = jnp.asarray(slot_ids)
    slots_col = [jnp.asarray(slot_ids[c].reshape(half, 1)) for c in range(2)]

    tgt_row, start_row, packed = prepare(
        lengths, routes, mixer_weight, output_weight, router_weight.T,
        (first_gain, first_shift, second_gain, second_shift), capacity,
    )
    expert_here = lax.axis_index("expert")
    core = my_bit("batch", 0).reshape(1).astype(jnp.int32)
    nb_bits = bits_of(lax.axis_size("batch"))
    ny = lax.axis_size("batch") // 2

    def exchange(value):
        shaped = value.reshape(experts, half_cap, width)
        return lax.all_to_all(shaped, "expert", split_axis=0, concat_axis=0, tiled=True).reshape(half, width)

    w1, w2 = inner_weight[0], outer_weight[0]
    ready = {}

    def beside(name, make):
        def run(other):
            other, *ready[name] = lax.optimization_barrier((other, *make()))
            return other

        return run

    own_rows, other_rows = gather_rows(
        packed,
        [
            beside("cot0", lambda: [dispatch(slots_col[0], tgt_row, cotangent)]),
            beside("cot1", lambda: [dispatch(slots_col[1], tgt_row, cotangent)]),
            beside("weights", lambda: flip(w1, w2)),
            beside("sent0", lambda: [exchange(ready["cot0"][0]), *columns(tgt_row, routes.reshape(1, rows))]),
        ],
    )
    w1t, w2t = ready["weights"]
    cot0, tgt_col, routes_col = ready["sent0"]
    cot1 = exchange(ready["cot1"][0])

    mixed, normed_t, output_full, small, small_t = first_stage(core, tokens, own_rows, other_rows, gain_one_at)
    counts = jnp.sum(small_t[counts_at : counts_at + experts], axis=1)
    balance_terms = (counts - average) / (average * total_tokens)
    bal = lax.dynamic_slice_in_dim(balance_terms, expert_here, 1).reshape(1, 1)
    rw = lax.dynamic_slice_in_dim(small_t, expert_here, 1, axis=0)
    att, att_t, lse = attend(mixed, start_row)
    stream, second_low, gates, second_sums = second_stage(att, output_full, small, tokens, small_t, routes_col, gain_two_at)
    low_again, bal, rw = lax.optimization_barrier((second_low, bal, rw))
    placed = [dispatch(slots_col[0], tgt_row, second_low), dispatch(slots_col[1], tgt_row, low_again)]

    placed0, cot1 = lax.optimization_barrier((placed[0], cot1))
    x0 = exchange(placed0)
    second_half, x0 = lax.optimization_barrier((placed[1], x0))
    x1 = exchange(second_half)
    e0 = expert_stage(bal, x0, cot0, w1t, w2, w2t, w1, inner_bias, outer_bias, rw)
    in0 = exchange(e0[5])
    e1 = expert_stage(bal, x1, cot1, w1t, w2, w2t, w1, inner_bias, outer_bias, rw)
    in1 = exchange(e1[5])

    wgrads = weight_grads(core, (e0[0], e1[0]), (e0[2], e1[2]), (e0[1], e1[1]), (e0[3], e1[3]))
    in0, in1, wgrads, out0_in = lax.optimization_barrier((in0, in1, tuple(wgrads), e0[4]))
    outer_away, inner_away, outer_kept, inner_kept = wgrads

    def together(kept, away):
        mine = over_cores(kept, away)
        for bit in range(2, nb_bits):
            mine = add_low(mine, swap(mine, "batch", bit))
        return mine

    out0 = exchange(out0_in)

    stream_grad, attended_grad, second_grads, out_keep, out_send = return_stage(
        core, slots_row, tgt_col, in0, in1, stream, cotangent, small_t, att_t, output_full, gain_two_at, ny
    )

    outer_mine, inner_mine = together(outer_kept, outer_away), together(inner_kept, inner_away)
    attended_grad, outer_mine, inner_mine = lax.optimization_barrier((attended_grad, outer_mine, inner_mine))
    inner_far = swap(inner_mine, "batch", 1)

    def backward(first, grad):
        *parts, keep, send = attend_back(core, mixed, grad, lse, start_row, normed_t, first, 2, ny)
        return parts, keep, send

    parts_a, *sums_a = backward(0, attended_grad)
    sum_o = over_cores(out_keep, out_send)
    outer_beside, inner_beside = swap(outer_mine, "batch", 0), swap(inner_mine, "batch", 0)
    attended_grad, sum_o, out0, out1_in, *sums_a = lax.optimization_barrier(
        (attended_grad, sum_o, out0, e1[4], *sums_a)
    )
    out1 = exchange(out1_in)
    parts_b, *sums_b = backward(2, attended_grad)
    sum_o, sum_a = over_x(sum_o), over_cores(*sums_a)
    attended_grad, sum_o, sum_a, outer_beside, inner_beside, *sums_b = lax.optimization_barrier(
        (attended_grad, sum_o, sum_a, outer_beside, inner_beside, *sums_b)
    )
    parts_c, *sums_c = backward(4, attended_grad)
    sum_a, sum_b = over_x(sum_a), over_cores(*sums_b)
    stream_grad, gates, sum_a, sum_b, inner_far, outer_mine, *sums_c = lax.optimization_barrier(
        (stream_grad, gates, sum_a, sum_b, inner_far, outer_mine, *sums_c)
    )
    outer_far = swap(outer_mine[: wide // 4], "batch", 1)
    block_output, result_sums = result_stage(slots_row, tgt_col, out0, out1, stream, gates)
    splits = ((0, 2), (2, 2), (4, 2))
    input_grad, first_grads = last_stage(
        core, parts_a + parts_b + parts_c, splits, own_rows, other_rows, tokens, stream_grad, small_t, gain_one_at
    )
    sum_b, sum_c = over_x(sum_b), over_x(over_cores(*sums_c))
    total = jnp.concatenate([sum_o, sum_a, sum_b, sum_c], axis=-1)
    first_grads, result_sums, outer_far, outer_mine = lax.optimization_barrier(
        (first_grads, result_sums, outer_far, outer_mine)
    )
    outer_last = swap(outer_mine[wide // 4 :], "batch", 1)
    other = 1 - core
    inner_held = place(core, False, inner_mine, inner_far)

    sums = collect(
        expert_here.reshape(1).astype(jnp.int32), experts,
        (e0[7], e1[7], e0[6], e1[6], second_grads, first_grads, second_sums, result_sums),
    )
    common = sums[: experts + 5]
    for bit in reversed(range(bits_of(experts))):
        common = common + swap(common, "expert", bit)
        if bit == bits_of(experts) - 2:
            common, total = lax.optimization_barrier((common, total))
    inner_w_sum = place(other, False, inner_beside, swap(inner_far, "batch", 0), inner_held)
    total = over_rest(total)
    sums = jnp.concatenate([common, sums[experts + 5 :]], axis=0)
    sums = sums + swap(sums, "batch", 0)
    outer_w_sum = place(core, True, outer_mine, outer_far, None, 0, 2)
    outer_w_sum = place(other, True, outer_beside, swap(outer_far, "batch", 0), outer_w_sum, 0, 2)
    sums, outer_last, inner_w_sum, outer_w_sum = lax.optimization_barrier((sums, outer_last, inner_w_sum, outer_w_sum))
    for bit in range(1, nb_bits):
        sums = sums + swap(sums, "batch", bit)
    outer_w_sum = place(core, True, outer_mine, outer_last, outer_w_sum, 1, 2)
    outer_w_sum = place(other, True, outer_beside, swap(outer_last, "batch", 0), outer_w_sum, 1, 2)
    outer_b_sum = sums[experts + 5 : experts + 6]
    inner_b_sum = sums[experts + 6 :].reshape(1, wide)
    output_grad = total[:, :width]
    mixer_grad = jnp.swapaxes(total[:, width:].reshape(shard_rows, PAIRS, 3, LANES), 1, 2)
    mixer_grad = mixer_grad.reshape(shard_rows, 3 * width)

    device = lax.axis_index("batch") * experts + expert_here
    mine = lax.dynamic_slice_in_dim(sums[: experts + 4], device * shard_rows, shard_rows, axis=1)
    numbers = sums[experts + 4]
    balance = jnp.sum((counts - average) / average * numbers[:experts]) / total_tokens
    squares = jnp.stack([numbers[2 * LANES], numbers[LANES], numbers[3 * LANES]])
    root_means = jnp.sqrt(squares / (total_tokens * width) + 1e-06)

    return (
        block_output,
        input_grad,
        mixer_grad,
        output_grad,
        mine[experts + 2],
        mine[experts + 3],
        mine[experts],
        mine[experts + 1],
        mine[:experts].T,
        inner_w_sum,
        inner_b_sum,
        outer_w_sum,
        outer_b_sum,
        balance,
        root_means,
    )


def solution(mesh):
    everywhere = P(ANYWHERE, None)
    line = P(ANYWHERE)
    in_specs = (
        everywhere, everywhere, everywhere, everywhere, everywhere, everywhere, line, line, line, line, everywhere,
        P("expert", None, None), P("expert", None), P("expert", None, None), P("expert", None),
    )
    out_specs = (
        everywhere, everywhere, everywhere, everywhere, line, line, line, line, everywhere,
        P("expert", None, None), P("expert", None), P("expert", None, None), P("expert", None), P(), P(),
    )
    return jax.shard_map(shards, mesh=mesh, in_specs=in_specs, out_specs=out_specs, check_vma=False)
```

```python
import functools

import jax
import jax.numpy as jnp
import numpy as np
from jax import lax
from jax.experimental import pallas as pl
from jax.experimental.pallas import tpu as pltpu
from jax.sharding import PartitionSpec as P

HEADS = 12
HEAD_DIM = 64
PAIRS = HEADS // 2
WINDOW = 512
BLOCK = 256
EPSILON = 1e-05
LANES = 128
BF = jnp.bfloat16
F32 = jnp.float32
ANYWHERE = ("batch", "expert")

NT = (((1,), (1,)), ((), ()))
NN = (((1,), (0,)), ((), ()))


def mm(a, b, dims=NN):
    return lax.dot_general(a, b, dims, preferred_element_type=F32)


def call(body, name, grid, in_specs, out_specs, out_shape, scratch=(), flops=0, bytes_=0, prefetch=0, aliases=None):
    return pl.pallas_call(
        body,
        name=name,
        grid_spec=pltpu.PrefetchScalarGridSpec(
            num_scalar_prefetch=prefetch,
            grid=grid,
            in_specs=in_specs,
            out_specs=out_specs,
            scratch_shapes=list(scratch),
        ),
        out_shape=out_shape,
        input_output_aliases=aliases or {},
        cost_estimate=pl.CostEstimate(flops=int(flops), bytes_accessed=int(bytes_), transcendentals=0),
    )


def sds(shape, dtype):
    return jax.ShapeDtypeStruct(shape, dtype)


def full(shape):
    return pl.BlockSpec(shape, lambda *_: (0,) * len(shape))


def bits_of(size):
    return size.bit_length() - 1


def swap(value, axis, bit):
    size = lax.axis_size(axis)
    return lax.ppermute(value, axis, [(i, i ^ (1 << bit)) for i in range(size)])


def my_bit(axis, bit):
    return (lax.axis_index(axis) >> bit) & 1


def gather_rows(shard, beside):
    nb, ne = lax.axis_size("batch"), lax.axis_size("expert")
    value = shard
    placed = []
    order = [("expert", b) for b in reversed(range(bits_of(ne)))] + [("batch", b) for b in reversed(range(1, bits_of(nb)))]
    for step, (axis, bit) in enumerate(order):
        weight = bit + (bits_of(ne) if axis == "batch" else 0)
        spot = sum(1 for w in placed if w > weight)
        placed.append(weight)
        other = swap(value, axis, bit)
        late = step + len(beside) - len(order)
        if late >= 0:
            other = beside[late](other)
        value, other = jnp.expand_dims(value, spot), jnp.expand_dims(other, spot)
        place = lax.broadcasted_iota(jnp.int32, value.shape[:spot] + (2,) + value.shape[spot + 1 :], spot)
        value = jnp.where(place == my_bit(axis, bit), value, other)
    value = value.reshape(nb // 2, ne * shard.shape[0], shard.shape[1])
    return value, swap(value, "batch", 0)


def merge_rows(out, own, other, core, first, last):
    ny, rows = own.shape[:2]
    for y in range(ny):
        for part, which in ((own, core), (other, 1 - core)):
            out[pl.ds(pl.multiple_of((2 * y + which) * rows, 16), rows), :] = part[y, :, first:last]


def add_low(a, b):
    return (a.astype(F32) + b.astype(F32)).astype(BF)


def over_cores(keep, send):
    return add_low(keep, swap(send, "batch", 0))


def over_x(total):
    ny, rows, width = total.shape
    ne = lax.axis_size("expert")
    total = total.reshape(ny, ne // 2, 2, rows // ne, width).transpose(2, 1, 0, 3, 4)
    low = my_bit("expert", 0)
    got = swap(lax.dynamic_index_in_dim(total, 1 - low, 0, keepdims=False), "expert", 0)
    return add_low(lax.dynamic_index_in_dim(total, low, 0, keepdims=False), got)


def over_rest(total):
    ne = lax.axis_size("expert")
    groups = [list(range(b, ne, 2)) for b in range(2)]
    pieces = lax.all_to_all(total, "expert", split_axis=0, concat_axis=0, axis_index_groups=groups, tiled=True)
    value = jnp.sum(pieces.astype(F32), axis=0)
    for bit in reversed(range(1, bits_of(lax.axis_size("batch")))):
        here = my_bit("batch", bit)
        value = value.reshape((2, value.shape[0] // 2) + value.shape[1:])
        out = lax.dynamic_index_in_dim(value, 1 - here, 0, keepdims=False)
        value = lax.dynamic_index_in_dim(value, here, 0, keepdims=False) + swap(out, "batch", bit)
    return value[0]


def prep_body(lengths_ref, routes_row, mixer, output, router, *rest, capacity, experts):
    vectors, (tgt_row, start_row, packed) = rest[:4], rest[4:]
    rows = routes_row.shape[1]
    at = lax.broadcasted_iota(jnp.int32, (1, rows), 1)
    start = jnp.zeros((1, rows), jnp.int32)
    off = jnp.int32(0)
    for s in range(lengths_ref.shape[1]):
        start = jnp.where(at >= off, off, start)
        off = off + lengths_ref[0, s]
    start_row[...] = start
    hot = routes_row[...] == lax.broadcasted_iota(jnp.int32, (LANES, rows), 0)
    hot_low = jnp.where(hot, 1.0, 0.0).astype(BF)
    before = lax.broadcasted_iota(jnp.int32, (rows, rows), 0) < lax.broadcasted_iota(jnp.int32, (rows, rows), 1)
    ranks = mm(hot_low, jnp.where(before, 1.0, 0.0).astype(BF))
    rank = jnp.sum(jnp.where(hot, ranks, 0.0), axis=0, keepdims=True)
    tgt_row[...] = routes_row[...] * capacity + rank.astype(jnp.int32)

    own, first = mixer.shape
    wide = first + output.shape[1]
    packed[:, :first] = mixer[...]
    packed[:, first:wide] = output[...]
    row = lax.broadcasted_iota(jnp.int32, (own, LANES), 0)
    lane = lax.broadcasted_iota(jnp.int32, (own, LANES), 1)
    lane_of = lax.broadcasted_iota(jnp.int32, (LANES, LANES), 1)
    row_of = lax.broadcasted_iota(jnp.int32, (LANES, LANES), 0)
    counts = jnp.sum(jnp.where(hot, 1.0, 0.0), axis=1, keepdims=True)
    counts = jnp.sum(jnp.where(lane_of == row_of + experts + 4, counts, 0.0), axis=0, keepdims=True)
    small = jnp.where((row == 0) & (lane < 2 * experts + 4), counts, 0.0)
    across = lax.broadcasted_iota(jnp.int32, (own, own), 0) == lax.broadcasted_iota(jnp.int32, (own, own), 1)
    lines = router[...].astype(F32)
    lines = [lines[k : k + 1, :] for k in range(experts)] + [v[...].astype(F32) for v in vectors]
    for k, line in enumerate(lines):
        column = jnp.sum(jnp.where(across, line, 0.0), axis=1, keepdims=True)
        small = jnp.where(lane == k, column, small)
    packed[:, wide:] = small.astype(BF)


def prepare(lengths, routes, mixer, output, router, vectors, capacity):
    rows = routes.shape[0]
    experts, own = router.shape
    wide = mixer.shape[1] + output.shape[1] + LANES
    return call(
        functools.partial(prep_body, capacity=capacity, experts=experts),
        "prep",
        (1,),
        [pl.BlockSpec(memory_space=pltpu.SMEM), full((1, rows)), full(mixer.shape), full(output.shape), full(router.shape)]
        + [full((1, own))] * 4,
        [full((1, rows)), full((1, rows)), full((own, wide))],
        [sds((1, rows), jnp.int32), sds((1, rows), jnp.int32), sds((own, wide), BF)],
        flops=2 * rows * rows * LANES,
        bytes_=rows * 1024,
    )(lengths, routes.reshape(1, rows), mixer, output, router, *[v.reshape(1, own) for v in vectors])


def columns_body(a, b, a_col, b_col):
    for row, col in ((a, a_col), (b, b_col)):
        wide = jnp.broadcast_to(row[...].astype(F32), (LANES, row.shape[1]))
        col[...] = wide.T[:, :1].astype(jnp.int32)


def columns(a, b):
    rows = a.shape[1]
    return call(
        columns_body, "columns", (1,), [full(a.shape)] * 2, [full((rows, 1))] * 2, [sds((rows, 1), jnp.int32)] * 2, bytes_=rows * 1024
    )(a, b)


def dispatch_body(slots, tgt, x, out):
    hot = jnp.where(slots[...] == tgt[...], 1.0, 0.0).astype(BF)
    out[...] = mm(hot, x[...]).astype(BF)


def dispatch(slots_col, tgt_row, x):
    rows, width = x.shape
    half = slots_col.shape[0]
    tile = BLOCK
    return call(
        dispatch_body,
        "dispatch",
        (half // tile,),
        [pl.BlockSpec((tile, 1), lambda t: (t, 0)), full((1, rows)), full((rows, width))],
        pl.BlockSpec((tile, width), lambda t: (t, 0)),
        sds((half, width), BF),
        flops=2 * half * rows * width,
        bytes_=rows * width * 4,
    )(slots_col, tgt_row, x)


def normalise(v):
    centre = v - jnp.mean(v, axis=-1, keepdims=True)
    spread = jnp.mean(centre * centre, axis=-1, keepdims=True)
    scale = lax.rsqrt(spread + EPSILON)
    return centre * scale, scale


def first_body(core, tokens, own, other, mixed, normed_t, output, small, gains, mixer, *, gain_at):
    @pl.when(pl.program_id(0) == 0)
    def _():
        wide, width = mixer.shape[1], output.shape[1]
        merge_rows(mixer, own, other, core[0], 0, wide)
        merge_rows(output, own, other, core[0], wide, wide + width)
        merge_rows(small, own, other, core[0], wide + width, wide + width + LANES)
        gains[...] = small[...].astype(F32).T

    hat, _ = normalise(tokens[...].astype(F32))
    normed = hat * gains[gain_at : gain_at + 1, :] + gains[gain_at + 1 : gain_at + 2, :]
    low = normed.astype(BF)
    normed_t[...] = low.T
    mixed[...] = mm(low, mixer[...]).astype(BF)


def first_stage(core, tokens, own, other, gain_at):
    rows, width = tokens.shape
    wide = 3 * width
    return call(
        functools.partial(first_body, gain_at=gain_at),
        "first",
        (rows // BLOCK,),
        [pl.BlockSpec((BLOCK, width), lambda i, s: (i, 0)), full(own.shape), full(own.shape)],
        [
            pl.BlockSpec((BLOCK, wide), lambda i, s: (i, 0)),
            pl.BlockSpec((width, BLOCK), lambda i, s: (0, i)),
            full((width, width)),
            full((width, LANES)),
            full((LANES, width)),
        ],
        [
            sds((rows, wide), BF),
            sds((width, rows), BF),
            sds((width, width), BF),
            sds((width, LANES), BF),
            sds((LANES, width), F32),
        ],
        [pltpu.VMEM((width, wide), BF)],
        flops=2 * rows * width * wide,
        bytes_=2 * (rows * (2 * width + wide) + width * wide),
        prefetch=1,
    )(core, tokens, own, other)


def fill_bias(bias, start):
    rows = bias.shape[0]
    for q in range(rows // BLOCK):
        k0 = max(0, (q + 1) * BLOCK - WINDOW - BLOCK)
        n = (q + 1) * BLOCK - k0
        key = k0 + lax.broadcasted_iota(jnp.int32, (n, BLOCK), 0)
        query = q * BLOCK + lax.broadcasted_iota(jnp.int32, (n, BLOCK), 1)
        seen = (key <= query) & (key >= start[:, q * BLOCK : (q + 1) * BLOCK])
        bias[k0 : k0 + n, q * BLOCK : (q + 1) * BLOCK] = jnp.where(seen, 0.0, -1e30)


def head_of(value, h):
    lane = lax.broadcasted_iota(jnp.int32, value.shape, 1)
    return jnp.where((lane >= HEAD_DIM * h) & (lane < HEAD_DIM * (h + 1)), value, jnp.zeros_like(value))


def attend_body(start, q, k, v, att, att_t, lse, bias, v_t):
    rows = q.shape[0]

    @pl.when(pl.program_id(0) == 0)
    def _():
        fill_bias(bias, start[...])

    v_t[...] = v[...].T
    for i in range(rows // BLOCK):
        k0 = max(0, (i + 1) * BLOCK - WINDOW - BLOCK)
        k1 = (i + 1) * BLOCK
        here = slice(i * BLOCK, k1)
        scaled = q[here, :] * jnp.asarray(HEAD_DIM**-0.5, BF)
        for h in range(2):
            s = mm(k[k0:k1, :], head_of(scaled, h), NT) + bias[k0:k1, here]
            top = jnp.max(s, axis=0, keepdims=True)
            e = jnp.exp(s - top)
            total = jnp.sum(e, axis=0, keepdims=True)
            o = mm(v_t[HEAD_DIM * h : HEAD_DIM * (h + 1), k0:k1], e.astype(BF)) / total
            att_t[HEAD_DIM * h : HEAD_DIM * (h + 1), here] = o.astype(BF)
            lse[0, h : h + 1, here] = top + jnp.log(total)
    att[...] = att_t[...].T


def attend(mixed, start_row):
    rows = mixed.shape[0]
    width = mixed.shape[1] // 3
    return call(
        attend_body,
        "attend",
        (PAIRS,),
        [
            full((1, rows)),
            pl.BlockSpec((rows, LANES), lambda p: (0, p)),
            pl.BlockSpec((rows, LANES), lambda p: (0, PAIRS + p)),
            pl.BlockSpec((rows, LANES), lambda p: (0, 2 * PAIRS + p)),
        ],
        [
            pl.BlockSpec((rows, LANES), lambda p: (0, p)),
            pl.BlockSpec((LANES, rows), lambda p: (p, 0)),
            pl.BlockSpec((1, 8, rows), lambda p: (p, 0, 0)),
        ],
        [sds((rows, width), BF), sds((width, rows), BF), sds((PAIRS, 8, rows), F32)],
        [pltpu.VMEM((rows, rows), F32), pltpu.VMEM((LANES, rows), BF)],
        flops=8 * HEADS * rows * rows * HEAD_DIM,
        bytes_=2 * rows * width * 5,
    )(start_row, mixed, mixed, mixed)


def attend_back_body(
    core, start, q, k, v, g, lse, normed_t, dq, dk, dv, keep, send, bias, k_t, dq_t, dk_acc, dv_acc, wide
):
    rows = q.shape[0]

    @pl.when(pl.program_id(0) == 0)
    def _():
        fill_bias(bias, start[...])

    k_t[...] = k[...].T
    dk_acc[...] = jnp.zeros_like(dk_acc)
    dv_acc[...] = jnp.zeros_like(dv_acc)
    for i in range(rows // BLOCK):
        k0 = max(0, (i + 1) * BLOCK - WINDOW - BLOCK)
        k1 = (i + 1) * BLOCK
        here = slice(i * BLOCK, k1)
        scaled = q[here, :] * jnp.asarray(HEAD_DIM**-0.5, BF)
        g_here = g[here, :]
        for h in range(2):
            q_h = head_of(scaled, h)
            g_h = head_of(g_here, h)
            s = mm(k[k0:k1, :], q_h, NT) + bias[k0:k1, here]
            p = jnp.exp(s - lse[0, h : h + 1, here])
            dp = mm(v[k0:k1, :], g_h, NT)
            inner = jnp.sum(p * dp, axis=0, keepdims=True)
            ds = (p * (dp - inner)).astype(BF)
            dv_acc[k0:k1, :] += mm(p.astype(BF), g_h)
            dk_acc[k0:k1, :] += mm(ds, q_h)
            dq_t[HEAD_DIM * h : HEAD_DIM * (h + 1), here] = mm(k_t[HEAD_DIM * h : HEAD_DIM * (h + 1), k0:k1], ds)
    wide[:, :LANES] = (dq_t[...].T * HEAD_DIM**-0.5).astype(BF)
    wide[:, LANES : 2 * LANES] = dk_acc[...].astype(BF)
    wide[:, 2 * LANES :] = dv_acc[...].astype(BF)
    dq[...] = wide[:, :LANES]
    dk[...] = wide[:, LANES : 2 * LANES]
    dv[...] = wide[:, 2 * LANES :]
    ny, block = keep.shape[:2]
    for y in range(ny):
        for out, which in ((keep, core[0]), (send, 1 - core[0])):
            at = pl.multiple_of((2 * y + which) * block, 16)
            out[y] = mm(normed_t[pl.ds(at, block), :], wide[...]).astype(BF)


def attend_back(core, mixed, attended_grad, lse, start_row, normed_t, first, count, ny):
    rows, width = attended_grad.shape
    block = width // (2 * ny)

    def column(offset):
        return pl.BlockSpec((rows, LANES), lambda p, s: (0, offset + first + p))

    out_column = pl.BlockSpec((rows, LANES), lambda p, s: (0, p))
    grads = pl.BlockSpec((ny, block, 3 * LANES), lambda p, s: (0, 0, p))
    return call(
        attend_back_body,
        "attend_back",
        (count,),
        [
            full((1, rows)),
            column(0),
            column(PAIRS),
            column(2 * PAIRS),
            column(0),
            pl.BlockSpec((1, 8, rows), lambda p, s: (first + p, 0, 0)),
            full((width, rows)),
        ],
        [out_column] * 3 + [grads] * 2,
        [sds((rows, LANES * count), BF)] * 3 + [sds((ny, block, 3 * LANES * count), BF)] * 2,
        [
            pltpu.VMEM((rows, rows), F32),
            pltpu.VMEM((LANES, rows), BF),
            pltpu.VMEM((LANES, rows), F32),
            pltpu.VMEM((rows, LANES), F32),
            pltpu.VMEM((rows, LANES), F32),
            pltpu.VMEM((rows, 3 * LANES), BF),
        ],
        flops=40 * count * rows * rows * HEAD_DIM,
        bytes_=2 * rows * LANES * count * 10,
        prefetch=1,
    )(core, start_row, mixed, mixed, mixed, attended_grad, lse, normed_t)


def second_body(att, w, tokens, gains, router, routes, stream, low, gates, sums, *, gain_at):
    attn = mm(att[...], w[...])
    total = tokens[...].astype(F32) + attn
    stream[...] = total
    hat, _ = normalise(total)
    normed = (hat * gains[gain_at : gain_at + 1, :] + gains[gain_at + 1 : gain_at + 2, :]).astype(BF)
    low[...] = normed
    logits = mm(normed, router[...])
    hot = routes[...] == lax.broadcasted_iota(jnp.int32, logits.shape, 1)
    gate = jax.nn.sigmoid(jnp.sum(jnp.where(hot, logits, 0.0), axis=1, keepdims=True))
    gates[...] = gate

    @pl.when(pl.program_id(0) == 0)
    def _():
        sums[...] = jnp.zeros_like(sums)

    row = lax.broadcasted_iota(jnp.int32, sums.shape, 0)
    by_expert = jnp.sum(jnp.where(hot, gate, 0.0), axis=0, keepdims=True)
    squares = jnp.sum(attn * attn)
    sums[...] += jnp.where(row == 0, by_expert, jnp.where(row == 1, squares, 0.0))


def second_stage(att, output, small, tokens, gains, routes, gain_at):
    rows, width = tokens.shape
    block = pl.BlockSpec((BLOCK, width), lambda i: (i, 0))
    thin = pl.BlockSpec((BLOCK, 1), lambda i: (i, 0))
    return call(
        functools.partial(second_body, gain_at=gain_at),
        "second",
        (rows // BLOCK,),
        [
            block,
            full((width, width)),
            block,
            full((LANES, width)),
            full((width, LANES)),
            thin,
        ],
        [block, block, thin, full((8, LANES))],
        [sds((rows, width), F32), sds((rows, width), BF), sds((rows, 1), F32), sds((8, LANES), F32)],
        flops=2 * rows * width * width,
        bytes_=rows * width * 10 + width * width * 2,
    )(att, output, tokens, gains, small, routes)


def flip_body(a, b, a_t, b_t):
    a_t[...] = a[...].T
    b_t[...] = b[...].T


def flip(inner, outer):
    width, wide = inner.shape
    tile = 512
    across = pl.BlockSpec((tile, width), lambda f: (f, 0))
    down = pl.BlockSpec((width, tile), lambda f: (0, f))
    return call(
        flip_body, "flip", (wide // tile,), [down, across], [across, down],
        [sds((wide, width), BF), sds((width, wide), BF)], bytes_=8 * width * wide,
    )(inner, outer)


def expert_body(
    bal, x, c, w1t, w2, w2t, w1, b1, b2, rw, act_t, pre_t, g_out, x_t, out, in_grad, b1_grad, rows_out,
    g, gate, out_acc, in_acc,
):
    step = pl.program_id(0)

    @pl.when(step == 0)
    def _():
        logits = jnp.sum(x[...].astype(F32) * rw[...], axis=1, keepdims=True)
        gate[...] = jax.nn.sigmoid(logits)
        g[...] = (gate[...] * c[...].astype(F32)).astype(BF)
        out_acc[...] = jnp.zeros_like(out_acc)
        in_acc[...] = jnp.zeros_like(in_acc)

    bias = jnp.broadcast_to(b1[...].astype(F32), (LANES, b1.shape[1])).T[:, :1]
    pre = mm(w1t[...], x[...], NT) + bias
    cdf = 0.5 * (1.0 + lax.erf(pre * (0.5**0.5)))
    act = (pre * cdf).astype(BF)
    slope = cdf + pre * jnp.exp(-0.5 * pre * pre) * ((2.0 * np.pi) ** -0.5)
    act_t[...] = act
    out_acc[...] += mm(w2t[...], act)
    back = (mm(w2[...], g[...], NT) * slope).astype(BF)
    pre_t[...] = back
    in_acc[...] += mm(w1[...], back)
    b1_grad[...] = mm(jnp.ones((8, back.shape[1]), BF), back, NT)

    @pl.when(step == pl.num_programs(0) - 1)
    def _():
        result = (out_acc[...].T + b2[...].astype(F32)).astype(BF)
        out[...] = result
        gate_grad = jnp.sum(c[...].astype(F32) * result.astype(F32), axis=1, keepdims=True) + bal[0, 0]
        logit_grad = gate_grad * gate[...] * (1.0 - gate[...])
        in_grad[...] = (in_acc[...].T + logit_grad * rw[...]).astype(BF)
        g_out[...] = g[...]
        x_t[...] = x[...].T
        row = lax.broadcasted_iota(jnp.int32, rows_out.shape, 0)
        router_part = jnp.sum(x[...].astype(F32) * logit_grad, axis=0, keepdims=True)
        bias_part = jnp.sum(g[...].astype(F32), axis=0, keepdims=True)
        rows_out[...] = jnp.where(row == 0, router_part, jnp.where(row == 1, bias_part, 0.0))


def expert_stage(bal, x, c, w1t, w2, w2t, w1, b1, b2, rw):
    rows, width = x.shape
    wide = w1.shape[1]
    tile = BLOCK
    across = pl.BlockSpec((tile, width), lambda f: (f, 0))
    down = pl.BlockSpec((width, tile), lambda f: (0, f))
    whole = full((rows, width))
    return call(
        expert_body,
        "expert",
        (wide // tile,),
        [
            pl.BlockSpec(memory_space=pltpu.SMEM),
            whole,
            whole,
            across,
            across,
            down,
            down,
            pl.BlockSpec((1, tile), lambda f: (0, f)),
            full((1, width)),
            full((1, width)),
        ],
        [
            pl.BlockSpec((tile, rows), lambda f: (f, 0)),
            pl.BlockSpec((tile, rows), lambda f: (f, 0)),
            whole,
            full((width, rows)),
            whole,
            whole,
            pl.BlockSpec((8, tile), lambda f: (0, f)),
            full((8, width)),
        ],
        [
            sds((wide, rows), BF),
            sds((wide, rows), BF),
            sds((rows, width), BF),
            sds((width, rows), BF),
            sds((rows, width), BF),
            sds((rows, width), BF),
            sds((8, wide), F32),
            sds((8, width), F32),
        ],
        [
            pltpu.VMEM((rows, width), BF),
            pltpu.VMEM((rows, 1), F32),
            pltpu.VMEM((width, rows), F32),
            pltpu.VMEM((width, rows), F32),
        ],
        flops=8 * rows * width * wide,
        bytes_=2 * (4 * width * wide + 2 * wide * rows + 6 * rows * width),
    )(bal, x, c, w1t, w2, w2t, w1, b1, b2, rw)


def weight_grad_body(
    core, a0, a1, g0, g1, p0, p1, x0, x1, outer_send, inner_send, outer_keep, inner_keep
):
    outer = (mm(a0[...], g0[...]) + mm(a1[...], g1[...])).astype(BF)
    inner = (mm(x0[...], p0[...], NT) + mm(x1[...], p1[...], NT)).astype(BF)

    @pl.when(pl.program_id(0) == 0)
    def _():
        outer_send[...] = outer
        inner_send[...] = inner

    @pl.when(pl.program_id(0) == 1)
    def _():
        outer_keep[...] = outer
        inner_keep[...] = inner


def weight_grads(core, acts, outs, pres, ins):
    tile = 512
    wide, rows = acts[0].shape
    width = outs[0].shape[1]
    steps = wide // 2 // tile

    def half(w, s):
        return jnp.where(w == 0, 1 - s[0], s[0])

    hidden = pl.BlockSpec((tile, rows), lambda w, f, s: (half(w, s) * steps + f, 0))

    def sent(w, f):
        return jnp.where(w == 0, f, steps - 1)

    def kept(w, f):
        return jnp.where(w == 0, 0, f)

    return call(
        weight_grad_body,
        "weight_grads",
        (2, steps),
        [hidden, hidden, full(outs[0].shape), full(outs[0].shape), hidden, hidden, full(ins[0].shape), full(ins[0].shape)],
        [
            pl.BlockSpec((tile, width), lambda w, f, s: (sent(w, f), 0)),
            pl.BlockSpec((width, tile), lambda w, f, s: (0, sent(w, f))),
            pl.BlockSpec((tile, width), lambda w, f, s: (kept(w, f), 0)),
            pl.BlockSpec((width, tile), lambda w, f, s: (0, kept(w, f))),
        ],
        [sds((wide // 2, width), BF), sds((width, wide // 2), BF)] * 2,
        flops=8 * rows * width * wide,
        bytes_=8 * (wide * rows + rows * width + width * wide),
        prefetch=1,
    )(core, *acts, *outs, *pres, *ins)


def place_body(which, a, b, *rest):
    rest[-1][0] = a[...].astype(F32) + b[...].astype(F32)


def place(which, outer, a, b, held=None, piece=0, pieces=1):
    steps = 4 // pieces
    offset = piece * steps
    if outer:
        block = (a.shape[0] // (steps * pieces), a.shape[1])
        whole = (1, 2 * a.shape[0], a.shape[1])
        a_spec = pl.BlockSpec(block, lambda i, s: (offset + i, 0))
        b_spec = pl.BlockSpec(block, lambda i, s: (i, 0))
        large = pl.BlockSpec((1,) + block, lambda i, s: (0, s[0] * steps * pieces + offset + i, 0))
    else:
        block = (a.shape[0], a.shape[1] // (steps * pieces))
        whole = (1, a.shape[0], 2 * a.shape[1])
        a_spec = pl.BlockSpec(block, lambda i, s: (0, offset + i))
        b_spec = pl.BlockSpec(block, lambda i, s: (0, i))
        large = pl.BlockSpec((1,) + block, lambda i, s: (0, 0, s[0] * steps * pieces + offset + i))
    extra = [] if held is None else [held]
    return call(
        place_body, "place", (steps,), [a_spec, b_spec] + [pl.BlockSpec(memory_space=pl.ANY)] * len(extra), large,
        sds(whole, F32), bytes_=b.size * 8, flops=b.size, prefetch=1, aliases={3: 0} if extra else None,
    )(which, a, b, *extra)


def layer_back(hat, scale, gain, grad):
    scaled = grad * gain
    return scale * (
        scaled - jnp.mean(scaled, axis=-1, keepdims=True) - hat * jnp.mean(scaled * hat, axis=-1, keepdims=True)
    )


def return_body(
    core, slots, tgt, r0, r1, stream, cot, gains, att_t, w, stream_grad, back, sums, keep, send, w_acc, *, gain_at
):
    step = pl.program_id(0)

    @pl.when(step == 0)
    def _():
        sums[...] = jnp.zeros_like(sums)
        w_acc[...] = jnp.zeros_like(w_acc)

    grad = mm(jnp.where(tgt[...] == slots[0:1, :], 1.0, 0.0).astype(BF), r0[...])
    grad += mm(jnp.where(tgt[...] == slots[1:2, :], 1.0, 0.0).astype(BF), r1[...])
    hat, scale = normalise(stream[...])
    total = cot[...].astype(F32) + layer_back(hat, scale, gains[gain_at : gain_at + 1, :], grad)
    stream_grad[...] = total
    low = total.astype(BF)
    back[...] = mm(low, w[...], NT).astype(BF)
    w_acc[...] += mm(att_t[...], low)
    row = lax.broadcasted_iota(jnp.int32, sums.shape, 0)
    sums[...] += jnp.where(
        row == 0,
        jnp.sum(grad * hat, axis=0, keepdims=True),
        jnp.where(row == 1, jnp.sum(grad, axis=0, keepdims=True), 0.0),
    )

    @pl.when(step == pl.num_programs(0) - 1)
    def _():
        ny, block = keep.shape[:2]
        for y in range(ny):
            for out, which in ((keep, core[0]), (send, 1 - core[0])):
                at = pl.multiple_of((2 * y + which) * block, 16)
                out[y] = w_acc[pl.ds(at, block), :].astype(BF)


def return_stage(core, slots_row, tgt_col, r0, r1, stream, cot, gains, att_t, output, gain_at, ny):
    rows, width = stream.shape
    block = pl.BlockSpec((BLOCK, width), lambda i, s: (i, 0))
    grads = (ny, width // (2 * ny), width)
    return call(
        functools.partial(return_body, gain_at=gain_at),
        "return",
        (rows // BLOCK,),
        [
            full(slots_row.shape),
            pl.BlockSpec((BLOCK, 1), lambda i, s: (i, 0)),
            full(r0.shape),
            full(r1.shape),
            block,
            block,
            full((LANES, width)),
            pl.BlockSpec((width, BLOCK), lambda i, s: (0, i)),
            full((width, width)),
        ],
        [block, block, full((8, width)), full(grads), full(grads)],
        [sds((rows, width), F32), sds((rows, width), BF), sds((8, width), F32), sds(grads, BF), sds(grads, BF)],
        [pltpu.VMEM((width, width), F32)],
        flops=2 * rows * width * (2 * r0.shape[0] + 2 * width),
        bytes_=rows * width * 16 + 4 * width * width,
        prefetch=1,
    )(core, slots_row, tgt_col, r0, r1, stream, cot, gains, att_t, output)


def last_body(*refs, gain_at, splits):
    core, parts, (own, other, tokens, stream_grad, gains, out, sums, mixer) = refs[0], refs[1:-8], refs[-8:]

    @pl.when(pl.program_id(0) == 0)
    def _():
        merge_rows(mixer, own, other, core[0], 0, mixer.shape[1])
        sums[...] = jnp.zeros_like(sums)

    width = tokens.shape[1]
    grad = jnp.zeros(tokens.shape, F32)
    for n, (first, count) in enumerate(splits):
        for j in range(3):
            at = j * width + first * LANES
            grad += mm(parts[3 * n + j][...], mixer[:, at : at + count * LANES], NT)
    hat, scale = normalise(tokens[...].astype(F32))
    out[...] = stream_grad[...] + layer_back(hat, scale, gains[gain_at : gain_at + 1, :], grad)
    row = lax.broadcasted_iota(jnp.int32, sums.shape, 0)
    sums[...] += jnp.where(
        row == 0,
        jnp.sum(grad * hat, axis=0, keepdims=True),
        jnp.where(row == 1, jnp.sum(grad, axis=0, keepdims=True), 0.0),
    )


def last_stage(core, parts, splits, own, other, tokens, stream_grad, gains, gain_at):
    rows, width = tokens.shape
    block = pl.BlockSpec((BLOCK, width), lambda i, s: (i, 0))
    weight = pl.BlockSpec(own.shape[:2] + (3 * width,), lambda i, s: (0, 0, 0))
    return call(
        functools.partial(last_body, gain_at=gain_at, splits=splits),
        "last",
        (rows // BLOCK,),
        [pl.BlockSpec((BLOCK, p.shape[1]), lambda i, s: (i, 0)) for p in parts]
        + [weight, weight, block, block, full((LANES, width))],
        [block, full((8, width))],
        [sds((rows, width), F32), sds((8, width), F32)],
        [pltpu.VMEM((width, 3 * width), BF)],
        flops=6 * rows * width * width,
        bytes_=rows * width * 16 + 6 * width * width,
        prefetch=1,
    )(core, *parts, own, other, tokens, stream_grad, gains)


def result_body(tgt, r0, r1, stream, gates, out, sums):
    @pl.when(pl.program_id(0) == 0)
    def _():
        sums[...] = jnp.zeros_like(sums)

    half = r0.shape[0]
    slot = lax.broadcasted_iota(jnp.int32, (1, half), 1)
    picked = mm(jnp.where(tgt[...] == slot, 1.0, 0.0).astype(BF), r0[...])
    picked += mm(jnp.where(tgt[...] == slot + half, 1.0, 0.0).astype(BF), r1[...])
    moe = gates[...] * picked
    total = stream[...] + moe
    out[...] = total.astype(BF)
    row = lax.broadcasted_iota(jnp.int32, sums.shape, 0)
    sums[...] += jnp.where(row == 0, jnp.sum(total * total), jnp.where(row == 1, jnp.sum(moe * moe), 0.0))


def result_stage(tgt_col, returned, stream, gates):
    rows, width = stream.shape
    half = returned.shape[0] // 2
    block = pl.BlockSpec((BLOCK, width), lambda i: (i, 0))
    thin = pl.BlockSpec((BLOCK, 1), lambda i: (i, 0))
    halves = [pl.BlockSpec((half, width), functools.partial(lambda c, i: (c, 0), c)) for c in range(2)]
    return call(
        result_body,
        "result",
        (rows // BLOCK,),
        [thin, *halves, block, thin],
        [block, full((8, LANES))],
        [sds((rows, width), BF), sds((8, LANES), F32)],
        flops=4 * rows * width * half,
        bytes_=rows * width * 10,
    )(tgt_col, returned, returned, stream, gates)


def collect_body(expert_here, r0, r1, b0, b1, second, first, forward, result, out, *, experts):
    row = lax.broadcasted_iota(jnp.int32, (experts, out.shape[1]), 0)
    router = r0[0:1, :] + r1[0:1, :]
    width = out.shape[1]
    out[...] = jnp.zeros_like(out)
    out[:experts, :] = jnp.where(row == expert_here[0], router, 0.0)
    out[experts : experts + 2, :] = second[0:2, :]
    out[experts + 2 : experts + 4, :] = first[0:2, :]
    at = experts + 4
    for k, (ref, line) in enumerate(((forward, 0), (forward, 1), (result, 0), (result, 1))):
        out[at : at + 1, k * LANES : (k + 1) * LANES] = ref[line : line + 1, :]
    out[at + 1 : at + 2, :] = r0[1:2, :] + r1[1:2, :]
    for k in range(b0.shape[1] // width):
        cut = slice(k * width, (k + 1) * width)
        out[at + 2 + k : at + 3 + k, :] = b0[0:1, cut] + b1[0:1, cut]


def collect(expert_here, experts, arrays):
    width = arrays[0].shape[1]
    shape = (experts + 6 + arrays[2].shape[1] // width, width)
    return call(
        functools.partial(collect_body, experts=experts),
        "collect",
        (1,),
        [pl.BlockSpec(memory_space=pltpu.SMEM)] + [full(a.shape) for a in arrays],
        full(shape),
        sds(shape, F32),
        bytes_=4 * shape[0] * width,
    )(expert_here, *arrays)


def shards(
    tokens, cotangent, lengths, routes, mixer_weight, output_weight, first_gain, first_shift, second_gain,
    second_shift, router_weight, inner_weight, inner_bias, outer_weight, outer_bias,
):
    rows, width = tokens.shape
    shard_rows = mixer_weight.shape[0]
    experts = router_weight.shape[1]
    wide = inner_weight.shape[2]
    devices = lax.axis_size(ANYWHERE)
    capacity = 3 * rows // (2 * experts)
    half_cap = capacity // 2
    half = experts * half_cap
    total_tokens = rows * devices
    average = total_tokens / experts
    gain_one_at, gain_two_at, counts_at = experts, experts + 2, experts + 4

    slot_ids = np.arange(experts * capacity, dtype=np.int32).reshape(experts, 2, half_cap).swapaxes(0, 1).reshape(2, half)
    slots_row = jnp.asarray(slot_ids)
    slots_col = [jnp.asarray(slot_ids[c].reshape(half, 1)) for c in range(2)]

    tgt_row, start_row, packed = prepare(
        lengths, routes, mixer_weight, output_weight, router_weight.T,
        (first_gain, first_shift, second_gain, second_shift), capacity,
    )
    expert_here = lax.axis_index("expert")
    core = my_bit("batch", 0).reshape(1).astype(jnp.int32)
    nb_bits = bits_of(lax.axis_size("batch"))
    ny = lax.axis_size("batch") // 2

    def exchange(value):
        shaped = value.reshape(experts, half_cap, width)
        return lax.all_to_all(shaped, "expert", split_axis=0, concat_axis=0, tiled=True).reshape(half, width)

    w1, w2 = inner_weight[0], outer_weight[0]
    ready = {}

    def beside(name, make):
        def run(other):
            other, *ready[name] = lax.optimization_barrier((other, *make()))
            return other

        return run

    own_rows, other_rows = gather_rows(
        packed,
        [
            beside("cot0", lambda: [dispatch(slots_col[0], tgt_row, cotangent)]),
            beside("cot1", lambda: [dispatch(slots_col[1], tgt_row, cotangent)]),
            beside("weights", lambda: flip(w1, w2)),
            beside("sent0", lambda: [exchange(ready["cot0"][0]), *columns(tgt_row, routes.reshape(1, rows))]),
        ],
    )
    w1t, w2t = ready["weights"]
    cot0, tgt_col, routes_col = ready["sent0"]
    cot1 = exchange(ready["cot1"][0])

    mixed, normed_t, output_full, small, small_t = first_stage(core, tokens, own_rows, other_rows, gain_one_at)
    counts = jnp.sum(small_t[counts_at : counts_at + experts], axis=1)
    balance_terms = (counts - average) / (average * total_tokens)
    bal = lax.dynamic_slice_in_dim(balance_terms, expert_here, 1).reshape(1, 1)
    rw = lax.dynamic_slice_in_dim(small_t, expert_here, 1, axis=0)
    att, att_t, lse = attend(mixed, start_row)
    stream, second_low, gates, second_sums = second_stage(att, output_full, small, tokens, small_t, routes_col, gain_two_at)
    low_again, bal, rw = lax.optimization_barrier((second_low, bal, rw))
    placed = [dispatch(slots_col[0], tgt_row, second_low), dispatch(slots_col[1], tgt_row, low_again)]

    placed0, cot1 = lax.optimization_barrier((placed[0], cot1))
    x0 = exchange(placed0)
    second_half, x0 = lax.optimization_barrier((placed[1], x0))
    x1 = exchange(second_half)
    e0 = expert_stage(bal, x0, cot0, w1t, w2, w2t, w1, inner_bias, outer_bias, rw)
    in0 = exchange(e0[5])
    e1 = expert_stage(bal, x1, cot1, w1t, w2, w2t, w1, inner_bias, outer_bias, rw)
    in1 = exchange(e1[5])

    wgrads = weight_grads(core, (e0[0], e1[0]), (e0[2], e1[2]), (e0[1], e1[1]), (e0[3], e1[3]))
    out_in = jnp.concatenate([e[4].reshape(experts, half_cap, width) for e in (e0, e1)], axis=1)
    in0, in1, wgrads, out_in = lax.optimization_barrier((in0, in1, tuple(wgrads), out_in))
    outer_away, inner_away, outer_kept, inner_kept = wgrads

    def together(kept, away):
        mine = over_cores(kept, away)
        for bit in range(2, nb_bits):
            mine = add_low(mine, swap(mine, "batch", bit))
        return mine

    out = lax.all_to_all(out_in, "expert", split_axis=0, concat_axis=0, tiled=True).reshape(2 * half, width)

    stream_grad, attended_grad, second_grads, out_keep, out_send = return_stage(
        core, slots_row, tgt_col, in0, in1, stream, cotangent, small_t, att_t, output_full, gain_two_at, ny
    )

    outer_mine, inner_mine = together(outer_kept, outer_away), together(inner_kept, inner_away)
    attended_grad, outer_mine, inner_mine = lax.optimization_barrier((attended_grad, outer_mine, inner_mine))
    inner_far = swap(inner_mine, "batch", 1)

    def backward(first, grad):
        *parts, keep, send = attend_back(core, mixed, grad, lse, start_row, normed_t, first, 2, ny)
        return parts, keep, send

    parts_a, *sums_a = backward(0, attended_grad)
    sum_o = over_cores(out_keep, out_send)
    outer_beside, inner_beside = swap(outer_mine, "batch", 0), swap(inner_mine, "batch", 0)
    attended_grad, sum_o, *sums_a = lax.optimization_barrier((attended_grad, sum_o, *sums_a))
    parts_b, *sums_b = backward(2, attended_grad)
    sum_o, sum_a = over_x(sum_o), over_cores(*sums_a)
    attended_grad, sum_o, sum_a, outer_beside, inner_beside, out, *sums_b = lax.optimization_barrier(
        (attended_grad, sum_o, sum_a, outer_beside, inner_beside, out, *sums_b)
    )
    parts_c, *sums_c = backward(4, attended_grad)
    sum_a, sum_b = over_x(sum_a), over_cores(*sums_b)
    stream_grad, gates, sum_a, sum_b, inner_far, outer_mine, *sums_c = lax.optimization_barrier(
        (stream_grad, gates, sum_a, sum_b, inner_far, outer_mine, *sums_c)
    )
    outer_far = swap(outer_mine[: wide // 4], "batch", 1)
    block_output, result_sums = result_stage(tgt_col, out, stream, gates)
    splits = ((0, 2), (2, 2), (4, 2))
    input_grad, first_grads = last_stage(
        core, parts_a + parts_b + parts_c, splits, own_rows, other_rows, tokens, stream_grad, small_t, gain_one_at
    )
    sum_b, sum_c = over_x(sum_b), over_x(over_cores(*sums_c))
    total = jnp.concatenate([sum_o, sum_a, sum_b, sum_c], axis=-1)
    first_grads, result_sums, outer_far, outer_mine = lax.optimization_barrier(
        (first_grads, result_sums, outer_far, outer_mine)
    )
    outer_last = swap(outer_mine[wide // 4 :], "batch", 1)
    other = 1 - core
    inner_held = place(core, False, inner_mine, inner_far)

    sums = collect(
        expert_here.reshape(1).astype(jnp.int32), experts,
        (e0[7], e1[7], e0[6], e1[6], second_grads, first_grads, second_sums, result_sums),
    )
    common = sums[: experts + 5]
    for bit in reversed(range(bits_of(experts))):
        common = common + swap(common, "expert", bit)
        if bit == bits_of(experts) - 2:
            common, total = lax.optimization_barrier((common, total))
    inner_w_sum = place(other, False, inner_beside, swap(inner_far, "batch", 0), inner_held)
    total = over_rest(total)
    sums = jnp.concatenate([common, sums[experts + 5 :]], axis=0)
    sums = sums + swap(sums, "batch", 0)
    outer_w_sum = place(core, True, outer_mine, outer_far, None, 0, 2)
    outer_w_sum = place(other, True, outer_beside, swap(outer_far, "batch", 0), outer_w_sum, 0, 2)
    sums, outer_last, inner_w_sum, outer_w_sum = lax.optimization_barrier((sums, outer_last, inner_w_sum, outer_w_sum))
    for bit in range(1, nb_bits):
        sums = sums + swap(sums, "batch", bit)
    outer_w_sum = place(core, True, outer_mine, outer_last, outer_w_sum, 1, 2)
    outer_w_sum = place(other, True, outer_beside, swap(outer_last, "batch", 0), outer_w_sum, 1, 2)
    outer_b_sum = sums[experts + 5 : experts + 6]
    inner_b_sum = sums[experts + 6 :].reshape(1, wide)
    output_grad = total[:, :width]
    mixer_grad = jnp.swapaxes(total[:, width:].reshape(shard_rows, PAIRS, 3, LANES), 1, 2)
    mixer_grad = mixer_grad.reshape(shard_rows, 3 * width)

    device = lax.axis_index("batch") * experts + expert_here
    mine = lax.dynamic_slice_in_dim(sums[: experts + 4], device * shard_rows, shard_rows, axis=1)
    numbers = sums[experts + 4]
    balance = jnp.sum((counts - average) / average * numbers[:experts]) / total_tokens
    squares = jnp.stack([numbers[2 * LANES], numbers[LANES], numbers[3 * LANES]])
    root_means = jnp.sqrt(squares / (total_tokens * width) + 1e-06)

    return (
        block_output,
        input_grad,
        mixer_grad,
        output_grad,
        mine[experts + 2],
        mine[experts + 3],
        mine[experts],
        mine[experts + 1],
        mine[:experts].T,
        inner_w_sum,
        inner_b_sum,
        outer_w_sum,
        outer_b_sum,
        balance,
        root_means,
    )


def solution(mesh):
    everywhere = P(ANYWHERE, None)
    line = P(ANYWHERE)
    in_specs = (
        everywhere, everywhere, everywhere, everywhere, everywhere, everywhere, line, line, line, line, everywhere,
        P("expert", None, None), P("expert", None), P("expert", None, None), P("expert", None),
    )
    out_specs = (
        everywhere, everywhere, everywhere, everywhere, line, line, line, line, everywhere,
        P("expert", None, None), P("expert", None), P("expert", None, None), P("expert", None), P(), P(),
    )
    return jax.shard_map(shards, mesh=mesh, in_specs=in_specs, out_specs=out_specs, check_vma=False)
```
